32 devices in a mesh: dp: 16 (over z, y, core), tensor: 2 (over x).
Axes of the slice: x: 2, y: 2, z: 4, core: 2. Of those that a mesh axis runs over, the one named last changes fastest.
Arguments:
- frames_in: bfloat16 [2, 16, 1024, 1024], P(None, 'dp', 'tensor'), may hold values from -6 to 6
- phone_len: int32 [2, 16], P(None, 'dp'), may hold values from 10 to 204
- frame_len: int32 [2, 16], P(None, 'dp'), may hold values from 512 to 819
- section: int32 [2, 16], P(None, 'dp'), may hold values from 0 to 6
- norm_gain: float32 [2, 1024], replicated, may hold values from 0.5 to 1.5
- norm_bias: float32 [2, 1024], replicated, may hold values from -4 to 4
- ada_scale: float32 [2, 7, 1024], replicated, may hold values from 0.5 to 1.5
- ada_shift: float32 [2, 7, 1024], replicated, may hold values from -4 to 4
- w_qkv: bfloat16 [2, 1024, 3, 1024], P(None, None, None, 'tensor'), may hold values from -0.1875 to 0.1875
- w_out: bfloat16 [2, 1024, 1024], P(None, 'tensor'), may hold values from -4 to 4
- w_up: bfloat16 [2, 1024, 4096], P(None, None, 'tensor'), may hold values from -0.1875 to 0.1875
- w_down: bfloat16 [2, 4096, 1024], P(None, 'tensor'), may hold values from -0.09375 to 0.09375
- out_grad: bfloat16 [2, 16, 1024, 1024], P(None, 'dp', 'tensor'), may hold values from -6 to 6
Outputs:
- frames_out: float32 [2, 16, 1024, 1024], P(None, 'dp', 'tensor')
- frames_grad: float32 [2, 16, 1024, 1024], P(None, 'dp', 'tensor')
- grad_qkv: float32 [2, 1024, 3, 1024], P(None, None, None, 'tensor')
- grad_out: float32 [2, 1024, 1024], P(None, 'tensor')
- grad_up: float32 [2, 1024, 4096], P(None, None, 'tensor')
- grad_down: float32 [2, 4096, 1024], P(None, 'tensor')
- grad_norm_gain: float32 [2, 1024], replicated
- grad_norm_bias: float32 [2, 1024], replicated
- grad_ada_scale: float32 [2, 7, 1024], replicated
- grad_ada_shift: float32 [2, 7, 1024], replicated
The draws below stay inside these ranges and needn't reach their ends.
All inputs are finite; a program needn't handle non-finite values.
Results may differ from the reference program's by a relative error of at most 0.028.
Values may be sent and summed in bfloat16 or wider, within the bound.
No kernel may reach another device: no remote copies, remote signals or barrier semaphores. Data moves between devices by JAX's collectives and lax.ppermute only.
A program may use at most 384 MiB of HBM per device.

```python
import jax
import jax.numpy as jnp
from jax import lax

D = 1024
HEADS = 16
HEAD_DIM = 64
FF = 4096
SECTIONS = 7
MICRO = 2
SEQ_LEN = 1024
SEQS = 16


def touch_ends(values, own_key, low, largest):
    shape = values.shape
    index_at = [jax.random.randint(jax.random.fold_in(own_key, axis), (), 0, shape[axis]) for axis in range(len(shape))]
    values = values.at[tuple(index_at)].set(low)
    longest = shape.index(max(shape))
    index_at[longest] = (index_at[longest] + 1) % shape[longest]
    return values.at[tuple(index_at)].set(largest)


def levels(stream_key, shape, cuts, least, top_value):
    level, own = 1.0, jax.random.fold_in(stream_key, 6)
    for dim, shards_of in cuts:
        steps = jnp.exp(jax.random.uniform(jax.random.fold_in(own, dim), (shards_of,), jnp.float32, least / len(cuts), top_value / len(cuts)))
        level = level * jnp.repeat(steps, shape[dim] // shards_of).reshape([-1 if axis == dim else 1 for axis in range(len(shape))])
    return level


def noise(rng, dims, width, bound, shards=(), kind=jnp.bfloat16):
    entries = width * jax.random.normal(rng, dims, jnp.float32)
    if shards:
        entries = entries * levels(rng, dims, shards, -0.22, 0.18)
    return jnp.clip(entries, -bound, bound).astype(kind)


def setup_inputs(seed: int = 0) -> dict:
    keys = jax.random.split(jax.random.key(seed), 14)
    frames_in = noise(keys[0], (MICRO, SEQS, SEQ_LEN, D), 1.0, 6.0, ((1, 16), (2, 2)))
    phone_len = touch_ends(jax.random.randint(keys[1], (MICRO, SEQS), max(2, SEQ_LEN // 100), SEQ_LEN // 5 + 1), jax.random.fold_in(keys[1], 1), max(2, SEQ_LEN // 100), (SEQ_LEN // 5 + 1) - 1).astype(jnp.int32)
    frame_len = touch_ends(jax.random.randint(keys[2], (MICRO, SEQS), SEQ_LEN // 2, SEQ_LEN - SEQ_LEN // 5), jax.random.fold_in(keys[2], 1), SEQ_LEN // 2, (SEQ_LEN - SEQ_LEN // 5) - 1).astype(jnp.int32)
    section = touch_ends(jax.random.randint(keys[3], (MICRO, SEQS), 0, SECTIONS), jax.random.fold_in(keys[3], 1), 0, SECTIONS - 1).astype(jnp.int32)
    norm_gain = jnp.clip(1.0 + 0.1 * jax.random.normal(keys[4], (2, D), jnp.float32), 0.5, 1.5)
    norm_bias = noise(keys[5], (2, D), 0.3, 4.0, (), jnp.float32)
    ada_scale = jnp.clip(1.0 + 0.1 * jax.random.normal(keys[6], (2, SECTIONS, D), jnp.float32), 0.5, 1.5)
    ada_shift = noise(keys[7], (2, SECTIONS, D), 0.3, 4.0, (), jnp.float32)
    w_qkv = noise(keys[8], (2, D, 3, D), D ** -0.5, 0.1875, ((3, 2),))
    w_out = noise(keys[9], (2, D, D), (max(1, 2 * D // SEQ_LEN)) ** -0.5, 4.0, ((1, 2),))
    w_up = noise(keys[10], (2, D, FF), D ** -0.5, 0.1875, ((2, 2),))
    w_down = noise(keys[11], (2, FF, D), FF ** -0.5, 0.09375, ((1, 2),))
    out_grad = noise(keys[12], (MICRO, SEQS, SEQ_LEN, D), 1.0, 6.0, ((1, 16), (2, 2)))
    return dict(frames_in=frames_in, phone_len=phone_len, frame_len=frame_len, section=section, norm_gain=norm_gain, norm_bias=norm_bias, ada_scale=ada_scale, ada_shift=ada_shift, w_qkv=w_qkv, w_out=w_out, w_up=w_up, w_down=w_down, out_grad=out_grad)


norm_eps = 1e-05
masked_score = -1000000000.0

@jax.custom_vjp
def low(v):
    return lax.optimization_barrier(v.astype(jnp.bfloat16)).astype(jnp.float32)

@jax.custom_vjp
def low_back(v):
    return v

def low_keep(v):
    return (low(v), None)

def low_pass(kept, grad):
    return (grad,)

def back_keep(v):
    return (v, None)

def back_low(kept, grad):
    return (low(grad),)
low.defvjp(low_keep, low_pass)
low_back.defvjp(back_keep, back_low)

def matmul(left, right):
    return jnp.dot(left, right, precision=lax.Precision.HIGHEST, preferred_element_type=jnp.float32)

def plain_norm(inputs):
    centered = inputs - lax.optimization_barrier(jnp.mean(inputs, axis=-1, keepdims=True))
    variance = lax.optimization_barrier(jnp.mean(centered * centered, axis=-1, keepdims=True))
    return centered * lax.rsqrt(variance + norm_eps)

def fixed_norm(inputs, gain_row, shift_row):
    return plain_norm(inputs) * gain_row + shift_row

def section_norm(inputs, scale_table, shift_table, picker):
    scale_row = matmul(picker, scale_table)
    shift_row = matmul(picker, shift_table)
    return plain_norm(inputs) * scale_row + shift_row

def key_allowed(query_pos, key_pos, prefix, valid_count, causal):
    allowed = key_pos[None, :] < valid_count
    if causal:
        allowed = allowed & ((key_pos[None, :] < prefix) | (key_pos[None, :] <= query_pos[:, None]))
    return allowed

def attention(normed, weight_qkv, weight_out, prefix, valid_count, causal):
    projected = low(low_back(matmul(normed, weight_qkv.reshape(D, 3 * D))))
    query_rows = projected[:, :D].reshape(SEQ_LEN, HEADS, HEAD_DIM)
    key_rows = projected[:, D:2 * D].reshape(SEQ_LEN, HEADS, HEAD_DIM)
    value_rows = projected[:, 2 * D:].reshape(SEQ_LEN, HEADS, HEAD_DIM)
    scores = jnp.einsum('qhd,khd->hqk', query_rows, key_rows, precision=lax.Precision.HIGHEST) * HEAD_DIM ** (-0.5)
    scores = low_back(scores)
    positions = jnp.arange(SEQ_LEN, dtype=jnp.int32)
    allowed = key_allowed(positions, positions, prefix, valid_count, causal)
    scores = jnp.where(allowed[None], scores, masked_score)
    highest = lax.optimization_barrier(jnp.max(scores, axis=-1, keepdims=True))
    weights = jnp.exp(scores - highest)
    shares = low(weights / lax.optimization_barrier(jnp.sum(weights, axis=-1, keepdims=True)))
    mixture = jnp.einsum('hqk,khd->qhd', shares, value_rows, precision=lax.Precision.HIGHEST).reshape(SEQ_LEN, D)
    mixture = low(low_back(mixture))
    return low_back(matmul(mixture, weight_out))

def feed_forward(normed, weight_up, weight_down):
    hidden = low_back(matmul(normed, weight_up))
    active = low(jax.nn.gelu(hidden, approximate=True))
    return low_back(matmul(active, weight_down))

def one_sequence(residual, prefix, valid_count, which_section, params):
    gains, biases, scale_tables, shift_tables, weight_qkv, weight_out, weight_up, weight_down = params
    picker = (jnp.arange(SECTIONS, dtype=jnp.int32) == which_section).astype(jnp.float32)[None, :]
    for layer_index in range(2):
        for part_index in range(2):
            if layer_index == 0:
                normed = fixed_norm(residual, gains[part_index], biases[part_index])
            else:
                normed = section_norm(residual, scale_tables[part_index], shift_tables[part_index], picker)
            normed = low(normed)
            if part_index == 0:
                branch = attention(normed, weight_qkv[layer_index], weight_out[layer_index], prefix, valid_count, layer_index == 0)
            else:
                branch = feed_forward(normed, weight_up[layer_index], weight_down[layer_index])
            residual = residual + branch
    return residual

def reference(frames_in, phone_len, frame_len, section, norm_gain, norm_bias, ada_scale, ada_shift, w_qkv, w_out, w_up, w_down, out_grad):
    params = (norm_gain.astype(jnp.float32), norm_bias.astype(jnp.float32), ada_scale.astype(jnp.float32), ada_shift.astype(jnp.float32), w_qkv.astype(jnp.float32), w_out.astype(jnp.float32), w_up.astype(jnp.float32), w_down.astype(jnp.float32))
    inputs = frames_in.astype(jnp.float32).reshape(MICRO * SEQS, SEQ_LEN, D)
    prefixes = phone_len.reshape(MICRO * SEQS).astype(jnp.int32)
    valid_counts = (phone_len + frame_len).reshape(MICRO * SEQS).astype(jnp.int32)
    section_ids = section.reshape(MICRO * SEQS).astype(jnp.int32)
    checked = jax.checkpoint(one_sequence)

    def run_all(all_inputs, all_params):

        def scan_step(scan_carry, scan_item):
            residual, prefix, valid_count, which_section = scan_item
            return (scan_carry, checked(residual, prefix, valid_count, which_section, all_params))
        _, frames_all = lax.scan(scan_step, None, (all_inputs, prefixes, valid_counts, section_ids))
        return frames_all
    frames_all, pullback = jax.vjp(run_all, inputs, params)
    cotangent = out_grad.astype(jnp.float32).reshape(MICRO * SEQS, SEQ_LEN, D)
    grad_inputs, grad_params = pullback(cotangent)
    frames_out = frames_all.reshape(MICRO, SEQS, SEQ_LEN, D)
    frames_grad = grad_inputs.reshape(MICRO, SEQS, SEQ_LEN, D)
    return (frames_out, frames_grad, grad_params[4], grad_params[5], grad_params[6], grad_params[7], grad_params[0], grad_params[1], grad_params[2], grad_params[3])
```

```python
from functools import partial

import jax
import jax.numpy as jnp
from jax import lax
from jax.experimental import pallas as pl
from jax.experimental.pallas import tpu as pltpu
from jax.sharding import PartitionSpec as P

HEAD_DIM = 64


norm_eps = 1e-05
masked_score = -1000000000.0
contract_rows = (((0,), (0,)), ((), ()))
contract_cols = (((1,), (1,)), ((), ()))


def plain_norm(inputs):
    centered = inputs - jnp.mean(inputs, axis=-1, keepdims=True)
    variance = jnp.mean(centered * centered, axis=-1, keepdims=True)
    return centered * lax.rsqrt(variance + norm_eps)


def fixed_norm(inputs, gain_row, shift_row):
    return plain_norm(inputs) * gain_row + shift_row


def section_norm(inputs, scale_table, shift_table, picker):
    scale_row = jnp.dot(
        picker, scale_table, precision=lax.Precision.HIGHEST, preferred_element_type=jnp.float32
    )
    shift_row = jnp.dot(
        picker, shift_table, precision=lax.Precision.HIGHEST, preferred_element_type=jnp.float32
    )
    return plain_norm(inputs) * scale_row + shift_row


def gather_normed(normed_low):
    return lax.all_gather(normed_low, "tensor", axis=0, tiled=True)


def gather_again(normed_low):
    return lax.all_gather(normed_low, "tensor", axis=0, tiled=True)


def sum_branch(branch_part):
    return lax.psum_scatter(
        branch_part.astype(jnp.bfloat16), "tensor", scatter_dimension=0, tiled=True
    ).astype(jnp.float32)


def gather_grad(grad_low):
    return lax.all_gather(grad_low, "tensor", axis=0, tiled=True)


def sum_normed(grad_part):
    return lax.psum_scatter(
        grad_part.astype(jnp.bfloat16), "tensor", scatter_dimension=0, tiled=True
    ).astype(jnp.float32)


def key_allowed(query_pos, key_pos, prefix, valid_count, causal):
    allowed = key_pos[None, :] < valid_count
    if causal:
        allowed = allowed & ((key_pos[None, :] < prefix) | (key_pos[None, :] <= query_pos[:, None]))
    return allowed


def split_heads(projected):
    length = projected.shape[0]
    head_width = projected.shape[1] // 3
    head_count = head_width // HEAD_DIM
    query_rows = projected[:, :head_width].reshape(length, head_count, HEAD_DIM)
    key_rows = projected[:, head_width : 2 * head_width].reshape(length, head_count, HEAD_DIM)
    value_rows = projected[:, 2 * head_width :].reshape(length, head_count, HEAD_DIM)
    return (query_rows, key_rows, value_rows)


def block_scores(query_block, key_rows, block_start, prefix, valid_count, causal):
    block_rows = query_block.shape[0]
    length = key_rows.shape[0]
    scores = jnp.einsum(
        "qhd,khd->hqk", query_block, key_rows, preferred_element_type=jnp.float32
    ) * HEAD_DIM ** (-0.5)
    query_pos = block_start + lax.iota(jnp.int32, block_rows)
    key_pos = lax.iota(jnp.int32, length)
    allowed = key_allowed(query_pos, key_pos, prefix, valid_count, causal)
    return jnp.where(allowed[None], scores, masked_score)


def attend_forward(projected, prefix, valid_count, causal, block_rows):
    length = projected.shape[0]
    head_width = projected.shape[1] // 3
    query_rows, key_rows, value_rows = split_heads(projected)

    def one_block(block_start):
        query_block = lax.dynamic_slice_in_dim(query_rows, block_start, block_rows, 0)
        scores = block_scores(query_block, key_rows, block_start, prefix, valid_count, causal)
        highest = jnp.max(scores, axis=-1, keepdims=True)
        row_total = jnp.sum(jnp.exp(scores - highest), axis=-1, keepdims=True)
        log_total = highest + jnp.log(row_total)
        shares = jnp.exp(scores - log_total).astype(jnp.bfloat16)
        mixture = jnp.einsum("hqk,khd->qhd", shares, value_rows, preferred_element_type=jnp.float32)
        return (mixture.astype(jnp.bfloat16), log_total)

    starts = lax.iota(jnp.int32, length // block_rows) * block_rows
    mixture, log_totals = lax.map(one_block, starts)
    return (mixture.reshape(length, head_width), log_totals)


def attend_backward(projected, log_totals, grad_mixture, prefix, valid_count, causal, block_rows):
    length = projected.shape[0]
    head_width = projected.shape[1] // 3
    query_rows, key_rows, value_rows = split_heads(projected)
    grad_rows = grad_mixture.reshape(query_rows.shape)
    score_scale = HEAD_DIM ** (-0.5)

    def one_block(grad_state, block_item):
        block_start, log_total = block_item
        grad_key, grad_value = grad_state
        query_block = lax.dynamic_slice_in_dim(query_rows, block_start, block_rows, 0)
        grad_block = lax.dynamic_slice_in_dim(grad_rows, block_start, block_rows, 0)
        scores = block_scores(query_block, key_rows, block_start, prefix, valid_count, causal)
        shares = jnp.exp(scores - log_total)
        shares_low = shares.astype(jnp.bfloat16)
        grad_shares = jnp.einsum(
            "qhd,khd->hqk", grad_block, value_rows, preferred_element_type=jnp.float32
        )
        inner_sum = jnp.sum(shares * grad_shares, axis=-1, keepdims=True)
        grad_scores = (shares * (grad_shares - inner_sum)).astype(jnp.bfloat16)
        grad_query = (
            jnp.einsum("hqk,khd->qhd", grad_scores, key_rows, preferred_element_type=jnp.float32)
            * score_scale
        )
        grad_key = (
            grad_key
            + jnp.einsum(
                "hqk,qhd->khd", grad_scores, query_block, preferred_element_type=jnp.float32
            )
            * score_scale
        )
        grad_value = grad_value + jnp.einsum(
            "hqk,qhd->khd", shares_low, grad_block, preferred_element_type=jnp.float32
        )
        return ((grad_key, grad_value), grad_query)

    starts = lax.iota(jnp.int32, length // block_rows) * block_rows
    zero_rows = jnp.zeros(query_rows.shape, jnp.float32)
    grad_state, grad_query = lax.scan(one_block, (zero_rows, zero_rows), (starts, log_totals))
    grad_key, grad_value = grad_state
    joined = jnp.concatenate(
        [
            grad_query.reshape(length, head_width),
            grad_key.reshape(length, head_width),
            grad_value.reshape(length, head_width),
        ],
        axis=1,
    )
    return joined.astype(jnp.bfloat16)


def grouped_device(
    frames_in,
    phone_len,
    frame_len,
    section,
    norm_gain,
    norm_bias,
    ada_scale,
    ada_shift,
    w_qkv,
    w_out,
    w_up,
    w_down,
    out_grad,
):
    micro_count, local_seqs, local_rows, model_width = frames_in.shape
    seq_length = local_rows * lax.axis_size("tensor")
    block_rows = min(512, seq_length)
    section_count = ada_scale.shape[1]
    qkv_mats = [w_qkv[layer_index].reshape(model_width, -1) for layer_index in range(2)]
    acc_qkv = [jnp.zeros(qkv_mats[layer_index].shape, jnp.float32) for layer_index in range(2)]
    acc_out = [jnp.zeros(w_out.shape[1:], jnp.float32) for layer_index in range(2)]
    acc_up = [jnp.zeros(w_up.shape[1:], jnp.float32) for layer_index in range(2)]
    acc_down = [jnp.zeros(w_down.shape[1:], jnp.float32) for layer_index in range(2)]
    acc_gain = [jnp.zeros((model_width,), jnp.float32) for part_index in range(2)]
    acc_bias = [jnp.zeros((model_width,), jnp.float32) for part_index in range(2)]
    acc_scale = [jnp.zeros((section_count, model_width), jnp.float32) for part_index in range(2)]
    acc_shift = [jnp.zeros((section_count, model_width), jnp.float32) for part_index in range(2)]
    frames_list = []
    grads_list = []
    for micro_index in range(micro_count):
        prefix = phone_len[micro_index, 0]
        valid_count = prefix + frame_len[micro_index, 0]
        picker = (lax.iota(jnp.int32, section_count) == section[micro_index, 0]).astype(
            jnp.float32
        )[None, :]
        residual = frames_in[micro_index, 0].astype(jnp.float32)
        stored = []
        for layer_index in range(2):
            for part_index in range(2):
                if layer_index == 0:
                    normed, norm_back = jax.vjp(
                        fixed_norm, residual, norm_gain[part_index], norm_bias[part_index]
                    )
                else:
                    normed, norm_back = jax.vjp(
                        partial(section_norm, picker=picker),
                        residual,
                        ada_scale[part_index],
                        ada_shift[part_index],
                    )
                normed_low = normed.astype(jnp.bfloat16)
                gathered = gather_normed(normed_low)
                if part_index == 0:
                    projected = jnp.dot(
                        gathered, qkv_mats[layer_index], preferred_element_type=jnp.float32
                    ).astype(jnp.bfloat16)
                    mixture, log_totals = attend_forward(
                        projected, prefix, valid_count, layer_index == 0, block_rows
                    )
                    branch = sum_branch(
                        jnp.dot(mixture, w_out[layer_index], preferred_element_type=jnp.float32)
                    )
                    saved_state = (projected, log_totals, mixture)
                else:
                    hidden = jnp.dot(
                        gathered, w_up[layer_index], preferred_element_type=jnp.float32
                    )
                    active = jax.nn.gelu(hidden, approximate=True).astype(jnp.bfloat16)
                    branch = sum_branch(
                        jnp.dot(active, w_down[layer_index], preferred_element_type=jnp.float32)
                    )
                    saved_state = (hidden, active)
                kept_rows = normed_low
                stored.append((norm_back, kept_rows, saved_state))
                residual = residual + branch
        out_group = [residual]
        grad_rows = out_grad[micro_index, 0].astype(jnp.float32)
        for layer_index in (1, 0):
            for part_index in (1, 0):
                norm_back, kept_rows, saved_state = stored[2 * layer_index + part_index]
                gathered = gather_again(kept_rows)
                grad_whole = gather_grad(grad_rows.astype(jnp.bfloat16))
                if part_index == 1:
                    hidden, active = saved_state
                    acc_down[layer_index] = acc_down[layer_index] + lax.dot_general(
                        active, grad_whole, contract_rows, preferred_element_type=jnp.float32
                    )
                    grad_active = lax.dot_general(
                        grad_whole,
                        w_down[layer_index],
                        contract_cols,
                        preferred_element_type=jnp.float32,
                    )
                    gelu_value, gelu_back = jax.vjp(partial(jax.nn.gelu, approximate=True), hidden)
                    grad_hidden = gelu_back(grad_active)[0].astype(jnp.bfloat16)
                    acc_up[layer_index] = acc_up[layer_index] + lax.dot_general(
                        gathered, grad_hidden, contract_rows, preferred_element_type=jnp.float32
                    )
                    grad_normed = sum_normed(
                        lax.dot_general(
                            grad_hidden,
                            w_up[layer_index],
                            contract_cols,
                            preferred_element_type=jnp.float32,
                        )
                    )
                else:
                    projected, log_totals, mixture = saved_state
                    acc_out[layer_index] = acc_out[layer_index] + lax.dot_general(
                        mixture, grad_whole, contract_rows, preferred_element_type=jnp.float32
                    )
                    grad_mixture = lax.dot_general(
                        grad_whole,
                        w_out[layer_index],
                        contract_cols,
                        preferred_element_type=jnp.float32,
                    ).astype(jnp.bfloat16)
                    grad_projected = attend_backward(
                        projected,
                        log_totals,
                        grad_mixture,
                        prefix,
                        valid_count,
                        layer_index == 0,
                        block_rows,
                    )
                    acc_qkv[layer_index] = acc_qkv[layer_index] + lax.dot_general(
                        gathered, grad_projected, contract_rows, preferred_element_type=jnp.float32
                    )
                    grad_normed = sum_normed(
                        lax.dot_general(
                            grad_projected,
                            qkv_mats[layer_index],
                            contract_cols,
                            preferred_element_type=jnp.float32,
                        )
                    )
                grad_input, grad_first, grad_second = norm_back(grad_normed)
                grad_rows = grad_rows + grad_input
                if layer_index == 0:
                    acc_gain[part_index] = acc_gain[part_index] + grad_first
                    acc_bias[part_index] = acc_bias[part_index] + grad_second
                else:
                    acc_scale[part_index] = acc_scale[part_index] + grad_first
                    acc_shift[part_index] = acc_shift[part_index] + grad_second
        grad_group = [grad_rows]
        frames_list.append(jnp.stack(out_group))
        grads_list.append(jnp.stack(grad_group))
    total_qkv, total_out, total_up, total_down = (
        lax.psum(jnp.stack(acc_qkv).astype(jnp.bfloat16), "dp").astype(jnp.float32),
        lax.psum(jnp.stack(acc_out).astype(jnp.bfloat16), "dp").astype(jnp.float32),
        lax.psum(jnp.stack(acc_up).astype(jnp.bfloat16), "dp").astype(jnp.float32),
        lax.psum(jnp.stack(acc_down).astype(jnp.bfloat16), "dp").astype(jnp.float32),
    )
    norm_totals = lax.psum(
        (jnp.stack(acc_gain), jnp.stack(acc_bias), jnp.stack(acc_scale), jnp.stack(acc_shift)),
        ("dp", "tensor"),
    )
    return (
        jnp.stack(frames_list),
        jnp.stack(grads_list),
        total_qkv.reshape(2, model_width, 3, -1),
        total_out,
        total_up,
        total_down,
        norm_totals[0],
        norm_totals[1],
        norm_totals[2],
        norm_totals[3],
    )


bf16,f32=jnp.bfloat16,jnp.float32
NT=(((1,),(1,)),((),()))
TN=(((0,),(0,)),((),()))

def _limits(lims_ref, start, rows, causal, axis):
    prefix, valid = lims_ref[0], lims_ref[1]
    shape=(rows,1) if axis==0 else (1,rows)
    pos=start+lax.broadcasted_iota(jnp.int32,shape,axis)
    if causal:
        return jnp.minimum(jnp.maximum(pos,prefix-1),valid-1)
    return jnp.zeros(shape,jnp.int32)+(valid-1)

def fwd_kernel(causal, bq, lims_ref, q_ref, k_ref, v_ref, o_ref, l_ref):
    length=q_ref.shape[0]
    lane=lax.broadcasted_iota(jnp.int32,(bq,128),1)
    def block(start, kk):
        q=q_ref[pl.ds(start,bq),:]*jnp.asarray(0.125,bf16)
        lim=_limits(lims_ref,start,bq,causal,0)
        outs=[];rows=[]
        for h in range(2):
            qm=jnp.where((lane<HEAD_DIM)==(h==0),q,jnp.zeros_like(q))
            s=lax.dot_general(qm,k_ref[0:kk,:],NT,preferred_element_type=f32)
            key=lax.broadcasted_iota(jnp.int32,(bq,kk),1)
            s=jnp.where(key<=lim,s,-1e9)
            m=jnp.max(s,axis=1,keepdims=True)
            e=jnp.exp(s-m)
            l=jnp.sum(e,axis=1,keepdims=True)
            o=jnp.dot(e.astype(bf16),v_ref[0:kk,:],preferred_element_type=f32)*(1.0/l)
            outs.append(o); rows.append(m+jnp.log(l))
        o_ref[pl.ds(start,bq),:]=jnp.where(lane<HEAD_DIM,outs[0],outs[1]).astype(bf16)
        both=jnp.where(lane<HEAD_DIM,rows[0],rows[1])
        bt=both.T
        l_ref[0,0:1,pl.ds(start,bq)]=bt[0:1,:]
        l_ref[0,1:2,pl.ds(start,bq)]=bt[HEAD_DIM:HEAD_DIM+1,:]
    nq=length//bq
    if causal:
        for i in range(nq): block(i*bq,(i+1)*bq)
    else:
        def body(i,c):
            block(pl.multiple_of(i*bq,bq),length); return c
        lax.fori_loop(0,nq,body,0)

def attn_fwd(qkv, lims, causal, bq=256):
    length=qkv.shape[0]; width=qkv.shape[1]//3; pairs=width//128
    spec=lambda off: pl.BlockSpec((length,128),lambda i,off=off:(0,off*pairs+i))
    return pl.pallas_call(partial(fwd_kernel,causal,bq),
        grid=(pairs,),
        in_specs=[pl.BlockSpec(memory_space=pltpu.SMEM),spec(0),spec(1),spec(2)],
        out_specs=[pl.BlockSpec((length,128),lambda i:(0,i)),pl.BlockSpec((1,2,length),lambda i:(i,0,0))],
        out_shape=[jax.ShapeDtypeStruct((length,width),bf16),jax.ShapeDtypeStruct((pairs,2,length),f32)],
        compiler_params=pltpu.CompilerParams(vmem_limit_bytes=48*2**20),
        cost_estimate=pl.CostEstimate(flops=pairs*2*4*length*length*128,bytes_accessed=length*width*8,transcendentals=pairs*2*length*length),
        name="attn_fwd_"+("causal" if causal else "full"),
    )(lims,qkv,qkv,qkv)

def bwd_kernel(causal,bq,lims_ref,q_ref,k_ref,v_ref,l_ref,do_ref,grad_ref,dk_acc,dv_acc):
    length=q_ref.shape[0]
    lane=lax.broadcasted_iota(jnp.int32,(bq,128),1)
    dk_acc[...]=jnp.zeros_like(dk_acc); dv_acc[...]=jnp.zeros_like(dv_acc)
    width=grad_ref.shape[1]//3
    at=[pl.multiple_of(part*width+pl.program_id(0)*128,128) for part in range(3)]
    def block(start,kk):
        q=q_ref[pl.ds(start,bq),:]*jnp.asarray(0.125,bf16)
        do=do_ref[pl.ds(start,bq),:]
        lim=_limits(lims_ref,start,bq,causal,1)
        dqs=[]
        for h in range(2):
            sel=(lane<HEAD_DIM)==(h==0)
            qm=jnp.where(sel,q,jnp.zeros_like(q)); dom=jnp.where(sel,do,jnp.zeros_like(do))
            s=lax.dot_general(k_ref[0:kk,:],qm,NT,preferred_element_type=f32)
            dp=lax.dot_general(v_ref[0:kk,:],dom,NT,preferred_element_type=f32)
            key=lax.broadcasted_iota(jnp.int32,(kk,bq),0)
            lrow=l_ref[0,h:h+1,pl.ds(start,bq)]
            p=jnp.where(key<=lim,jnp.exp(s-lrow),0.0)
            pd=p*dp
            D=jnp.sum(pd,axis=0,keepdims=True)
            ds=(pd-p*D).astype(bf16)
            dv_acc[0:kk,:]+=jnp.dot(p.astype(bf16),dom,preferred_element_type=f32)
            dk_acc[0:kk,:]+=jnp.dot(ds,qm,preferred_element_type=f32)
            dqs.append(lax.dot_general(ds,k_ref[0:kk,:],TN,preferred_element_type=f32))
        grad_ref[pl.ds(start,bq),pl.ds(at[0],128)]=(jnp.where(lane<HEAD_DIM,dqs[0],dqs[1])*0.125).astype(bf16)
    nq=length//bq
    if causal:
        for i in range(nq): block(i*bq,(i+1)*bq)
    else:
        def body(i,c):
            block(pl.multiple_of(i*bq,bq),length); return c
        lax.fori_loop(0,nq,body,0)
    grad_ref[:,pl.ds(at[1],128)]=dk_acc[...].astype(bf16)
    grad_ref[:,pl.ds(at[2],128)]=dv_acc[...].astype(bf16)

def attn_bwd(qkv,L,do,lims,causal,bq=256):
    length=qkv.shape[0]; width=qkv.shape[1]//3; pairs=width//128
    spec=lambda off: pl.BlockSpec((length,128),lambda i,off=off:(0,off*pairs+i))
    one=pl.BlockSpec((length,128),lambda i:(0,i))
    return pl.pallas_call(partial(bwd_kernel,causal,bq),
        grid=(pairs,),
        in_specs=[pl.BlockSpec(memory_space=pltpu.SMEM),spec(0),spec(1),spec(2),pl.BlockSpec((1,2,length),lambda i:(i,0,0)),one],
        out_specs=pl.BlockSpec((length,3*width),lambda i:(0,0)),
        out_shape=jax.ShapeDtypeStruct((length,3*width),bf16),
        scratch_shapes=[pltpu.VMEM((length,128),f32)]*2,
        compiler_params=pltpu.CompilerParams(vmem_limit_bytes=48*2**20),
        cost_estimate=pl.CostEstimate(flops=pairs*2*10*length*length*128,bytes_accessed=length*width*14,transcendentals=pairs*2*length*length),
        name="attn_bwd_"+("causal" if causal else "full"),
    )(lims,qkv,qkv,qkv,L,do)


def swap_tensor(block):
    return lax.ppermute(block, "tensor", [(0, 1), (1, 0)])


def swap_bit(block, bit, dp_size):
    return lax.ppermute(block, "dp", [(place, place ^ (1 << bit)) for place in range(dp_size)])


def in_order(flag, mine, other):
    first = jnp.where(flag == 0, mine, other)
    second = jnp.where(flag == 0, other, mine)
    return jnp.concatenate([first, second], axis=0)


def add_rounded(left, right):
    return (left.astype(f32) + right.astype(f32)).astype(bf16)


def norm_forward(rows, gain_row, shift_row):
    mean = jnp.mean(rows, axis=-1, keepdims=True)
    centered = rows - mean
    rate = lax.rsqrt(jnp.mean(centered * centered, axis=-1, keepdims=True) + norm_eps)
    normed = centered * rate * gain_row + shift_row
    return normed.astype(bf16), (rows, mean, rate)


def norm_backward(saved, grad_normed, gain_row):
    rows, mean, rate = saved
    unit = (rows - mean) * rate
    grad_unit = grad_normed * gain_row
    grad_rows = rate * (
        grad_unit
        - jnp.mean(grad_unit, axis=-1, keepdims=True)
        - unit * jnp.mean(grad_unit * unit, axis=-1, keepdims=True)
    )
    return grad_rows, jnp.sum(grad_normed * unit, axis=0), jnp.sum(grad_normed, axis=0)


def gelu_pair(hidden):
    square = hidden * hidden
    inner = 0.7978845608 * hidden * (1.0 + 0.044715 * square)
    bent = jnp.tanh(inner)
    value = 0.5 * hidden * (1.0 + bent)
    slope = 0.5 * (1.0 + bent) + 0.5 * hidden * (1.0 - bent * bent) * 0.7978845608 * (
        1.0 + 3.0 * 0.044715 * square
    )
    return value.astype(bf16), slope.astype(bf16)


def dot_sum(pairs, dims):
    total = None
    for left, right in pairs:
        term = lax.dot_general(left, right, dims, preferred_element_type=f32)
        total = term if total is None else total + term
    return total


NN = (((1,), (0,)), ((), ()))


def quarter_of(kind, half, place):
    if kind == "qkv":
        heads = half.reshape(half.shape[0], 3, -1)
        width = heads.shape[2] // 2
        picked = lax.dynamic_slice_in_dim(heads, place * width, width, 2)
        return picked.reshape(half.shape[0], 3 * width)
    axis = 1 if kind == "up" else 0
    width = half.shape[axis] // 2
    return lax.dynamic_slice_in_dim(half, place * width, width, axis)


def row_half(block, place):
    height = block.shape[0] // 2
    return lax.dynamic_slice_in_dim(block, place * height, height, 0)


def paired_device(
    dp_size,
    frames_in,
    phone_len,
    frame_len,
    section,
    norm_gain,
    norm_bias,
    ada_scale,
    ada_shift,
    w_qkv,
    w_out,
    w_up,
    w_down,
    out_grad,
):
    model_width = frames_in.shape[3]
    section_count = ada_scale.shape[1]
    side = lax.axis_index("tensor")
    place = lax.axis_index("dp")
    bit_count = dp_size.bit_length() - 1
    bits = [(place >> bit) & 1 for bit in range(bit_count)]
    core = bits[0]

    def whole_rows(halves):
        mine = lax.dynamic_index_in_dim(halves[:, 0], side, 0, keepdims=False)
        away = lax.dynamic_index_in_dim(halves[:, 0], 1 - side, 0, keepdims=False)
        return in_order(side, mine, swap_tensor(away))

    def split_rows(rows):
        height = rows.shape[0] // 2
        mine = lax.dynamic_slice_in_dim(rows, side * height, height, 0)
        away = lax.dynamic_slice_in_dim(rows, (1 - side) * height, height, 0)
        other = swap_tensor(away.astype(bf16)).astype(f32)
        first = jnp.where(side == 0, mine, other)
        second = jnp.where(side == 0, other, mine)
        return jnp.stack([first, second])[:, None]

    def other_half(kind, half):
        piece = row_half(quarter_of(kind, half, core), bits[1])
        piece = swap_tensor(piece)
        near = in_order(bits[1], piece, swap_bit(piece, 1, dp_size))
        far = swap_bit(near, 0, dp_size)
        return [half, near, far]

    def reduce_grad(kind, grads):
        own, near, far = grads
        own_there = swap_bit(quarter_of(kind, own, 1 - core), 0, dp_size)
        near_there = swap_bit(far, 0, dp_size)
        across = swap_tensor(add_rounded(near, near_there))
        total = quarter_of(kind, own, core).astype(f32) + own_there.astype(f32) + across.astype(f32)
        total = total.astype(bf16)
        for bit in range(1, bit_count):
            sent = swap_bit(row_half(total, 1 - bits[bit]), bit, dp_size)
            total = add_rounded(row_half(total, bits[bit]), sent)
        whole = lax.all_gather(total, "dp", axis=0, tiled=False)
        rows, columns = total.shape
        whole = whole.reshape((2,) * bit_count + (rows, columns))
        order = tuple(bit_count - 1 - bit for bit in range(1, bit_count))
        core_axis = bit_count - 1
        full_rows = rows * 2 ** (bit_count - 1)
        if kind in ("out", "down"):
            whole = whole.transpose((core_axis,) + order + (bit_count, bit_count + 1))
            return whole.reshape(2 * full_rows, columns)
        if kind == "up":
            whole = whole.transpose(order + (bit_count, core_axis, bit_count + 1))
            return whole.reshape(full_rows, 2 * columns)
        whole = whole.reshape((2,) * bit_count + (rows, 3, columns // 3))
        whole = whole.transpose(order + (bit_count, bit_count + 1, core_axis, bit_count + 2))
        return whole.reshape(full_rows, 3, 2 * columns // 3)

    prefix = lax.dynamic_index_in_dim(phone_len[:, 0], side, 0, keepdims=False)
    frames = lax.dynamic_index_in_dim(frame_len[:, 0], side, 0, keepdims=False)
    chosen = lax.dynamic_index_in_dim(section[:, 0], side, 0, keepdims=False)
    limits = jnp.stack([prefix, prefix + frames]).astype(jnp.int32)
    picker = (lax.iota(jnp.int32, section_count) == chosen).astype(f32)[:, None]

    gains = [
        [norm_gain[0], norm_gain[1]],
        [jnp.sum(picker * ada_scale[part], axis=0) for part in range(2)],
    ]
    shifts = [
        [norm_bias[0], norm_bias[1]],
        [jnp.sum(picker * ada_shift[part], axis=0) for part in range(2)],
    ]

    rows = whole_rows(frames_in).astype(f32)
    weights = []
    for layer in range(2):
        weights.append(
            {
                "qkv": other_half("qkv", w_qkv[layer].reshape(model_width, -1)),
                "out": other_half("out", w_out[layer]),
                "up": other_half("up", w_up[layer]),
                "down": other_half("down", w_down[layer]),
            }
        )
    kept = []
    for layer in range(2):
        causal = layer == 0
        mats = weights[layer]
        normed, norm_kept = norm_forward(rows, gains[layer][0], shifts[layer][0])
        projected = [
            jnp.dot(normed, part, preferred_element_type=f32).astype(bf16) for part in mats["qkv"]
        ]
        mixed = [attn_fwd(part, limits, causal, 512) for part in projected]
        rows = rows + dot_sum([(mix[0], part) for mix, part in zip(mixed, mats["out"])], NN)
        kept.append((normed, norm_kept, projected, mixed))
        normed, norm_kept = norm_forward(rows, gains[layer][1], shifts[layer][1])
        pairs = [gelu_pair(jnp.dot(normed, part, preferred_element_type=f32)) for part in mats["up"]]
        rows = rows + dot_sum([(pair[0], part) for pair, part in zip(pairs, mats["down"])], NN)
        kept.append((normed, norm_kept, pairs))
    frames_out = split_rows(rows)

    grad_rows = whole_rows(out_grad).astype(f32)
    sums = {}
    norm_sums = [[None, None], [None, None]]
    for layer in (1, 0):
        causal = layer == 0
        mats = weights[layer]
        normed, norm_kept, pairs = kept[2 * layer + 1]
        low = grad_rows.astype(bf16)
        grad_hidden = [
            (
                lax.dot_general(low, part, NT, preferred_element_type=f32) * pair[1].astype(f32)
            ).astype(bf16)
            for pair, part in zip(pairs, mats["down"])
        ]
        sums["down", layer] = reduce_grad(
            "down",
            [
                lax.dot_general(pair[0], low, TN, preferred_element_type=f32).astype(bf16)
                for pair in pairs
            ],
        )
        sums["up", layer] = reduce_grad(
            "up",
            [
                lax.dot_general(normed, part, TN, preferred_element_type=f32).astype(bf16)
                for part in grad_hidden
            ],
        )
        grad_normed = dot_sum(list(zip(grad_hidden, mats["up"])), NT)
        added, grad_gain, grad_shift = norm_backward(norm_kept, grad_normed, gains[layer][1])
        norm_sums[layer][1] = (grad_gain, grad_shift)
        grad_rows = grad_rows + added

        normed, norm_kept, projected, mixed = kept[2 * layer]
        low = grad_rows.astype(bf16)
        sums["out", layer] = reduce_grad(
            "out",
            [
                lax.dot_general(mix[0], low, TN, preferred_element_type=f32).astype(bf16)
                for mix in mixed
            ],
        )
        grad_mixed = [
            lax.dot_general(low, part, NT, preferred_element_type=f32).astype(bf16)
            for part in mats["out"]
        ]
        grad_projected = [
            attn_bwd(part, mix[1], grad_mix, limits, causal, 512)
            for part, mix, grad_mix in zip(projected, mixed, grad_mixed)
        ]
        sums["qkv", layer] = reduce_grad(
            "qkv",
            [
                lax.dot_general(normed, part, TN, preferred_element_type=f32).astype(bf16)
                for part in grad_projected
            ],
        )
        grad_normed = dot_sum(list(zip(grad_projected, mats["qkv"])), NT)
        added, grad_gain, grad_shift = norm_backward(norm_kept, grad_normed, gains[layer][0])
        norm_sums[layer][0] = (grad_gain, grad_shift)
        grad_rows = grad_rows + added

    frames_grad = split_rows(grad_rows)

    def everywhere(block):
        block = block + swap_tensor(block)
        for bit in range(bit_count):
            block = block + swap_bit(block, bit, dp_size)
        return block

    late = everywhere(
        jnp.stack(
            [
                norm_sums[0][0][0],
                norm_sums[0][1][0],
                norm_sums[0][0][1],
                norm_sums[0][1][1],
            ]
        )
    )
    early = everywhere(
        jnp.concatenate(
            [
                picker * norm_sums[1][0][0][None],
                picker * norm_sums[1][1][0][None],
                picker * norm_sums[1][0][1][None],
                picker * norm_sums[1][1][1][None],
            ]
        )
    ).reshape(4, section_count, model_width)

    def both(kind):
        return jnp.stack([sums[kind, 0].astype(f32), sums[kind, 1].astype(f32)])

    return (
        frames_out,
        frames_grad,
        both("qkv"),
        both("out"),
        both("up"),
        both("down"),
        late[0:2],
        late[2:4],
        early[0:2],
        early[2:4],
    )


def per_device(dp_size, tensor_size, *arrays):
    micro_count, local_seqs = arrays[0].shape[:2]
    paired = micro_count == 2 and tensor_size == 2 and local_seqs == 1
    if paired and dp_size >= 4 and dp_size & (dp_size - 1) == 0:
        return paired_device(dp_size, *arrays)
    return grouped_device(*arrays)


def solution(mesh):
    return jax.shard_map(
        partial(per_device, mesh.shape["dp"], mesh.shape["tensor"]),
        mesh=mesh,
        in_specs=(
            P(None, "dp", "tensor", None),
            P(None, "dp"),
            P(None, "dp"),
            P(None, "dp"),
            P(),
            P(),
            P(),
            P(),
            P(None, None, None, "tensor"),
            P(None, "tensor", None),
            P(None, None, "tensor"),
            P(None, "tensor", None),
            P(None, "dp", "tensor", None),
        ),
        out_specs=(
            P(None, "dp", "tensor", None),
            P(None, "dp", "tensor", None),
            P(None, None, None, "tensor"),
            P(None, "tensor", None),
            P(None, None, "tensor"),
            P(None, "tensor", None),
            P(),
            P(),
            P(),
            P(),
        ),
        check_vma=False,
    )
```

```python
from functools import partial

import jax
import jax.numpy as jnp
from jax import lax
from jax.experimental import pallas as pl
from jax.experimental.pallas import tpu as pltpu
from jax.sharding import PartitionSpec as P

HEAD_DIM = 64


norm_eps = 1e-05
masked_score = -1000000000.0
contract_rows = (((0,), (0,)), ((), ()))
contract_cols = (((1,), (1,)), ((), ()))


def plain_norm(inputs):
    centered = inputs - jnp.mean(inputs, axis=-1, keepdims=True)
    variance = jnp.mean(centered * centered, axis=-1, keepdims=True)
    return centered * lax.rsqrt(variance + norm_eps)


def fixed_norm(inputs, gain_row, shift_row):
    return plain_norm(inputs) * gain_row + shift_row


def section_norm(inputs, scale_table, shift_table, picker):
    scale_row = jnp.dot(
        picker, scale_table, precision=lax.Precision.HIGHEST, preferred_element_type=jnp.float32
    )
    shift_row = jnp.dot(
        picker, shift_table, precision=lax.Precision.HIGHEST, preferred_element_type=jnp.float32
    )
    return plain_norm(inputs) * scale_row + shift_row


def gather_normed(normed_low):
    return lax.all_gather(normed_low, "tensor", axis=0, tiled=True)


def gather_again(normed_low):
    return lax.all_gather(normed_low, "tensor", axis=0, tiled=True)


def sum_branch(branch_part):
    return lax.psum_scatter(
        branch_part.astype(jnp.bfloat16), "tensor", scatter_dimension=0, tiled=True
    ).astype(jnp.float32)


def gather_grad(grad_low):
    return lax.all_gather(grad_low, "tensor", axis=0, tiled=True)


def sum_normed(grad_part):
    return lax.psum_scatter(
        grad_part.astype(jnp.bfloat16), "tensor", scatter_dimension=0, tiled=True
    ).astype(jnp.float32)


def key_allowed(query_pos, key_pos, prefix, valid_count, causal):
    allowed = key_pos[None, :] < valid_count
    if causal:
        allowed = allowed & ((key_pos[None, :] < prefix) | (key_pos[None, :] <= query_pos[:, None]))
    return allowed


def split_heads(projected):
    length = projected.shape[0]
    head_width = projected.shape[1] // 3
    head_count = head_width // HEAD_DIM
    query_rows = projected[:, :head_width].reshape(length, head_count, HEAD_DIM)
    key_rows = projected[:, head_width : 2 * head_width].reshape(length, head_count, HEAD_DIM)
    value_rows = projected[:, 2 * head_width :].reshape(length, head_count, HEAD_DIM)
    return (query_rows, key_rows, value_rows)


def block_scores(query_block, key_rows, block_start, prefix, valid_count, causal):
    block_rows = query_block.shape[0]
    length = key_rows.shape[0]
    scores = jnp.einsum(
        "qhd,khd->hqk", query_block, key_rows, preferred_element_type=jnp.float32
    ) * HEAD_DIM ** (-0.5)
    query_pos = block_start + lax.iota(jnp.int32, block_rows)
    key_pos = lax.iota(jnp.int32, length)
    allowed = key_allowed(query_pos, key_pos, prefix, valid_count, causal)
    return jnp.where(allowed[None], scores, masked_score)


def attend_forward(projected, prefix, valid_count, causal, block_rows):
    length = projected.shape[0]
    head_width = projected.shape[1] // 3
    query_rows, key_rows, value_rows = split_heads(projected)

    def one_block(block_start):
        query_block = lax.dynamic_slice_in_dim(query_rows, block_start, block_rows, 0)
        scores = block_scores(query_block, key_rows, block_start, prefix, valid_count, causal)
        highest = jnp.max(scores, axis=-1, keepdims=True)
        row_total = jnp.sum(jnp.exp(scores - highest), axis=-1, keepdims=True)
        log_total = highest + jnp.log(row_total)
        shares = jnp.exp(scores - log_total).astype(jnp.bfloat16)
        mixture = jnp.einsum("hqk,khd->qhd", shares, value_rows, preferred_element_type=jnp.float32)
        return (mixture.astype(jnp.bfloat16), log_total)

    starts = lax.iota(jnp.int32, length // block_rows) * block_rows
    mixture, log_totals = lax.map(one_block, starts)
    return (mixture.reshape(length, head_width), log_totals)


def attend_backward(projected, log_totals, grad_mixture, prefix, valid_count, causal, block_rows):
    length = projected.shape[0]
    head_width = projected.shape[1] // 3
    query_rows, key_rows, value_rows = split_heads(projected)
    grad_rows = grad_mixture.reshape(query_rows.shape)
    score_scale = HEAD_DIM ** (-0.5)

    def one_block(grad_state, block_item):
        block_start, log_total = block_item
        grad_key, grad_value = grad_state
        query_block = lax.dynamic_slice_in_dim(query_rows, block_start, block_rows, 0)
        grad_block = lax.dynamic_slice_in_dim(grad_rows, block_start, block_rows, 0)
        scores = block_scores(query_block, key_rows, block_start, prefix, valid_count, causal)
        shares = jnp.exp(scores - log_total)
        shares_low = shares.astype(jnp.bfloat16)
        grad_shares = jnp.einsum(
            "qhd,khd->hqk", grad_block, value_rows, preferred_element_type=jnp.float32
        )
        inner_sum = jnp.sum(shares * grad_shares, axis=-1, keepdims=True)
        grad_scores = (shares * (grad_shares - inner_sum)).astype(jnp.bfloat16)
        grad_query = (
            jnp.einsum("hqk,khd->qhd", grad_scores, key_rows, preferred_element_type=jnp.float32)
            * score_scale
        )
        grad_key = (
            grad_key
            + jnp.einsum(
                "hqk,qhd->khd", grad_scores, query_block, preferred_element_type=jnp.float32
            )
            * score_scale
        )
        grad_value = grad_value + jnp.einsum(
            "hqk,qhd->khd", shares_low, grad_block, preferred_element_type=jnp.float32
        )
        return ((grad_key, grad_value), grad_query)

    starts = lax.iota(jnp.int32, length // block_rows) * block_rows
    zero_rows = jnp.zeros(query_rows.shape, jnp.float32)
    grad_state, grad_query = lax.scan(one_block, (zero_rows, zero_rows), (starts, log_totals))
    grad_key, grad_value = grad_state
    joined = jnp.concatenate(
        [
            grad_query.reshape(length, head_width),
            grad_key.reshape(length, head_width),
            grad_value.reshape(length, head_width),
        ],
        axis=1,
    )
    return joined.astype(jnp.bfloat16)


def grouped_device(
    frames_in,
    phone_len,
    frame_len,
    section,
    norm_gain,
    norm_bias,
    ada_scale,
    ada_shift,
    w_qkv,
    w_out,
    w_up,
    w_down,
    out_grad,
):
    micro_count, local_seqs, local_rows, model_width = frames_in.shape
    seq_length = local_rows * lax.axis_size("tensor")
    block_rows = min(512, seq_length)
    section_count = ada_scale.shape[1]
    qkv_mats = [w_qkv[layer_index].reshape(model_width, -1) for layer_index in range(2)]
    acc_qkv = [jnp.zeros(qkv_mats[layer_index].shape, jnp.float32) for layer_index in range(2)]
    acc_out = [jnp.zeros(w_out.shape[1:], jnp.float32) for layer_index in range(2)]
    acc_up = [jnp.zeros(w_up.shape[1:], jnp.float32) for layer_index in range(2)]
    acc_down = [jnp.zeros(w_down.shape[1:], jnp.float32) for layer_index in range(2)]
    acc_gain = [jnp.zeros((model_width,), jnp.float32) for part_index in range(2)]
    acc_bias = [jnp.zeros((model_width,), jnp.float32) for part_index in range(2)]
    acc_scale = [jnp.zeros((section_count, model_width), jnp.float32) for part_index in range(2)]
    acc_shift = [jnp.zeros((section_count, model_width), jnp.float32) for part_index in range(2)]
    frames_list = []
    grads_list = []
    for micro_index in range(micro_count):
        prefix = phone_len[micro_index, 0]
        valid_count = prefix + frame_len[micro_index, 0]
        picker = (lax.iota(jnp.int32, section_count) == section[micro_index, 0]).astype(
            jnp.float32
        )[None, :]
        residual = frames_in[micro_index, 0].astype(jnp.float32)
        stored = []
        for layer_index in range(2):
            for part_index in range(2):
                if layer_index == 0:
                    normed, norm_back = jax.vjp(
                        fixed_norm, residual, norm_gain[part_index], norm_bias[part_index]
                    )
                else:
                    normed, norm_back = jax.vjp(
                        partial(section_norm, picker=picker),
                        residual,
                        ada_scale[part_index],
                        ada_shift[part_index],
                    )
                normed_low = normed.astype(jnp.bfloat16)
                gathered = gather_normed(normed_low)
                if part_index == 0:
                    projected = jnp.dot(
                        gathered, qkv_mats[layer_index], preferred_element_type=jnp.float32
                    ).astype(jnp.bfloat16)
                    mixture, log_totals = attend_forward(
                        projected, prefix, valid_count, layer_index == 0, block_rows
                    )
                    branch = sum_branch(
                        jnp.dot(mixture, w_out[layer_index], preferred_element_type=jnp.float32)
                    )
                    saved_state = (projected, log_totals, mixture)
                else:
                    hidden = jnp.dot(
                        gathered, w_up[layer_index], preferred_element_type=jnp.float32
                    )
                    active = jax.nn.gelu(hidden, approximate=True).astype(jnp.bfloat16)
                    branch = sum_branch(
                        jnp.dot(active, w_down[layer_index], preferred_element_type=jnp.float32)
                    )
                    saved_state = (hidden, active)
                kept_rows = normed_low
                stored.append((norm_back, kept_rows, saved_state))
                residual = residual + branch
        out_group = [residual]
        grad_rows = out_grad[micro_index, 0].astype(jnp.float32)
        for layer_index in (1, 0):
            for part_index in (1, 0):
                norm_back, kept_rows, saved_state = stored[2 * layer_index + part_index]
                gathered = gather_again(kept_rows)
                grad_whole = gather_grad(grad_rows.astype(jnp.bfloat16))
                if part_index == 1:
                    hidden, active = saved_state
                    acc_down[layer_index] = acc_down[layer_index] + lax.dot_general(
                        active, grad_whole, contract_rows, preferred_element_type=jnp.float32
                    )
                    grad_active = lax.dot_general(
                        grad_whole,
                        w_down[layer_index],
                        contract_cols,
                        preferred_element_type=jnp.float32,
                    )
                    gelu_value, gelu_back = jax.vjp(partial(jax.nn.gelu, approximate=True), hidden)
                    grad_hidden = gelu_back(grad_active)[0].astype(jnp.bfloat16)
                    acc_up[layer_index] = acc_up[layer_index] + lax.dot_general(
                        gathered, grad_hidden, contract_rows, preferred_element_type=jnp.float32
                    )
                    grad_normed = sum_normed(
                        lax.dot_general(
                            grad_hidden,
                            w_up[layer_index],
                            contract_cols,
                            preferred_element_type=jnp.float32,
                        )
                    )
                else:
                    projected, log_totals, mixture = saved_state
                    acc_out[layer_index] = acc_out[layer_index] + lax.dot_general(
                        mixture, grad_whole, contract_rows, preferred_element_type=jnp.float32
                    )
                    grad_mixture = lax.dot_general(
                        grad_whole,
                        w_out[layer_index],
                        contract_cols,
                        preferred_element_type=jnp.float32,
                    ).astype(jnp.bfloat16)
                    grad_projected = attend_backward(
                        projected,
                        log_totals,
                        grad_mixture,
                        prefix,
                        valid_count,
                        layer_index == 0,
                        block_rows,
                    )
                    acc_qkv[layer_index] = acc_qkv[layer_index] + lax.dot_general(
                        gathered, grad_projected, contract_rows, preferred_element_type=jnp.float32
                    )
                    grad_normed = sum_normed(
                        lax.dot_general(
                            grad_projected,
                            qkv_mats[layer_index],
                            contract_cols,
                            preferred_element_type=jnp.float32,
                        )
                    )
                grad_input, grad_first, grad_second = norm_back(grad_normed)
                grad_rows = grad_rows + grad_input
                if layer_index == 0:
                    acc_gain[part_index] = acc_gain[part_index] + grad_first
                    acc_bias[part_index] = acc_bias[part_index] + grad_second
                else:
                    acc_scale[part_index] = acc_scale[part_index] + grad_first
                    acc_shift[part_index] = acc_shift[part_index] + grad_second
        grad_group = [grad_rows]
        frames_list.append(jnp.stack(out_group))
        grads_list.append(jnp.stack(grad_group))
    total_qkv, total_out, total_up, total_down = (
        lax.psum(jnp.stack(acc_qkv).astype(jnp.bfloat16), "dp").astype(jnp.float32),
        lax.psum(jnp.stack(acc_out).astype(jnp.bfloat16), "dp").astype(jnp.float32),
        lax.psum(jnp.stack(acc_up).astype(jnp.bfloat16), "dp").astype(jnp.float32),
        lax.psum(jnp.stack(acc_down).astype(jnp.bfloat16), "dp").astype(jnp.float32),
    )
    norm_totals = lax.psum(
        (jnp.stack(acc_gain), jnp.stack(acc_bias), jnp.stack(acc_scale), jnp.stack(acc_shift)),
        ("dp", "tensor"),
    )
    return (
        jnp.stack(frames_list),
        jnp.stack(grads_list),
        total_qkv.reshape(2, model_width, 3, -1),
        total_out,
        total_up,
        total_down,
        norm_totals[0],
        norm_totals[1],
        norm_totals[2],
        norm_totals[3],
    )


bf16,f32=jnp.bfloat16,jnp.float32
NT=(((1,),(1,)),((),()))
TN=(((0,),(0,)),((),()))

def _limits(lims_ref, start, rows, causal, axis):
    prefix, valid = lims_ref[0], lims_ref[1]
    shape=(rows,1) if axis==0 else (1,rows)
    pos=start+lax.broadcasted_iota(jnp.int32,shape,axis)
    if causal:
        return jnp.minimum(jnp.maximum(pos,prefix-1),valid-1)
    return jnp.zeros(shape,jnp.int32)+(valid-1)

def fwd_kernel(causal, bq, lims_ref, q_ref, k_ref, v_ref, o_ref, l_ref):
    length=q_ref.shape[0]
    lane=lax.broadcasted_iota(jnp.int32,(bq,128),1)
    def block(start, kk):
        q=q_ref[pl.ds(start,bq),:]*jnp.asarray(0.125,bf16)
        lim=_limits(lims_ref,start,bq,causal,0)
        outs=[];rows=[]
        for h in range(2):
            qm=jnp.where((lane<HEAD_DIM)==(h==0),q,jnp.zeros_like(q))
            s=lax.dot_general(qm,k_ref[0:kk,:],NT,preferred_element_type=f32)
            key=lax.broadcasted_iota(jnp.int32,(bq,kk),1)
            s=jnp.where(key<=lim,s,-1e9)
            m=jnp.max(s,axis=1,keepdims=True)
            e=jnp.exp(s-m)
            l=jnp.sum(e,axis=1,keepdims=True)
            o=jnp.dot(e.astype(bf16),v_ref[0:kk,:],preferred_element_type=f32)*(1.0/l)
            outs.append(o); rows.append(m+jnp.log(l))
        o_ref[pl.ds(start,bq),:]=jnp.where(lane<HEAD_DIM,outs[0],outs[1]).astype(bf16)
        both=jnp.where(lane<HEAD_DIM,rows[0],rows[1])
        bt=both.T
        l_ref[0,0:1,pl.ds(start,bq)]=bt[0:1,:]
        l_ref[0,1:2,pl.ds(start,bq)]=bt[HEAD_DIM:HEAD_DIM+1,:]
    nq=length//bq
    if causal:
        for i in range(nq): block(i*bq,(i+1)*bq)
    else:
        def body(i,c):
            block(pl.multiple_of(i*bq,bq),length); return c
        lax.fori_loop(0,nq,body,0)

def attn_fwd(qkv, lims, group, causal, bq=256):
    length=qkv.shape[0]; width=qkv.shape[1]//3; pairs=width//128
    per=group//128
    spec=lambda off: pl.BlockSpec((length,128),lambda i,off=off:(0,(i//per)*3*per+off*per+i%per))
    return pl.pallas_call(partial(fwd_kernel,causal,bq),
        grid=(pairs,),
        in_specs=[pl.BlockSpec(memory_space=pltpu.SMEM),spec(0),spec(1),spec(2)],
        out_specs=[pl.BlockSpec((length,128),lambda i:(0,i)),pl.BlockSpec((1,2,length),lambda i:(i,0,0))],
        out_shape=[jax.ShapeDtypeStruct((length,width),bf16),jax.ShapeDtypeStruct((pairs,2,length),f32)],
        compiler_params=pltpu.CompilerParams(vmem_limit_bytes=48*2**20),
        cost_estimate=pl.CostEstimate(flops=pairs*2*4*length*length*128,bytes_accessed=length*width*8,transcendentals=pairs*2*length*length),
        name="attn_fwd_"+("causal" if causal else "full"),
    )(lims,qkv,qkv,qkv)

def bwd_kernel(causal,bq,group,lims_ref,q_ref,k_ref,v_ref,l_ref,do_ref,grad_ref,dk_acc,dv_acc):
    length=q_ref.shape[0]
    lane=lax.broadcasted_iota(jnp.int32,(bq,128),1)
    dk_acc[...]=jnp.zeros_like(dk_acc); dv_acc[...]=jnp.zeros_like(dv_acc)
    per=group//128
    pair=pl.program_id(0)
    at=[pl.multiple_of((lax.div(pair,per)*3*per+part*per+lax.rem(pair,per))*128,128) for part in range(3)]
    def block(start,kk):
        q=q_ref[pl.ds(start,bq),:]*jnp.asarray(0.125,bf16)
        do=do_ref[pl.ds(start,bq),:]
        lim=_limits(lims_ref,start,bq,causal,1)
        dqs=[]
        for h in range(2):
            sel=(lane<HEAD_DIM)==(h==0)
            qm=jnp.where(sel,q,jnp.zeros_like(q)); dom=jnp.where(sel,do,jnp.zeros_like(do))
            s=lax.dot_general(k_ref[0:kk,:],qm,NT,preferred_element_type=f32)
            dp=lax.dot_general(v_ref[0:kk,:],dom,NT,preferred_element_type=f32)
            key=lax.broadcasted_iota(jnp.int32,(kk,bq),0)
            lrow=l_ref[0,h:h+1,pl.ds(start,bq)]
            p=jnp.where(key<=lim,jnp.exp(s-lrow),0.0)
            pd=p*dp
            D=jnp.sum(pd,axis=0,keepdims=True)
            ds=(pd-p*D).astype(bf16)
            dv_acc[0:kk,:]+=jnp.dot(p.astype(bf16),dom,preferred_element_type=f32)
            dk_acc[0:kk,:]+=jnp.dot(ds,qm,preferred_element_type=f32)
            dqs.append(lax.dot_general(ds,k_ref[0:kk,:],TN,preferred_element_type=f32))
        grad_ref[pl.ds(start,bq),pl.ds(at[0],128)]=(jnp.where(lane<HEAD_DIM,dqs[0],dqs[1])*0.125).astype(bf16)
    nq=length//bq
    if causal:
        for i in range(nq): block(i*bq,(i+1)*bq)
    else:
        def body(i,c):
            block(pl.multiple_of(i*bq,bq),length); return c
        lax.fori_loop(0,nq,body,0)
    grad_ref[:,pl.ds(at[1],128)]=dk_acc[...].astype(bf16)
    grad_ref[:,pl.ds(at[2],128)]=dv_acc[...].astype(bf16)

def attn_bwd(qkv,L,do,lims,group,causal,bq=256):
    length=qkv.shape[0]; width=qkv.shape[1]//3; pairs=width//128
    per=group//128
    spec=lambda off: pl.BlockSpec((length,128),lambda i,off=off:(0,(i//per)*3*per+off*per+i%per))
    one=pl.BlockSpec((length,128),lambda i:(0,i))
    return pl.pallas_call(partial(bwd_kernel,causal,bq,group),
        grid=(pairs,),
        in_specs=[pl.BlockSpec(memory_space=pltpu.SMEM),spec(0),spec(1),spec(2),pl.BlockSpec((1,2,length),lambda i:(i,0,0)),one],
        out_specs=pl.BlockSpec((length,3*width),lambda i:(0,0)),
        out_shape=jax.ShapeDtypeStruct((length,3*width),bf16),
        scratch_shapes=[pltpu.VMEM((length,128),f32)]*2,
        compiler_params=pltpu.CompilerParams(vmem_limit_bytes=48*2**20),
        cost_estimate=pl.CostEstimate(flops=pairs*2*10*length*length*128,bytes_accessed=length*width*14,transcendentals=pairs*2*length*length),
        name="attn_bwd_"+("causal" if causal else "full"),
    )(lims,qkv,qkv,qkv,L,do)


def pin(*values):
    return lax.optimization_barrier(values)


def swap_tensor(block):
    return lax.ppermute(block, "tensor", [(0, 1), (1, 0)])


def swap_bit(block, bit, dp_size):
    return lax.ppermute(block, "dp", [(place, place ^ (1 << bit)) for place in range(dp_size)])


def in_order(flag, mine, other):
    first = jnp.where(flag == 0, mine, other)
    second = jnp.where(flag == 0, other, mine)
    return jnp.concatenate([first, second], axis=0)


def add_rounded(left, right):
    return (left.astype(f32) + right.astype(f32)).astype(bf16)


def norm_forward(rows, gain_row, shift_row):
    mean = jnp.mean(rows, axis=-1, keepdims=True)
    centered = rows - mean
    rate = lax.rsqrt(jnp.mean(centered * centered, axis=-1, keepdims=True) + norm_eps)
    normed = centered * rate * gain_row + shift_row
    return normed.astype(bf16), (rows, mean, rate)


def norm_backward(saved, grad_normed, gain_row):
    rows, mean, rate = saved
    unit = (rows - mean) * rate
    grad_unit = grad_normed * gain_row
    grad_rows = rate * (
        grad_unit
        - jnp.mean(grad_unit, axis=-1, keepdims=True)
        - unit * jnp.mean(grad_unit * unit, axis=-1, keepdims=True)
    )
    return grad_rows, jnp.sum(grad_normed * unit, axis=0), jnp.sum(grad_normed, axis=0)


def gelu_pair(hidden):
    square = hidden * hidden
    inner = 0.7978845608 * hidden * (1.0 + 0.044715 * square)
    bent = jnp.tanh(inner)
    value = 0.5 * hidden * (1.0 + bent)
    slope = 0.5 * (1.0 + bent) + 0.5 * hidden * (1.0 - bent * bent) * 0.7978845608 * (
        1.0 + 3.0 * 0.044715 * square
    )
    return value.astype(bf16), slope.astype(bf16)


def dot_sum(pairs, dims):
    total = None
    for left, right in pairs:
        term = lax.dot_general(left, right, dims, preferred_element_type=f32)
        total = term if total is None else total + term
    return total


def dot_low(left, right, dims):
    return lax.dot_general(left, right, dims, preferred_element_type=f32).astype(bf16)


NN = (((1,), (0,)), ((), ()))
SPLIT_AXIS = {"qkv": 1, "out": 0, "up": 1, "down": 0}
PACK_WIDTH = 512


def quarter_of(kind, half, place):
    axis = SPLIT_AXIS[kind]
    width = half.shape[axis] // 2
    return lax.dynamic_slice_in_dim(half, place * width, width, axis)


def row_half(block, place):
    height = block.shape[0] // 2
    return lax.dynamic_slice_in_dim(block, place * height, height, 0)


def pack_piece(half, place, dp_size):
    height = half.shape[0] // dp_size
    piece = lax.dynamic_slice_in_dim(half, place * height, height, 0)
    return [
        lax.slice_in_dim(piece, at, at + PACK_WIDTH, axis=1)
        for at in range(0, half.shape[1], PACK_WIDTH)
    ]


def unpack_halves(gathered, shapes):
    dp_size = gathered.shape[0]
    halves, at = [], 0
    for height, width in shapes:
        rows = height // dp_size
        count = width // PACK_WIDTH
        part = lax.slice_in_dim(gathered, at, at + rows * count, axis=1)
        part = part.reshape(dp_size, count, rows, PACK_WIDTH).transpose(0, 2, 1, 3)
        halves.append(part.reshape(height, width))
        at += rows * count
    return halves


def place_kernel(kind, whole_ref, *refs):
    out_ref = refs[-1]
    block = whole_ref[0].astype(f32)
    if kind == "qkv":
        width = block.shape[1] // 3
        for part in range(3):
            out_ref[0, :, part, :] = block[:, part * width : (part + 1) * width]
    else:
        out_ref[0] = block


def place_grad(kind, whole, layer, base):
    dp_size, rows, columns = whole.shape
    bit_count = dp_size.bit_length() - 1

    def source(step):
        group, core = (step // (dp_size // 2), 0)
        block = step % (dp_size // 2)
        index = group
        for bit in range(1, bit_count):
            index = index + ((block >> (bit_count - 1 - bit)) & 1) * (1 << bit)
        return index

    half = dp_size // 2
    if kind in ("out", "down"):
        out_shape = (2, dp_size * rows, columns)
        out_spec = pl.BlockSpec((1, rows, columns), lambda step: (layer, step, 0))
    elif kind == "up":
        out_shape = (2, half * rows, 2 * columns)
        out_spec = pl.BlockSpec((1, rows, columns), lambda step: (layer, step % half, step // half))
    else:
        out_shape = (2, half * rows, 3, 2 * columns // 3)
        out_spec = pl.BlockSpec(
            (1, rows, 3, columns // 3), lambda step: (layer, step % half, 0, step // half)
        )
    operands, in_specs, aliases = [whole], [pl.BlockSpec((1, rows, columns), lambda step: (source(step), 0, 0))], {}
    if base is not None:
        operands.append(base)
        in_specs.append(pl.BlockSpec(memory_space=pl.ANY))
        aliases = {1: 0}
    return pl.pallas_call(
        partial(place_kernel, kind),
        grid=(dp_size,),
        in_specs=in_specs,
        out_specs=out_spec,
        out_shape=jax.ShapeDtypeStruct(out_shape, f32),
        input_output_aliases=aliases,
        cost_estimate=pl.CostEstimate(flops=0, bytes_accessed=6 * dp_size * rows * columns, transcendentals=0),
        name="place_" + kind,
    )(*operands)


def frame_kernel(side_ref, mine_ref, other_ref, out_ref):
    own = pl.program_id(0) == side_ref[0]
    out_ref[0, 0] = jnp.where(own, mine_ref[...], other_ref[...].astype(f32))


def place_frames(side, mine, other):
    height, width = mine.shape
    rows = height // 2
    spec = pl.BlockSpec((rows, width), lambda slot, step, side_ref: (step, 0))
    return pl.pallas_call(
        frame_kernel,
        grid_spec=pltpu.PrefetchScalarGridSpec(
            num_scalar_prefetch=1,
            grid=(2, 2),
            in_specs=[spec, spec],
            out_specs=pl.BlockSpec((1, 1, rows, width), lambda slot, step, side_ref: (slot, 0, step, 0)),
        ),
        out_shape=jax.ShapeDtypeStruct((2, 1, height, width), f32),
        name="place_frames",
    )(side.reshape(1).astype(jnp.int32), mine, other)


class Chain:
    def __init__(self, kind, layer, own, near, far, place, dp_size):
        self.kind, self.layer, self.place, self.dp_size = kind, layer, place, dp_size
        self.bit_count = dp_size.bit_length() - 1
        core = place & 1
        self.near = near
        self.kept = quarter_of(kind, own, core)
        self.flight = [
            swap_bit(far, 0, dp_size),
            swap_bit(quarter_of(kind, own, 1 - core), 0, dp_size),
        ]
        self.stage = "core"

    def bit(self, index):
        return (self.place >> index) & 1

    def advance(self, arrived):
        if self.stage == "core":
            near_there, own_there = arrived
            self.kept = self.kept.astype(f32) + own_there.astype(f32)
            self.flight = [swap_tensor(add_rounded(self.near, near_there))]
            self.near = None
            self.stage = 0
            return
        total = (self.kept.astype(f32) + arrived[0].astype(f32)).astype(bf16)
        self.stage += 1
        if self.stage < self.bit_count:
            bit = self.bit(self.stage)
            self.kept = row_half(total, bit)
            self.flight = [swap_bit(row_half(total, 1 - bit), self.stage, self.dp_size)]
        else:
            self.flight = []
            self.whole = lax.all_gather(total, "dp", axis=0, tiled=False)


def move(state, *chains):
    state, flights = pin(state, [chain.flight for chain in chains])
    for chain, flight in zip(chains, flights):
        chain.advance(flight)
    return state


def paired_device(
    dp_size,
    frames_in,
    phone_len,
    frame_len,
    section,
    norm_gain,
    norm_bias,
    ada_scale,
    ada_shift,
    w_qkv,
    w_out,
    w_up,
    w_down,
    out_grad,
):
    model_width = frames_in.shape[3]
    section_count = ada_scale.shape[1]
    side = lax.axis_index("tensor")
    place = lax.axis_index("dp")
    bit_count = dp_size.bit_length() - 1
    core, near_row = place & 1, (place >> 1) & 1
    group = w_qkv.shape[3] // 2

    def away_rows(halves):
        return lax.dynamic_index_in_dim(halves[:, 0], 1 - side, 0, keepdims=False)

    def whole_rows(halves, other):
        mine = lax.dynamic_index_in_dim(halves[:, 0], side, 0, keepdims=False)
        return in_order(side, mine, other)

    prefix = lax.dynamic_index_in_dim(phone_len[:, 0], side, 0, keepdims=False)
    frames = lax.dynamic_index_in_dim(frame_len[:, 0], side, 0, keepdims=False)
    chosen = lax.dynamic_index_in_dim(section[:, 0], side, 0, keepdims=False)
    limits = jnp.stack([prefix, prefix + frames]).astype(jnp.int32)
    picker = (lax.iota(jnp.int32, section_count) == chosen).astype(f32)[:, None]

    gains = [
        [norm_gain[0], norm_gain[1]],
        [jnp.sum(picker * ada_scale[part], axis=0) for part in range(2)],
    ]
    shifts = [
        [norm_bias[0], norm_bias[1]],
        [jnp.sum(picker * ada_shift[part], axis=0) for part in range(2)],
    ]

    def flat_qkv(layer):
        split = w_qkv[layer].reshape(model_width, 3, 2, group).transpose(0, 2, 1, 3)
        return split.reshape(model_width, 6 * group)

    own = [
        {"qkv": flat_qkv(layer), "out": w_out[layer], "up": w_up[layer], "down": w_down[layer]}
        for layer in range(2)
    ]

    def packed(layer, kinds):
        pieces = []
        for kind in kinds:
            pieces += pack_piece(own[layer][kind], place, dp_size)
        return jnp.concatenate(pieces, axis=0)

    def gathered(arrived, layer, kinds):
        whole = lax.all_gather(arrived, "dp", axis=0, tiled=False)
        return dict(zip(kinds, unpack_halves(whole, [own[layer][kind].shape for kind in kinds])))

    attn_kinds, all_kinds = ("qkv", "out"), ("qkv", "out", "up", "down")
    first_pack = swap_tensor(packed(0, attn_kinds))
    other_rows = swap_tensor(away_rows(frames_in))
    first = gathered(first_pack, 0, attn_kinds)
    second_send = packed(1, all_kinds)
    up_send = row_half(quarter_of("up", own[0]["up"], core), near_row)
    down_send = row_half(quarter_of("down", own[0]["down"], core), near_row)
    other_rows, second_send, up_send, down_send = pin(other_rows, second_send, up_send, down_send)
    second_pack = swap_tensor(second_send)
    rows = whole_rows(frames_in, other_rows).astype(f32)
    normed, norm_kept = norm_forward(rows, gains[0][0], shifts[0][0])
    mine = dot_low(normed, own[0]["qkv"], NN)
    mine, second_pack, up_send, down_send = pin(mine, second_pack, up_send, down_send)
    second = gathered(second_pack, 1, all_kinds)
    up_piece = swap_tensor(up_send)
    mix_mine = attn_fwd(mine, limits, group, True, 512)
    mix_mine, up_piece, down_send = pin(mix_mine, up_piece, down_send)
    down_piece = swap_tensor(down_send)
    up_there = swap_bit(up_piece, 1, dp_size)
    theirs = dot_low(normed, first["qkv"], NN)
    mix_theirs = attn_fwd(theirs, limits, group, True, 512)
    mix_theirs, up_there, down_piece = pin(mix_theirs, up_there, down_piece)
    up_near = in_order(near_row, up_piece, up_there)
    up_far = swap_bit(up_near, 0, dp_size)
    down_there = swap_bit(down_piece, 1, dp_size)
    kept = [(normed, norm_kept, [mine, theirs], [mix_mine, mix_theirs])]
    rows = rows + dot_sum([(mix_mine[0], own[0]["out"]), (mix_theirs[0], first["out"])], NN)
    normed, norm_kept = norm_forward(rows, gains[0][1], shifts[0][1])
    pair_own = gelu_pair(jnp.dot(normed, own[0]["up"], preferred_element_type=f32))
    pair_own, up_far, normed = pin(pair_own, up_far, normed)
    pair_near = gelu_pair(jnp.dot(normed, up_near, preferred_element_type=f32))
    pair_far = gelu_pair(jnp.dot(normed, up_far, preferred_element_type=f32))
    rows = rows + dot_sum([(pair_own[0], own[0]["down"])], NN)
    rows, pair_near, pair_far, down_there = pin(rows, pair_near, pair_far, down_there)
    down_near = in_order(near_row, down_piece, down_there)
    down_far = swap_bit(down_near, 0, dp_size)
    grad_send = away_rows(out_grad)
    down_near, grad_send = pin(down_near, grad_send)
    grad_other = swap_tensor(grad_send)
    rows = rows + dot_sum([(pair_near[0], down_near), (pair_far[0], down_far)], NN)
    kept.append((normed, norm_kept, [pair_own, pair_near, pair_far]))
    weights = [
        {
            "qkv": [own[0]["qkv"], first["qkv"]],
            "out": [own[0]["out"], first["out"]],
            "up": [own[0]["up"], up_near, up_far],
            "down": [own[0]["down"], down_near, down_far],
        },
        {kind: [own[1][kind], second[kind]] for kind in all_kinds},
    ]

    normed, norm_kept = norm_forward(rows, gains[1][0], shifts[1][0])
    projected = [dot_low(normed, part, NN) for part in weights[1]["qkv"]]
    mixed = [attn_fwd(part, limits, group, False, 512) for part in projected]
    rows = rows + dot_sum([(mix[0], part) for mix, part in zip(mixed, weights[1]["out"])], NN)
    kept.append((normed, norm_kept, projected, mixed))
    normed, norm_kept = norm_forward(rows, gains[1][1], shifts[1][1])
    pairs = [gelu_pair(jnp.dot(normed, part, preferred_element_type=f32)) for part in weights[1]["up"]]
    rows = rows + dot_sum([(pair[0], part) for pair, part in zip(pairs, weights[1]["down"])], NN)
    kept.append((normed, norm_kept, pairs))
    rows, grad_other = pin(rows, grad_other)

    def halves_of(block):
        height = block.shape[0] // 2
        mine = lax.dynamic_slice_in_dim(block, side * height, height, 0)
        away = lax.dynamic_slice_in_dim(block, (1 - side) * height, height, 0)
        return mine, away.astype(bf16)

    out_mine, out_away = halves_of(rows)

    norm_sums = [[None, None], [None, None]]
    grad_rows = whole_rows(out_grad, grad_other).astype(f32)

    def chain(kind, layer, parts):
        if len(parts) == 2:
            near, far = (quarter_of(kind, parts[1], core), quarter_of(kind, parts[1], 1 - core))
        else:
            near, far = parts[1:]
        return Chain(kind, layer, parts[0], near, far, place, dp_size)

    def hidden_grads(layer, low):
        pairs = kept[2 * layer + 1][2]
        return [
            (
                lax.dot_general(low, part, NT, preferred_element_type=f32) * pair[1].astype(f32)
            ).astype(bf16)
            for pair, part in zip(pairs, weights[layer]["down"])
        ]

    def down_grads(layer, low):
        return [dot_low(pair[0], low, TN) for pair in kept[2 * layer + 1][2]]

    def up_grads(layer, hidden):
        return [dot_low(kept[2 * layer + 1][0], part, TN) for part in hidden]

    def out_grads(layer, low):
        return [dot_low(mix[0], low, TN) for mix in kept[2 * layer][3]]

    def mixed_grads(layer, low):
        return [dot_low(low, part, NT) for part in weights[layer]["out"]]

    def attention_grad(layer, part, grad_mix):
        _, _, projected, mixed = kept[2 * layer]
        return attn_bwd(projected[part], mixed[part][1], grad_mix, limits, group, layer == 0, 512)

    def norm_step(layer, part, grad_rows, grad_normed):
        added, grad_gain, grad_shift = norm_backward(
            kept[2 * layer + part][1], grad_normed, gains[layer][part]
        )
        norm_sums[layer][part] = (grad_gain, grad_shift)
        return grad_rows + added

    low = grad_rows.astype(bf16)
    parts = down_grads(1, low)
    hidden = hidden_grads(1, low)
    parts, hidden, grad_rows = pin(parts, hidden, grad_rows)
    down1 = chain("down", 1, parts)
    parts = up_grads(1, hidden)
    grad_normed = dot_sum(list(zip(hidden, weights[1]["up"])), NT)
    parts, grad_normed = move((parts, grad_normed), down1)
    up1 = chain("up", 1, parts)
    grad_rows = norm_step(1, 1, grad_rows, grad_normed)
    low = grad_rows.astype(bf16)
    parts = out_grads(1, low)
    mine, theirs = mixed_grads(1, low)
    theirs = attention_grad(1, 1, theirs)
    parts, mine, theirs, grad_rows = move((parts, mine, theirs, grad_rows), down1, up1)
    out1 = chain("out", 1, parts)
    mine = attention_grad(1, 0, mine)
    mine, theirs = move((mine, theirs), down1, out1)
    parts = [dot_low(kept[2][0], part, TN) for part in (mine, theirs)]
    grad_normed = dot_sum(list(zip((mine, theirs), weights[1]["qkv"])), NT)
    parts, grad_normed = move((parts, grad_normed), down1, up1)
    qkv1 = chain("qkv", 1, parts)
    grad_rows = norm_step(1, 0, grad_rows, grad_normed)
    low = grad_rows.astype(bf16)
    parts = down_grads(0, low)
    parts, low, grad_rows = move((parts, low, grad_rows), down1, out1, qkv1)
    down0 = chain("down", 0, parts)
    hidden = hidden_grads(0, low)
    (hidden,) = move((hidden,), up1, out1, down0)
    parts = up_grads(0, hidden)
    grad_normed = dot_sum(list(zip(hidden, weights[0]["up"])), NT)
    parts, grad_normed = move((parts, grad_normed), up1, out1, qkv1)
    up0 = chain("up", 0, parts)
    grad_rows = norm_step(0, 1, grad_rows, grad_normed)
    low = grad_rows.astype(bf16)
    out_parts = out_grads(0, low)
    mine, theirs = mixed_grads(0, low)
    theirs = attention_grad(0, 1, theirs)
    out_parts, mine, theirs, grad_rows = move(
        (out_parts, mine, theirs, grad_rows), up1, out1, qkv1, down0, up0
    )
    out0 = chain("out", 0, out_parts)
    part_theirs = dot_low(kept[0][0], theirs, TN)
    mine = attention_grad(0, 0, mine)
    mine, theirs, part_theirs = move((mine, theirs, part_theirs), qkv1, down0, out0)
    part_mine = dot_low(kept[0][0], mine, TN)
    grad_normed = dot_sum([(mine, weights[0]["qkv"][0]), (theirs, weights[0]["qkv"][1])], NT)
    part_mine, grad_normed = move((part_mine, grad_normed), up0, qkv1)
    qkv0 = chain("qkv", 0, [part_mine, part_theirs])
    grad_rows = norm_step(0, 0, grad_rows, grad_normed)
    grad_mine, grad_away = halves_of(grad_rows)
    (grad_mine, grad_away) = move((grad_mine, grad_away), qkv0, out0, down0)
    frames_grad = place_frames(side, grad_mine, swap_tensor(grad_away))
    move((), up0, out0, down0)
    frames_out = place_frames(side, out_mine, swap_tensor(out_away))
    for one in (up0, out0, down0, qkv0):
        while one.flight:
            one.advance(one.flight)

    def everywhere(block):
        block = block + swap_tensor(block)
        for bit in range(bit_count):
            block = block + swap_bit(block, bit, dp_size)
        return block

    late = everywhere(
        jnp.stack(
            [
                norm_sums[0][0][0],
                norm_sums[0][1][0],
                norm_sums[0][0][1],
                norm_sums[0][1][1],
            ]
        )
    )
    early = everywhere(
        jnp.concatenate(
            [
                picker * norm_sums[1][0][0][None],
                picker * norm_sums[1][1][0][None],
                picker * norm_sums[1][0][1][None],
                picker * norm_sums[1][1][1][None],
            ]
        )
    ).reshape(4, section_count, model_width)

    def both(kind, later, sooner):
        return place_grad(kind, sooner.whole, 0, place_grad(kind, later.whole, 1, None))

    return (
        frames_out,
        frames_grad,
        both("qkv", qkv1, qkv0),
        both("out", out1, out0),
        both("up", up1, up0),
        both("down", down1, down0),
        late[0:2],
        late[2:4],
        early[0:2],
        early[2:4],
    )


def per_device(dp_size, tensor_size, *arrays):
    micro_count, local_seqs = arrays[0].shape[:2]
    paired = micro_count == 2 and tensor_size == 2 and local_seqs == 1
    if paired and dp_size >= 4 and dp_size & (dp_size - 1) == 0:
        return paired_device(dp_size, *arrays)
    return grouped_device(*arrays)


def solution(mesh):
    return jax.shard_map(
        partial(per_device, mesh.shape["dp"], mesh.shape["tensor"]),
        mesh=mesh,
        in_specs=(
            P(None, "dp", "tensor", None),
            P(None, "dp"),
            P(None, "dp"),
            P(None, "dp"),
            P(),
            P(),
            P(),
            P(),
            P(None, None, None, "tensor"),
            P(None, "tensor", None),
            P(None, None, "tensor"),
            P(None, "tensor", None),
            P(None, "dp", "tensor", None),
        ),
        out_specs=(
            P(None, "dp", "tensor", None),
            P(None, "dp", "tensor", None),
            P(None, None, None, "tensor"),
            P(None, "tensor", None),
            P(None, None, "tensor"),
            P(None, "tensor", None),
            P(),
            P(),
            P(),
            P(),
        ),
        check_vma=False,
    )
```

```python
from functools import partial

import jax
import jax.numpy as jnp
from jax import lax
from jax.experimental import pallas as pl
from jax.experimental.pallas import tpu as pltpu
from jax.sharding import PartitionSpec as P

HEAD_DIM = 64


norm_eps = 1e-05
masked_score = -1000000000.0
contract_rows = (((0,), (0,)), ((), ()))
contract_cols = (((1,), (1,)), ((), ()))


def plain_norm(inputs):
    centered = inputs - jnp.mean(inputs, axis=-1, keepdims=True)
    variance = jnp.mean(centered * centered, axis=-1, keepdims=True)
    return centered * lax.rsqrt(variance + norm_eps)


def fixed_norm(inputs, gain_row, shift_row):
    return plain_norm(inputs) * gain_row + shift_row


def section_norm(inputs, scale_table, shift_table, picker):
    scale_row = jnp.dot(
        picker, scale_table, precision=lax.Precision.HIGHEST, preferred_element_type=jnp.float32
    )
    shift_row = jnp.dot(
        picker, shift_table, precision=lax.Precision.HIGHEST, preferred_element_type=jnp.float32
    )
    return plain_norm(inputs) * scale_row + shift_row


def gather_normed(normed_low):
    return lax.all_gather(normed_low, "tensor", axis=0, tiled=True)


def gather_again(normed_low):
    return lax.all_gather(normed_low, "tensor", axis=0, tiled=True)


def sum_branch(branch_part):
    return lax.psum_scatter(
        branch_part.astype(jnp.bfloat16), "tensor", scatter_dimension=0, tiled=True
    ).astype(jnp.float32)


def gather_grad(grad_low):
    return lax.all_gather(grad_low, "tensor", axis=0, tiled=True)


def sum_normed(grad_part):
    return lax.psum_scatter(
        grad_part.astype(jnp.bfloat16), "tensor", scatter_dimension=0, tiled=True
    ).astype(jnp.float32)


def key_allowed(query_pos, key_pos, prefix, valid_count, causal):
    allowed = key_pos[None, :] < valid_count
    if causal:
        allowed = allowed & ((key_pos[None, :] < prefix) | (key_pos[None, :] <= query_pos[:, None]))
    return allowed


def split_heads(projected):
    length = projected.shape[0]
    head_width = projected.shape[1] // 3
    head_count = head_width // HEAD_DIM
    query_rows = projected[:, :head_width].reshape(length, head_count, HEAD_DIM)
    key_rows = projected[:, head_width : 2 * head_width].reshape(length, head_count, HEAD_DIM)
    value_rows = projected[:, 2 * head_width :].reshape(length, head_count, HEAD_DIM)
    return (query_rows, key_rows, value_rows)


def block_scores(query_block, key_rows, block_start, prefix, valid_count, causal):
    block_rows = query_block.shape[0]
    length = key_rows.shape[0]
    scores = jnp.einsum(
        "qhd,khd->hqk", query_block, key_rows, preferred_element_type=jnp.float32
    ) * HEAD_DIM ** (-0.5)
    query_pos = block_start + lax.iota(jnp.int32, block_rows)
    key_pos = lax.iota(jnp.int32, length)
    allowed = key_allowed(query_pos, key_pos, prefix, valid_count, causal)
    return jnp.where(allowed[None], scores, masked_score)


def attend_forward(projected, prefix, valid_count, causal, block_rows):
    length = projected.shape[0]
    head_width = projected.shape[1] // 3
    query_rows, key_rows, value_rows = split_heads(projected)

    def one_block(block_start):
        query_block = lax.dynamic_slice_in_dim(query_rows, block_start, block_rows, 0)
        scores = block_scores(query_block, key_rows, block_start, prefix, valid_count, causal)
        highest = jnp.max(scores, axis=-1, keepdims=True)
        row_total = jnp.sum(jnp.exp(scores - highest), axis=-1, keepdims=True)
        log_total = highest + jnp.log(row_total)
        shares = jnp.exp(scores - log_total).astype(jnp.bfloat16)
        mixture = jnp.einsum("hqk,khd->qhd", shares, value_rows, preferred_element_type=jnp.float32)
        return (mixture.astype(jnp.bfloat16), log_total)

    starts = lax.iota(jnp.int32, length // block_rows) * block_rows
    mixture, log_totals = lax.map(one_block, starts)
    return (mixture.reshape(length, head_width), log_totals)


def attend_backward(projected, log_totals, grad_mixture, prefix, valid_count, causal, block_rows):
    length = projected.shape[0]
    head_width = projected.shape[1] // 3
    query_rows, key_rows, value_rows = split_heads(projected)
    grad_rows = grad_mixture.reshape(query_rows.shape)
    score_scale = HEAD_DIM ** (-0.5)

    def one_block(grad_state, block_item):
        block_start, log_total = block_item
        grad_key, grad_value = grad_state
        query_block = lax.dynamic_slice_in_dim(query_rows, block_start, block_rows, 0)
        grad_block = lax.dynamic_slice_in_dim(grad_rows, block_start, block_rows, 0)
        scores = block_scores(query_block, key_rows, block_start, prefix, valid_count, causal)
        shares = jnp.exp(scores - log_total)
        shares_low = shares.astype(jnp.bfloat16)
        grad_shares = jnp.einsum(
            "qhd,khd->hqk", grad_block, value_rows, preferred_element_type=jnp.float32
        )
        inner_sum = jnp.sum(shares * grad_shares, axis=-1, keepdims=True)
        grad_scores = (shares * (grad_shares - inner_sum)).astype(jnp.bfloat16)
        grad_query = (
            jnp.einsum("hqk,khd->qhd", grad_scores, key_rows, preferred_element_type=jnp.float32)
            * score_scale
        )
        grad_key = (
            grad_key
            + jnp.einsum(
                "hqk,qhd->khd", grad_scores, query_block, preferred_element_type=jnp.float32
            )
            * score_scale
        )
        grad_value = grad_value + jnp.einsum(
            "hqk,qhd->khd", shares_low, grad_block, preferred_element_type=jnp.float32
        )
        return ((grad_key, grad_value), grad_query)

    starts = lax.iota(jnp.int32, length // block_rows) * block_rows
    zero_rows = jnp.zeros(query_rows.shape, jnp.float32)
    grad_state, grad_query = lax.scan(one_block, (zero_rows, zero_rows), (starts, log_totals))
    grad_key, grad_value = grad_state
    joined = jnp.concatenate(
        [
            grad_query.reshape(length, head_width),
            grad_key.reshape(length, head_width),
            grad_value.reshape(length, head_width),
        ],
        axis=1,
    )
    return joined.astype(jnp.bfloat16)


def grouped_device(
    frames_in,
    phone_len,
    frame_len,
    section,
    norm_gain,
    norm_bias,
    ada_scale,
    ada_shift,
    w_qkv,
    w_out,
    w_up,
    w_down,
    out_grad,
):
    micro_count, local_seqs, local_rows, model_width = frames_in.shape
    seq_length = local_rows * lax.axis_size("tensor")
    block_rows = min(512, seq_length)
    section_count = ada_scale.shape[1]
    qkv_mats = [w_qkv[layer_index].reshape(model_width, -1) for layer_index in range(2)]
    acc_qkv = [jnp.zeros(qkv_mats[layer_index].shape, jnp.float32) for layer_index in range(2)]
    acc_out = [jnp.zeros(w_out.shape[1:], jnp.float32) for layer_index in range(2)]
    acc_up = [jnp.zeros(w_up.shape[1:], jnp.float32) for layer_index in range(2)]
    acc_down = [jnp.zeros(w_down.shape[1:], jnp.float32) for layer_index in range(2)]
    acc_gain = [jnp.zeros((model_width,), jnp.float32) for part_index in range(2)]
    acc_bias = [jnp.zeros((model_width,), jnp.float32) for part_index in range(2)]
    acc_scale = [jnp.zeros((section_count, model_width), jnp.float32) for part_index in range(2)]
    acc_shift = [jnp.zeros((section_count, model_width), jnp.float32) for part_index in range(2)]
    frames_list = []
    grads_list = []
    for micro_index in range(micro_count):
        prefix = phone_len[micro_index, 0]
        valid_count = prefix + frame_len[micro_index, 0]
        picker = (lax.iota(jnp.int32, section_count) == section[micro_index, 0]).astype(
            jnp.float32
        )[None, :]
        residual = frames_in[micro_index, 0].astype(jnp.float32)
        stored = []
        for layer_index in range(2):
            for part_index in range(2):
                if layer_index == 0:
                    normed, norm_back = jax.vjp(
                        fixed_norm, residual, norm_gain[part_index], norm_bias[part_index]
                    )
                else:
                    normed, norm_back = jax.vjp(
                        partial(section_norm, picker=picker),
                        residual,
                        ada_scale[part_index],
                        ada_shift[part_index],
                    )
                normed_low = normed.astype(jnp.bfloat16)
                gathered = gather_normed(normed_low)
                if part_index == 0:
                    projected = jnp.dot(
                        gathered, qkv_mats[layer_index], preferred_element_type=jnp.float32
                    ).astype(jnp.bfloat16)
                    mixture, log_totals = attend_forward(
                        projected, prefix, valid_count, layer_index == 0, block_rows
                    )
                    branch = sum_branch(
                        jnp.dot(mixture, w_out[layer_index], preferred_element_type=jnp.float32)
                    )
                    saved_state = (projected, log_totals, mixture)
                else:
                    hidden = jnp.dot(
                        gathered, w_up[layer_index], preferred_element_type=jnp.float32
                    )
                    active = jax.nn.gelu(hidden, approximate=True).astype(jnp.bfloat16)
                    branch = sum_branch(
                        jnp.dot(active, w_down[layer_index], preferred_element_type=jnp.float32)
                    )
                    saved_state = (hidden, active)
                kept_rows = normed_low
                stored.append((norm_back, kept_rows, saved_state))
                residual = residual + branch
        out_group = [residual]
        grad_rows = out_grad[micro_index, 0].astype(jnp.float32)
        for layer_index in (1, 0):
            for part_index in (1, 0):
                norm_back, kept_rows, saved_state = stored[2 * layer_index + part_index]
                gathered = gather_again(kept_rows)
                grad_whole = gather_grad(grad_rows.astype(jnp.bfloat16))
                if part_index == 1:
                    hidden, active = saved_state
                    acc_down[layer_index] = acc_down[layer_index] + lax.dot_general(
                        active, grad_whole, contract_rows, preferred_element_type=jnp.float32
                    )
                    grad_active = lax.dot_general(
                        grad_whole,
                        w_down[layer_index],
                        contract_cols,
                        preferred_element_type=jnp.float32,
                    )
                    gelu_value, gelu_back = jax.vjp(partial(jax.nn.gelu, approximate=True), hidden)
                    grad_hidden = gelu_back(grad_active)[0].astype(jnp.bfloat16)
                    acc_up[layer_index] = acc_up[layer_index] + lax.dot_general(
                        gathered, grad_hidden, contract_rows, preferred_element_type=jnp.float32
                    )
                    grad_normed = sum_normed(
                        lax.dot_general(
                            grad_hidden,
                            w_up[layer_index],
                            contract_cols,
                            preferred_element_type=jnp.float32,
                        )
                    )
                else:
                    projected, log_totals, mixture = saved_state
                    acc_out[layer_index] = acc_out[layer_index] + lax.dot_general(
                        mixture, grad_whole, contract_rows, preferred_element_type=jnp.float32
                    )
                    grad_mixture = lax.dot_general(
                        grad_whole,
                        w_out[layer_index],
                        contract_cols,
                        preferred_element_type=jnp.float32,
                    ).astype(jnp.bfloat16)
                    grad_projected = attend_backward(
                        projected,
                        log_totals,
                        grad_mixture,
                        prefix,
                        valid_count,
                        layer_index == 0,
                        block_rows,
                    )
                    acc_qkv[layer_index] = acc_qkv[layer_index] + lax.dot_general(
                        gathered, grad_projected, contract_rows, preferred_element_type=jnp.float32
                    )
                    grad_normed = sum_normed(
                        lax.dot_general(
                            grad_projected,
                            qkv_mats[layer_index],
                            contract_cols,
                            preferred_element_type=jnp.float32,
                        )
                    )
                grad_input, grad_first, grad_second = norm_back(grad_normed)
                grad_rows = grad_rows + grad_input
                if layer_index == 0:
                    acc_gain[part_index] = acc_gain[part_index] + grad_first
                    acc_bias[part_index] = acc_bias[part_index] + grad_second
                else:
                    acc_scale[part_index] = acc_scale[part_index] + grad_first
                    acc_shift[part_index] = acc_shift[part_index] + grad_second
        grad_group = [grad_rows]
        frames_list.append(jnp.stack(out_group))
        grads_list.append(jnp.stack(grad_group))
    total_qkv, total_out, total_up, total_down = (
        lax.psum(jnp.stack(acc_qkv).astype(jnp.bfloat16), "dp").astype(jnp.float32),
        lax.psum(jnp.stack(acc_out).astype(jnp.bfloat16), "dp").astype(jnp.float32),
        lax.psum(jnp.stack(acc_up).astype(jnp.bfloat16), "dp").astype(jnp.float32),
        lax.psum(jnp.stack(acc_down).astype(jnp.bfloat16), "dp").astype(jnp.float32),
    )
    norm_totals = lax.psum(
        (jnp.stack(acc_gain), jnp.stack(acc_bias), jnp.stack(acc_scale), jnp.stack(acc_shift)),
        ("dp", "tensor"),
    )
    return (
        jnp.stack(frames_list),
        jnp.stack(grads_list),
        total_qkv.reshape(2, model_width, 3, -1),
        total_out,
        total_up,
        total_down,
        norm_totals[0],
        norm_totals[1],
        norm_totals[2],
        norm_totals[3],
    )


bf16,f32=jnp.bfloat16,jnp.float32
NT=(((1,),(1,)),((),()))
TN=(((0,),(0,)),((),()))

def _limits(lims_ref, start, rows, causal, axis):
    prefix, valid = lims_ref[0], lims_ref[1]
    shape=(rows,1) if axis==0 else (1,rows)
    pos=start+lax.broadcasted_iota(jnp.int32,shape,axis)
    if causal:
        return jnp.minimum(jnp.maximum(pos,prefix-1),valid-1)
    return jnp.zeros(shape,jnp.int32)+(valid-1)

def fwd_kernel(causal, bq, lims_ref, q_ref, k_ref, v_ref, o_ref, l_ref):
    length=q_ref.shape[0]
    lane=lax.broadcasted_iota(jnp.int32,(bq,128),1)
    def block(start, kk):
        q=q_ref[pl.ds(start,bq),:]*jnp.asarray(0.125,bf16)
        lim=_limits(lims_ref,start,bq,causal,0)
        outs=[];rows=[]
        for h in range(2):
            qm=jnp.where((lane<HEAD_DIM)==(h==0),q,jnp.zeros_like(q))
            s=lax.dot_general(qm,k_ref[0:kk,:],NT,preferred_element_type=f32)
            key=lax.broadcasted_iota(jnp.int32,(bq,kk),1)
            s=jnp.where(key<=lim,s,-1e9)
            m=jnp.max(s,axis=1,keepdims=True)
            e=jnp.exp(s-m)
            l=jnp.sum(e,axis=1,keepdims=True)
            o=jnp.dot(e.astype(bf16),v_ref[0:kk,:],preferred_element_type=f32)*(1.0/l)
            outs.append(o); rows.append(m+jnp.log(l))
        o_ref[pl.ds(start,bq),:]=jnp.where(lane<HEAD_DIM,outs[0],outs[1]).astype(bf16)
        both=jnp.where(lane<HEAD_DIM,rows[0],rows[1])
        bt=both.T
        l_ref[0,0:1,pl.ds(start,bq)]=bt[0:1,:]
        l_ref[0,1:2,pl.ds(start,bq)]=bt[HEAD_DIM:HEAD_DIM+1,:]
    nq=length//bq
    if causal:
        for i in range(nq): block(i*bq,(i+1)*bq)
    else:
        def body(i,c):
            block(pl.multiple_of(i*bq,bq),length); return c
        lax.fori_loop(0,nq,body,0)

def attn_fwd(qkv, lims, causal, bq=256):
    length=qkv.shape[0]; width=qkv.shape[1]//3; pairs=width//128
    spec=lambda off: pl.BlockSpec((length,128),lambda i,off=off:(0,off*pairs+i))
    return pl.pallas_call(partial(fwd_kernel,causal,bq),
        grid=(pairs,),
        in_specs=[pl.BlockSpec(memory_space=pltpu.SMEM),spec(0),spec(1),spec(2)],
        out_specs=[pl.BlockSpec((length,128),lambda i:(0,i)),pl.BlockSpec((1,2,length),lambda i:(i,0,0))],
        out_shape=[jax.ShapeDtypeStruct((length,width),bf16),jax.ShapeDtypeStruct((pairs,2,length),f32)],
        compiler_params=pltpu.CompilerParams(vmem_limit_bytes=48*2**20),
        cost_estimate=pl.CostEstimate(flops=pairs*2**20,bytes_accessed=length*width*8,transcendentals=0),
        name="attn_fwd_"+("causal" if causal else "full"),
    )(lims,qkv,qkv,qkv)

def bwd_kernel(causal,bq,lims_ref,q_ref,k_ref,v_ref,l_ref,do_ref,grad_ref,dk_acc,dv_acc):
    length=q_ref.shape[0]
    lane=lax.broadcasted_iota(jnp.int32,(bq,128),1)
    dk_acc[...]=jnp.zeros_like(dk_acc); dv_acc[...]=jnp.zeros_like(dv_acc)
    width=grad_ref.shape[1]//3
    at=[pl.multiple_of(part*width+pl.program_id(0)*128,128) for part in range(3)]
    def block(start,kk):
        q=q_ref[pl.ds(start,bq),:]*jnp.asarray(0.125,bf16)
        do=do_ref[pl.ds(start,bq),:]
        lim=_limits(lims_ref,start,bq,causal,1)
        dqs=[]
        for h in range(2):
            sel=(lane<HEAD_DIM)==(h==0)
            qm=jnp.where(sel,q,jnp.zeros_like(q)); dom=jnp.where(sel,do,jnp.zeros_like(do))
            s=lax.dot_general(k_ref[0:kk,:],qm,NT,preferred_element_type=f32)
            dp=lax.dot_general(v_ref[0:kk,:],dom,NT,preferred_element_type=f32)
            key=lax.broadcasted_iota(jnp.int32,(kk,bq),0)
            lrow=l_ref[0,h:h+1,pl.ds(start,bq)]
            p=jnp.where(key<=lim,jnp.exp(s-lrow),0.0)
            pd=p*dp
            D=jnp.sum(pd,axis=0,keepdims=True)
            ds=(pd-p*D).astype(bf16)
            dv_acc[0:kk,:]+=jnp.dot(p.astype(bf16),dom,preferred_element_type=f32)
            dk_acc[0:kk,:]+=jnp.dot(ds,qm,preferred_element_type=f32)
            dqs.append(lax.dot_general(ds,k_ref[0:kk,:],TN,preferred_element_type=f32))
        grad_ref[pl.ds(start,bq),pl.ds(at[0],128)]=(jnp.where(lane<HEAD_DIM,dqs[0],dqs[1])*0.125).astype(bf16)
    nq=length//bq
    if causal:
        for i in range(nq): block(i*bq,(i+1)*bq)
    else:
        def body(i,c):
            block(pl.multiple_of(i*bq,bq),length); return c
        lax.fori_loop(0,nq,body,0)
    grad_ref[:,pl.ds(at[1],128)]=dk_acc[...].astype(bf16)
    grad_ref[:,pl.ds(at[2],128)]=dv_acc[...].astype(bf16)

def attn_bwd(qkv,L,do,lims,causal,bq=256):
    length=qkv.shape[0]; width=qkv.shape[1]//3; pairs=width//128
    spec=lambda off: pl.BlockSpec((length,128),lambda i,off=off:(0,off*pairs+i))
    one=pl.BlockSpec((length,128),lambda i:(0,i))
    return pl.pallas_call(partial(bwd_kernel,causal,bq),
        grid=(pairs,),
        in_specs=[pl.BlockSpec(memory_space=pltpu.SMEM),spec(0),spec(1),spec(2),pl.BlockSpec((1,2,length),lambda i:(i,0,0)),one],
        out_specs=pl.BlockSpec((length,3*width),lambda i:(0,0)),
        out_shape=jax.ShapeDtypeStruct((length,3*width),bf16),
        scratch_shapes=[pltpu.VMEM((length,128),f32)]*2,
        compiler_params=pltpu.CompilerParams(vmem_limit_bytes=48*2**20),
        cost_estimate=pl.CostEstimate(flops=pairs*2**20,bytes_accessed=length*width*8,transcendentals=0),
        name="attn_bwd_"+("causal" if causal else "full"),
    )(lims,qkv,qkv,qkv,L,do)


def pin(*values):
    return lax.optimization_barrier(values)


def swap_tensor(block):
    return lax.ppermute(block, "tensor", [(0, 1), (1, 0)])


def swap_bit(block, bit, dp_size):
    return lax.ppermute(block, "dp", [(place, place ^ (1 << bit)) for place in range(dp_size)])


def in_order(flag, mine, other):
    first = jnp.where(flag == 0, mine, other)
    second = jnp.where(flag == 0, other, mine)
    return jnp.concatenate([first, second], axis=0)


def add_rounded(left, right):
    return (left.astype(f32) + right.astype(f32)).astype(bf16)


def norm_forward(rows, gain_row, shift_row):
    mean = jnp.mean(rows, axis=-1, keepdims=True)
    centered = rows - mean
    rate = lax.rsqrt(jnp.mean(centered * centered, axis=-1, keepdims=True) + norm_eps)
    normed = centered * rate * gain_row + shift_row
    return normed.astype(bf16), (rows, mean, rate)


def norm_backward(saved, grad_normed, gain_row):
    rows, mean, rate = saved
    unit = (rows - mean) * rate
    grad_unit = grad_normed * gain_row
    grad_rows = rate * (
        grad_unit
        - jnp.mean(grad_unit, axis=-1, keepdims=True)
        - unit * jnp.mean(grad_unit * unit, axis=-1, keepdims=True)
    )
    return grad_rows, jnp.sum(grad_normed * unit, axis=0), jnp.sum(grad_normed, axis=0)


def gelu_pair(hidden):
    square = hidden * hidden
    inner = 0.7978845608 * hidden * (1.0 + 0.044715 * square)
    bent = jnp.tanh(inner)
    value = 0.5 * hidden * (1.0 + bent)
    slope = 0.5 * (1.0 + bent) + 0.5 * hidden * (1.0 - bent * bent) * 0.7978845608 * (
        1.0 + 3.0 * 0.044715 * square
    )
    return value.astype(bf16), slope.astype(bf16)


def dot_sum(pairs, dims):
    total = None
    for left, right in pairs:
        term = lax.dot_general(left, right, dims, preferred_element_type=f32)
        total = term if total is None else total + term
    return total


def dot_low(left, right, dims):
    return lax.dot_general(left, right, dims, preferred_element_type=f32).astype(bf16)


NN = (((1,), (0,)), ((), ()))
SPLIT_AXIS = {"up": 1, "down": 0}
PACK_WIDTH = 512


def quarter_of(kind, half, place):
    axis = SPLIT_AXIS[kind]
    width = half.shape[axis] // 2
    return lax.dynamic_slice_in_dim(half, place * width, width, axis)


def row_half(block, place):
    height = block.shape[0] // 2
    return lax.dynamic_slice_in_dim(block, place * height, height, 0)


def flat_kernel(in_ref, out_ref):
    width = in_ref.shape[3]
    for part in range(3):
        out_ref[:, part * width : (part + 1) * width] = in_ref[0, part]


def flat_qkv(stacked, layer):
    _, _, height, width = stacked.shape
    rows = height // 2
    return pl.pallas_call(
        flat_kernel,
        grid=(2,),
        in_specs=[pl.BlockSpec((1, 3, rows, width), lambda step: (layer, 0, step, 0))],
        out_specs=pl.BlockSpec((rows, 3 * width), lambda step: (step, 0)),
        out_shape=jax.ShapeDtypeStruct((height, 3 * width), bf16),
        cost_estimate=pl.CostEstimate(flops=0, bytes_accessed=12 * height * width, transcendentals=0),
        name="flat_qkv",
    )(stacked)


def pack_kernel(kinds, place_ref, *refs):
    out_ref = refs[-1]
    at = 0
    for kind, ref in zip(kinds, refs):
        if kind == "qkv":
            pieces = [ref[0, part] for part in range(3)]
        else:
            count = ref.shape[2] // PACK_WIDTH
            pieces = [ref[0, :, part * PACK_WIDTH : (part + 1) * PACK_WIDTH] for part in range(count)]
        for piece in pieces:
            out_ref[at : at + piece.shape[0], :] = piece
            at += piece.shape[0]


def pack_pieces(place, layer, dp_size, kinds, arrays):
    specs, total = [], 0
    for kind, array in zip(kinds, arrays):
        height, width = array.shape[-2:]
        rows = height // dp_size
        if kind == "qkv":
            specs.append(pl.BlockSpec((1, 3, rows, width), lambda step, at: (layer, 0, at[0], 0)))
            total += 3 * rows * width // PACK_WIDTH
        else:
            specs.append(pl.BlockSpec((1, rows, width), lambda step, at: (layer, at[0], 0)))
            total += rows * width // PACK_WIDTH
    return pl.pallas_call(
        partial(pack_kernel, kinds),
        grid_spec=pltpu.PrefetchScalarGridSpec(
            num_scalar_prefetch=1,
            grid=(1,),
            in_specs=specs,
            out_specs=pl.BlockSpec((total, PACK_WIDTH), lambda step, at: (0, 0)),
        ),
        out_shape=jax.ShapeDtypeStruct((total, PACK_WIDTH), bf16),
        cost_estimate=pl.CostEstimate(flops=0, bytes_accessed=4 * total * PACK_WIDTH, transcendentals=0),
        name="pack_pieces",
    )(place.reshape(1).astype(jnp.int32), *arrays)


def unpack_kernel(in_ref, *refs):
    at = 0
    for ref in refs:
        rows = ref.shape[0] // in_ref.shape[0]
        for part in range(ref.shape[1] // PACK_WIDTH):
            for block in range(in_ref.shape[0]):
                ref[block * rows : (block + 1) * rows, part * PACK_WIDTH : (part + 1) * PACK_WIDTH] = in_ref[
                    block, at : at + rows, :
                ]
            at += rows


def unpack_halves(gathered, shapes):
    dp_size, total, _ = gathered.shape
    some = max(1, dp_size // 4)
    return pl.pallas_call(
        unpack_kernel,
        grid=(dp_size // some,),
        in_specs=[pl.BlockSpec((some, total, PACK_WIDTH), lambda step: (step, 0, 0))],
        out_specs=[
            pl.BlockSpec((height // dp_size * some, width), lambda step: (step, 0)) for height, width in shapes
        ],
        out_shape=[jax.ShapeDtypeStruct(shape, bf16) for shape in shapes],
        compiler_params=pltpu.CompilerParams(vmem_limit_bytes=32 * 2**20),
        cost_estimate=pl.CostEstimate(
            flops=0, bytes_accessed=4 * dp_size * total * PACK_WIDTH, transcendentals=0
        ),
        name="unpack_halves",
    )(gathered)


def place_kernel(kind, whole_ref, *refs):
    out_ref = refs[-1]
    block = whole_ref[...].reshape(-1, whole_ref.shape[-1]).astype(f32)
    if kind == "qkv":
        width = block.shape[1] // 3
        for part in range(3):
            out_ref[0, part] = block[:, part * width : (part + 1) * width]
    else:
        out_ref[0] = block


def place_grad(kind, whole, layer, split, base):
    dp_size, rows, columns = whole.shape
    half, some = dp_size // 2, dp_size // 4
    whole = whole.reshape(half, 2, rows, columns)
    if split == "rows":
        block, source = (some, 2, rows, columns), lambda step: (step, 0, 0, 0)
        steps = half // some
        tall = some * 2 * rows
        if kind == "qkv":
            out_shape = (2, 3, dp_size * rows, columns // 3)
            out_spec = pl.BlockSpec((1, 3, tall, columns // 3), lambda step: (layer, 0, step, 0))
        else:
            out_shape = (2, dp_size * rows, columns)
            out_spec = pl.BlockSpec((1, tall, columns), lambda step: (layer, step, 0))
    else:
        block, source = (some, None, rows, columns), lambda step: (step % 2, step // 2, 0, 0)
        steps = 4
        if kind == "down":
            out_shape = (2, dp_size * rows, columns)
            out_spec = pl.BlockSpec((1, some * rows, columns), lambda step: (layer, step, 0))
        else:
            out_shape = (2, half * rows, 2 * columns)
            out_spec = pl.BlockSpec((1, some * rows, columns), lambda step: (layer, step % 2, step // 2))
    operands, in_specs, aliases = [whole], [pl.BlockSpec(block, source)], {}
    if base is not None:
        operands.append(base)
        in_specs.append(pl.BlockSpec(memory_space=pl.ANY))
        aliases = {1: 0}
    return pl.pallas_call(
        partial(place_kernel, kind),
        grid=(steps,),
        in_specs=in_specs,
        out_specs=out_spec,
        out_shape=jax.ShapeDtypeStruct(out_shape, f32),
        input_output_aliases=aliases,
        compiler_params=pltpu.CompilerParams(vmem_limit_bytes=32 * 2**20),
        cost_estimate=pl.CostEstimate(flops=0, bytes_accessed=6 * dp_size * rows * columns, transcendentals=0),
        name="place_" + kind,
    )(*operands)


def frame_kernel(side_ref, mine_ref, other_ref, out_ref):
    own = pl.program_id(0) == side_ref[0]
    out_ref[0, 0] = jnp.where(own, mine_ref[...], other_ref[...].astype(f32))


def place_frames(side, mine, other):
    height, width = mine.shape
    rows = height // 2
    spec = pl.BlockSpec((rows, width), lambda slot, step, side_ref: (step, 0))
    return pl.pallas_call(
        frame_kernel,
        grid_spec=pltpu.PrefetchScalarGridSpec(
            num_scalar_prefetch=1,
            grid=(2, 2),
            in_specs=[spec, spec],
            out_specs=pl.BlockSpec((1, 1, rows, width), lambda slot, step, side_ref: (slot, 0, step, 0)),
        ),
        out_shape=jax.ShapeDtypeStruct((2, 1, height, width), f32),
        name="place_frames",
    )(side.reshape(1).astype(jnp.int32), mine, other)


def take_axis(block, index):
    return lax.dynamic_index_in_dim(block, index, 1, keepdims=False)


def flat_rows(block):
    return block.reshape(-1, block.shape[-1])


class Chain:
    def __init__(self, place, dp_size, rows, columns, kind, gather):
        self.place, self.dp_size, self.kind, self.gather = place, dp_size, kind, gather
        self.rows, self.columns = rows, columns
        self.bit_count = dp_size.bit_length() - 1
        self.flight = []

    def bit(self, index):
        return (self.place >> index) & 1

    def swap(self, block, bit):
        return swap_bit(block, bit, self.dp_size)

    def pair(self, block):
        return block.reshape(-1, 2, self.rows, self.columns)

    def start(self, near, far, ours=None, own_far=None):
        self.near, self.ours = near, ours
        self.flight = [self.swap(far, 0)] + ([] if ours is None else [self.swap(own_far, 0)])
        self.state = "core"

    def start_rows(self, own, other):
        self.start_other(other)
        self.add_own(own)

    def start_other(self, other):
        split, core = self.pair(other), self.bit(0)
        self.start(flat_rows(take_axis(split, core)), flat_rows(take_axis(split, 1 - core)))

    def add_own(self, own):
        split, core = self.pair(own), self.bit(0)
        self.flight = self.flight + [self.swap(flat_rows(take_axis(split, 1 - core)), 0)]
        self.ours = flat_rows(take_axis(split, core))

    def halves(self, block, bit):
        split, here = self.pair(block), self.bit(bit)
        return flat_rows(take_axis(split, here)), flat_rows(take_axis(split, 1 - here))

    def settle(self, arrived):
        self.near_here, self.near_away = self.halves(add_rounded(self.near, arrived[0]), 1)
        if self.ours is not None:
            self.kept_here, self.kept_away = self.halves(add_rounded(self.ours, arrived[1]), 1)
        self.flight, self.state = [], "ready"

    def launch(self):
        self.flight = [swap_tensor(self.near_away) if self.kind == "x" else self.swap(self.near_away, 1)]
        self.state = "first"

    def second(self, arrived):
        if len(arrived) > 1:
            self.kept_here, self.kept_away = self.halves(add_rounded(self.ours, arrived[1]), 1)
        if self.kind == "x":
            self.kept_away = add_rounded(self.kept_away, arrived[0])
        else:
            self.near_here = add_rounded(self.near_here, arrived[0])
        self.flight = [swap_tensor(self.near_here), self.swap(self.kept_away, 1)]
        self.state = "second"

    def next_bit(self, total, index):
        if index == self.bit_count:
            self.kept, self.state = total, "gather"
            if self.gather == "native":
                self.flight = [lax.all_gather(total, "dp", axis=0, tiled=False)]
                return
            self.kept, self.level = total[None], index - 1
            self.flight = [self.swap(self.kept, self.level)]
            return
        self.kept, away = self.halves(total, index)
        self.flight, self.index, self.state = [self.swap(away, index)], index, "bits"

    def advance(self, arrived, hold=False):
        if self.state == "done":
            return
        if self.state == "core":
            self.settle(arrived)
            if not hold:
                self.launch()
        elif self.state == "ready":
            self.launch()
        elif self.state == "first":
            self.second(arrived)
        elif self.state == "second":
            total = self.kept_here.astype(f32) + arrived[0].astype(f32) + arrived[1].astype(f32)
            self.next_bit(total.astype(bf16), 2)
        elif self.state == "bits":
            self.next_bit(add_rounded(self.kept, arrived[0]), self.index + 1)
        elif self.gather == "native":
            self.whole, self.flight, self.state = arrived[0], [], "done"
        else:
            here = self.bit(self.level)
            first = jnp.where(here == 0, self.kept, arrived[0])
            second = jnp.where(here == 0, arrived[0], self.kept)
            joined = jnp.stack([first, second], axis=1)
            self.kept = joined.reshape((-1,) + joined.shape[2:])
            self.level -= 1
            if self.level < 0:
                self.whole, self.flight, self.state = self.kept, [], "done"
            else:
                self.flight = [self.swap(self.kept, self.level)]


class Spread:
    def __init__(self, block, dp_size):
        self.block, self.dp_size = block, dp_size
        self.bits = list(range(dp_size.bit_length() - 1))
        self.flight = [swap_tensor(block)]

    def advance(self, arrived):
        if not arrived:
            return
        self.block = self.block + arrived[0]
        self.flight = [swap_bit(self.block, self.bits.pop(0), self.dp_size)] if self.bits else []


def move(state, *chains, hold=()):
    everyone = chains + tuple(hold)
    state, flights = pin(state, [one.flight for one in everyone])
    for one, flight in zip(everyone, flights):
        if one in hold:
            one.advance(flight, hold=True)
        else:
            one.advance(flight)
    return state


def paired_device(
    dp_size,
    frames_in,
    phone_len,
    frame_len,
    section,
    norm_gain,
    norm_bias,
    ada_scale,
    ada_shift,
    w_qkv,
    w_out,
    w_up,
    w_down,
    out_grad,
):
    model_width = frames_in.shape[3]
    section_count = ada_scale.shape[1]
    side = lax.axis_index("tensor")
    place = lax.axis_index("dp")
    core, near_row = place & 1, (place >> 1) & 1

    def away_rows(halves):
        return lax.dynamic_index_in_dim(halves[:, 0], 1 - side, 0, keepdims=False)

    def whole_rows(halves, other):
        mine = lax.dynamic_index_in_dim(halves[:, 0], side, 0, keepdims=False)
        return in_order(side, mine, other)

    prefix = lax.dynamic_index_in_dim(phone_len[:, 0], side, 0, keepdims=False)
    frames = lax.dynamic_index_in_dim(frame_len[:, 0], side, 0, keepdims=False)
    chosen = lax.dynamic_index_in_dim(section[:, 0], side, 0, keepdims=False)
    limits = jnp.stack([prefix, prefix + frames]).astype(jnp.int32)
    picker = (lax.iota(jnp.int32, section_count) == chosen).astype(f32)[:, None]

    gains = [
        [norm_gain[0], norm_gain[1]],
        [jnp.sum(picker * ada_scale[part], axis=0) for part in range(2)],
    ]
    shifts = [
        [norm_bias[0], norm_bias[1]],
        [jnp.sum(picker * ada_shift[part], axis=0) for part in range(2)],
    ]

    stacked = w_qkv.transpose(0, 2, 1, 3)
    arrays = {"qkv": stacked, "out": w_out, "up": w_up, "down": w_down}
    flat_shape = {
        "qkv": (model_width, 3 * stacked.shape[3]),
        "out": w_out.shape[1:],
        "up": w_up.shape[1:],
        "down": w_down.shape[1:],
    }

    def packed(layer, kinds):
        return pack_pieces(place, layer, dp_size, kinds, [arrays[kind] for kind in kinds])

    def gathered(arrived):
        return lax.all_gather(arrived, "dp", axis=0, tiled=False)

    def unpacked(whole, kinds):
        return dict(zip(kinds, unpack_halves(whole, [flat_shape[kind] for kind in kinds])))

    attn_kinds, all_kinds = ("qkv", "out"), ("qkv", "out", "up", "down")
    first_pack = swap_tensor(packed(0, attn_kinds))
    other_rows = swap_tensor(away_rows(frames_in))
    first_whole = gathered(first_pack)
    second_send = packed(1, all_kinds)
    up_send = row_half(quarter_of("up", w_up[0], core), near_row)
    down_send = row_half(quarter_of("down", w_down[0], core), near_row)
    own_qkv = [flat_qkv(stacked, layer) for layer in range(2)]
    other_rows, second_send, up_send, down_send, own_qkv = pin(
        other_rows, second_send, up_send, down_send, own_qkv
    )
    second_pack = swap_tensor(second_send)
    rows = whole_rows(frames_in, other_rows).astype(f32)
    normed, norm_kept = norm_forward(rows, gains[0][0], shifts[0][0])
    mine = dot_low(normed, own_qkv[0], NN)
    mine, second_pack, up_send, down_send = pin(mine, second_pack, up_send, down_send)
    second_whole = gathered(second_pack)
    up_piece = swap_tensor(up_send)
    mix_mine = attn_fwd(mine, limits, True, 512)
    mix_mine, up_piece, down_send = pin(mix_mine, up_piece, down_send)
    down_piece = swap_tensor(down_send)
    up_there = swap_bit(up_piece, 1, dp_size)
    first = unpacked(first_whole, attn_kinds)
    theirs = dot_low(normed, first["qkv"], NN)
    mix_theirs = attn_fwd(theirs, limits, True, 512)
    mix_theirs, up_there, down_piece = pin(mix_theirs, up_there, down_piece)
    up_near = in_order(near_row, up_piece, up_there)
    up_far = swap_bit(up_near, 0, dp_size)
    down_there = swap_bit(down_piece, 1, dp_size)
    kept = [(normed, norm_kept, [mine, theirs], [mix_mine, mix_theirs])]
    rows = rows + dot_sum([(mix_mine[0], w_out[0]), (mix_theirs[0], first["out"])], NN)
    normed, norm_kept = norm_forward(rows, gains[0][1], shifts[0][1])
    pair_own = gelu_pair(jnp.dot(normed, w_up[0], preferred_element_type=f32))
    pair_own, up_far, normed, norm_kept, rows = pin(pair_own, up_far, normed, norm_kept, rows)
    pair_near = gelu_pair(jnp.dot(normed, up_near, preferred_element_type=f32))
    pair_far = gelu_pair(jnp.dot(normed, up_far, preferred_element_type=f32))
    rows = rows + dot_sum([(pair_own[0], w_down[0])], NN)
    rows, pair_near, pair_far, down_there = pin(rows, pair_near, pair_far, down_there)
    down_near = in_order(near_row, down_piece, down_there)
    down_far = swap_bit(down_near, 0, dp_size)
    grad_send = away_rows(out_grad)
    rows = rows + dot_sum([(pair_near[0], down_near)], NN)
    rows, grad_send, down_far = pin(rows, grad_send, down_far)
    grad_other = swap_tensor(grad_send)
    rows = rows + dot_sum([(pair_far[0], down_far)], NN)
    kept.append((normed, norm_kept, [pair_own, pair_near, pair_far]))

    normed, norm_kept = norm_forward(rows, gains[1][0], shifts[1][0])
    mine = dot_low(normed, own_qkv[1], NN)
    mix_mine = attn_fwd(mine, limits, False, 512)
    mix_mine, second_whole = pin(mix_mine, second_whole)
    second = unpacked(second_whole, all_kinds)
    weights = [
        {
            "qkv": [own_qkv[0], first["qkv"]],
            "out": [w_out[0], first["out"]],
            "up": [w_up[0], up_near, up_far],
            "down": [w_down[0], down_near, down_far],
        },
        {
            "qkv": [own_qkv[1], second["qkv"]],
            "out": [w_out[1], second["out"]],
            "up": [w_up[1], second["up"]],
            "down": [w_down[1], second["down"]],
        },
    ]
    theirs = dot_low(normed, second["qkv"], NN)
    mix_theirs = attn_fwd(theirs, limits, False, 512)
    mixed = [mix_mine, mix_theirs]
    kept.append((normed, norm_kept, [mine, theirs], mixed))
    rows = rows + dot_sum([(mix[0], part) for mix, part in zip(mixed, weights[1]["out"])], NN)
    normed, norm_kept = norm_forward(rows, gains[1][1], shifts[1][1])
    pairs = [gelu_pair(jnp.dot(normed, part, preferred_element_type=f32)) for part in weights[1]["up"]]
    pairs, rows, normed, norm_kept = pin(pairs, rows, normed, norm_kept)
    rows = rows + dot_sum([(pair[0], part) for pair, part in zip(pairs, weights[1]["down"])], NN)
    kept.append((normed, norm_kept, pairs))
    rows, grad_other = pin(rows, grad_other)

    def halves_of(block):
        height = block.shape[0] // 2
        mine = lax.dynamic_slice_in_dim(block, side * height, height, 0)
        away = lax.dynamic_slice_in_dim(block, (1 - side) * height, height, 0)
        return mine, away.astype(bf16)

    out_mine, out_away = halves_of(rows)

    norm_sums = [[None, None], [None, None]]
    grad_rows = whole_rows(out_grad, grad_other).astype(f32)
    def chain(kind, first, gather, split="rows"):
        height, width = flat_shape[kind]
        if split == "core":
            count = dp_size // 2
            height, width = (height, width // 2) if kind == "up" else (height // 2, width)
        else:
            count = dp_size
        return Chain(place, dp_size, height // count, width, first, gather)

    def start_quarters(one, kind, parts):
        own, near, far = parts
        one.start(near, far, quarter_of(kind, own, core), quarter_of(kind, own, 1 - core))

    def hidden_grads(layer, low):
        pairs = kept[2 * layer + 1][2]
        return [
            (
                lax.dot_general(low, part, NT, preferred_element_type=f32) * pair[1].astype(f32)
            ).astype(bf16)
            for pair, part in zip(pairs, weights[layer]["down"])
        ]

    def down_grads(layer, low):
        return [dot_low(pair[0], low, TN) for pair in kept[2 * layer + 1][2]]

    def up_grads(layer, hidden):
        return [dot_low(kept[2 * layer + 1][0], part, TN) for part in hidden]

    def out_grads(layer, low):
        return [dot_low(mix[0], low, TN) for mix in kept[2 * layer][3]]

    def mixed_grads(layer, low):
        return [dot_low(low, part, NT) for part in weights[layer]["out"]]

    def attention_grad(layer, part, grad_mix):
        _, _, projected, mixed = kept[2 * layer]
        rows = 256 if layer == 0 else 512
        return attn_bwd(projected[part], mixed[part][1], grad_mix, limits, layer == 0, rows)

    def norm_step(layer, part, grad_rows, grad_normed):
        added, grad_gain, grad_shift = norm_backward(
            kept[2 * layer + part][1], grad_normed, gains[layer][part]
        )
        norm_sums[layer][part] = (grad_gain, grad_shift)
        return grad_rows + added

    down1, up1 = chain("down", "x", "native"), chain("up", "y", "native")
    out1, qkv1 = chain("out", "x", "native"), chain("qkv", "y", "native")
    down0, up0 = chain("down", "x", "native", "core"), chain("up", "y", "swaps", "core")
    out0, qkv0 = chain("out", "x", "swaps"), chain("qkv", "y", "swaps")

    low = grad_rows.astype(bf16)
    parts = down_grads(1, low)
    hidden = hidden_grads(1, low)
    parts, hidden, grad_rows = pin(parts, hidden, grad_rows)
    down1.start_rows(*parts)
    parts = up_grads(1, hidden)
    parts, hidden, grad_rows = move((parts, hidden, grad_rows), down1)
    up1.start_rows(*parts)
    grad_normed = dot_sum(list(zip(hidden, weights[1]["up"])), NT)
    grad_rows = norm_step(1, 1, grad_rows, grad_normed)
    low = grad_rows.astype(bf16)
    out_parts = out_grads(1, low)
    mine, theirs = mixed_grads(1, low)
    out_parts, mine, theirs, grad_rows = move((out_parts, mine, theirs, grad_rows), down1, hold=[up1])
    out1.start_rows(*out_parts)
    theirs = attention_grad(1, 1, theirs)
    mine, theirs, grad_rows = move((mine, theirs, grad_rows), down1, up1, out1)
    mine = attention_grad(1, 0, mine)
    mine, theirs, grad_rows = move((mine, theirs, grad_rows), down1, up1, out1)
    parts = [dot_low(kept[2][0], part, TN) for part in (mine, theirs)]
    grad_normed = dot_sum(list(zip((mine, theirs), weights[1]["qkv"])), NT)
    grad_rows = norm_step(1, 0, grad_rows, grad_normed)
    early = Spread(
        jnp.concatenate(
            [picker * norm_sums[1][part][which][None] for which in range(2) for part in range(2)]
        ),
        dp_size,
    )
    low = grad_rows.astype(bf16)
    parts, low, grad_rows = move((parts, low, grad_rows), down1, up1, out1)
    qkv1.start_rows(*parts)
    parts = down_grads(0, low)
    parts, low, grad_rows = move((parts, low, grad_rows), up1, qkv1, early)
    start_quarters(down0, "down", parts)
    hidden = hidden_grads(0, low)
    hidden, grad_rows = move((hidden, grad_rows), down1, up1, qkv1, out1, early, hold=[down0])
    parts = up_grads(0, hidden)
    grad_normed = dot_sum(list(zip(hidden, weights[0]["up"])), NT)
    parts, grad_normed, grad_rows = move((parts, grad_normed, grad_rows), qkv1, out1, down0, early)
    start_quarters(up0, "up", parts)
    grad_rows = norm_step(0, 1, grad_rows, grad_normed)
    low = grad_rows.astype(bf16)
    out_parts = out_grads(0, low)
    mine, theirs = mixed_grads(0, low)
    out_parts, mine, theirs, grad_rows = move((out_parts, mine, theirs, grad_rows), up0, qkv1, down0, early)
    out0.start_rows(*out_parts)
    theirs = attention_grad(0, 1, theirs)
    mine, theirs, grad_rows = move((mine, theirs, grad_rows), up1, down0, up0, qkv1, early, hold=[out0])
    part_theirs = dot_low(kept[0][0], theirs, TN)
    qkv0.start_other(part_theirs)
    mine = attention_grad(0, 0, mine)
    mine, theirs, grad_rows = move((mine, theirs, grad_rows), out1, down0, up0, qkv0)
    part_mine = dot_low(kept[0][0], mine, TN)
    qkv0.add_own(part_mine)
    grad_normed = dot_sum([(mine, weights[0]["qkv"][0]), (theirs, weights[0]["qkv"][1])], NT)
    grad_rows = norm_step(0, 0, grad_rows, grad_normed)
    grad_mine, grad_away = halves_of(grad_rows)
    late = Spread(
        jnp.stack([norm_sums[0][part][which] for which in range(2) for part in range(2)]), dp_size
    )
    both_away = (grad_away, out_away)
    both_away, grad_mine = move((both_away, grad_mine), qkv0, up0, down0, out0)
    both_away, grad_mine = move((both_away, grad_mine), qkv0, up0, out0, late)
    there = [swap_tensor(block) for block in both_away]
    there, grad_mine = move((there, grad_mine), qkv0, up0, out0, late)
    (grad_mine,) = move((grad_mine,), qkv1, qkv0, up0, out0, late)

    def placed(kind, one):
        return place_grad(kind, one.whole, 1, "rows", None)

    bases = {"down": placed("down", down1), "up": placed("up", up1)}
    bases, grad_mine = move((bases, grad_mine), qkv0, up0, out0, late)
    bases["out"], bases["qkv"] = placed("out", out1), placed("qkv", qkv1)
    bases, grad_mine = move((bases, grad_mine), down0, qkv0, up0, out0)
    frames_grad = place_frames(side, grad_mine, there[0])
    frames_out = place_frames(side, out_mine, there[1])
    frames_grad, frames_out = move((frames_grad, frames_out), qkv0, up0, out0)
    for one in (qkv0, up0, out0, down0, late, down1, up1, out1, qkv1, early):
        while one.flight:
            one.advance(one.flight)

    def both(kind, sooner, split="rows"):
        return place_grad(kind, sooner.whole, 0, split, bases[kind])

    gain_rows = early.block.reshape(4, section_count, model_width)
    return (
        frames_out,
        frames_grad,
        both("qkv", qkv0).transpose(0, 2, 1, 3),
        both("out", out0),
        both("up", up0, "core"),
        both("down", down0, "core"),
        late.block[0:2],
        late.block[2:4],
        gain_rows[0:2],
        gain_rows[2:4],
    )


def per_device(dp_size, tensor_size, *arrays):
    micro_count, local_seqs = arrays[0].shape[:2]
    paired = micro_count == 2 and tensor_size == 2 and local_seqs == 1
    if paired and dp_size >= 4 and dp_size & (dp_size - 1) == 0:
        return paired_device(dp_size, *arrays)
    return grouped_device(*arrays)


def solution(mesh):
    return jax.shard_map(
        partial(per_device, mesh.shape["dp"], mesh.shape["tensor"]),
        mesh=mesh,
        in_specs=(
            P(None, "dp", "tensor", None),
            P(None, "dp"),
            P(None, "dp"),
            P(None, "dp"),
            P(),
            P(),
            P(),
            P(),
            P(None, None, None, "tensor"),
            P(None, "tensor", None),
            P(None, None, "tensor"),
            P(None, "tensor", None),
            P(None, "dp", "tensor", None),
        ),
        out_specs=(
            P(None, "dp", "tensor", None),
            P(None, "dp", "tensor", None),
            P(None, None, None, "tensor"),
            P(None, "tensor", None),
            P(None, None, "tensor"),
            P(None, "tensor", None),
            P(),
            P(),
            P(),
            P(),
        ),
        check_vma=False,
    )
```

```python
from functools import partial

import jax
import jax.numpy as jnp
from jax import lax
from jax.experimental import pallas as pl
from jax.experimental.pallas import tpu as pltpu
from jax.sharding import PartitionSpec as P

HEAD_DIM = 64


norm_eps = 1e-05
masked_score = -1000000000.0
contract_rows = (((0,), (0,)), ((), ()))
contract_cols = (((1,), (1,)), ((), ()))


def plain_norm(inputs):
    centered = inputs - jnp.mean(inputs, axis=-1, keepdims=True)
    variance = jnp.mean(centered * centered, axis=-1, keepdims=True)
    return centered * lax.rsqrt(variance + norm_eps)


def fixed_norm(inputs, gain_row, shift_row):
    return plain_norm(inputs) * gain_row + shift_row


def section_norm(inputs, scale_table, shift_table, picker):
    scale_row = jnp.dot(
        picker, scale_table, precision=lax.Precision.HIGHEST, preferred_element_type=jnp.float32
    )
    shift_row = jnp.dot(
        picker, shift_table, precision=lax.Precision.HIGHEST, preferred_element_type=jnp.float32
    )
    return plain_norm(inputs) * scale_row + shift_row


def gather_normed(normed_low):
    return lax.all_gather(normed_low, "tensor", axis=0, tiled=True)


def gather_again(normed_low):
    return lax.all_gather(normed_low, "tensor", axis=0, tiled=True)


def sum_branch(branch_part):
    return lax.psum_scatter(
        branch_part.astype(jnp.bfloat16), "tensor", scatter_dimension=0, tiled=True
    ).astype(jnp.float32)


def gather_grad(grad_low):
    return lax.all_gather(grad_low, "tensor", axis=0, tiled=True)


def sum_normed(grad_part):
    return lax.psum_scatter(
        grad_part.astype(jnp.bfloat16), "tensor", scatter_dimension=0, tiled=True
    ).astype(jnp.float32)


def key_allowed(query_pos, key_pos, prefix, valid_count, causal):
    allowed = key_pos[None, :] < valid_count
    if causal:
        allowed = allowed & ((key_pos[None, :] < prefix) | (key_pos[None, :] <= query_pos[:, None]))
    return allowed


def split_heads(projected):
    length = projected.shape[0]
    head_width = projected.shape[1] // 3
    head_count = head_width // HEAD_DIM
    query_rows = projected[:, :head_width].reshape(length, head_count, HEAD_DIM)
    key_rows = projected[:, head_width : 2 * head_width].reshape(length, head_count, HEAD_DIM)
    value_rows = projected[:, 2 * head_width :].reshape(length, head_count, HEAD_DIM)
    return (query_rows, key_rows, value_rows)


def block_scores(query_block, key_rows, block_start, prefix, valid_count, causal):
    block_rows = query_block.shape[0]
    length = key_rows.shape[0]
    scores = jnp.einsum(
        "qhd,khd->hqk", query_block, key_rows, preferred_element_type=jnp.float32
    ) * HEAD_DIM ** (-0.5)
    query_pos = block_start + lax.iota(jnp.int32, block_rows)
    key_pos = lax.iota(jnp.int32, length)
    allowed = key_allowed(query_pos, key_pos, prefix, valid_count, causal)
    return jnp.where(allowed[None], scores, masked_score)


def attend_forward(projected, prefix, valid_count, causal, block_rows):
    length = projected.shape[0]
    head_width = projected.shape[1] // 3
    query_rows, key_rows, value_rows = split_heads(projected)

    def one_block(block_start):
        query_block = lax.dynamic_slice_in_dim(query_rows, block_start, block_rows, 0)
        scores = block_scores(query_block, key_rows, block_start, prefix, valid_count, causal)
        highest = jnp.max(scores, axis=-1, keepdims=True)
        row_total = jnp.sum(jnp.exp(scores - highest), axis=-1, keepdims=True)
        log_total = highest + jnp.log(row_total)
        shares = jnp.exp(scores - log_total).astype(jnp.bfloat16)
        mixture = jnp.einsum("hqk,khd->qhd", shares, value_rows, preferred_element_type=jnp.float32)
        return (mixture.astype(jnp.bfloat16), log_total)

    starts = lax.iota(jnp.int32, length // block_rows) * block_rows
    mixture, log_totals = lax.map(one_block, starts)
    return (mixture.reshape(length, head_width), log_totals)


def attend_backward(projected, log_totals, grad_mixture, prefix, valid_count, causal, block_rows):
    length = projected.shape[0]
    head_width = projected.shape[1] // 3
    query_rows, key_rows, value_rows = split_heads(projected)
    grad_rows = grad_mixture.reshape(query_rows.shape)
    score_scale = HEAD_DIM ** (-0.5)

    def one_block(grad_state, block_item):
        block_start, log_total = block_item
        grad_key, grad_value = grad_state
        query_block = lax.dynamic_slice_in_dim(query_rows, block_start, block_rows, 0)
        grad_block = lax.dynamic_slice_in_dim(grad_rows, block_start, block_rows, 0)
        scores = block_scores(query_block, key_rows, block_start, prefix, valid_count, causal)
        shares = jnp.exp(scores - log_total)
        shares_low = shares.astype(jnp.bfloat16)
        grad_shares = jnp.einsum(
            "qhd,khd->hqk", grad_block, value_rows, preferred_element_type=jnp.float32
        )
        inner_sum = jnp.sum(shares * grad_shares, axis=-1, keepdims=True)
        grad_scores = (shares * (grad_shares - inner_sum)).astype(jnp.bfloat16)
        grad_query = (
            jnp.einsum("hqk,khd->qhd", grad_scores, key_rows, preferred_element_type=jnp.float32)
            * score_scale
        )
        grad_key = (
            grad_key
            + jnp.einsum(
                "hqk,qhd->khd", grad_scores, query_block, preferred_element_type=jnp.float32
            )
            * score_scale
        )
        grad_value = grad_value + jnp.einsum(
            "hqk,qhd->khd", shares_low, grad_block, preferred_element_type=jnp.float32
        )
        return ((grad_key, grad_value), grad_query)

    starts = lax.iota(jnp.int32, length // block_rows) * block_rows
    zero_rows = jnp.zeros(query_rows.shape, jnp.float32)
    grad_state, grad_query = lax.scan(one_block, (zero_rows, zero_rows), (starts, log_totals))
    grad_key, grad_value = grad_state
    joined = jnp.concatenate(
        [
            grad_query.reshape(length, head_width),
            grad_key.reshape(length, head_width),
            grad_value.reshape(length, head_width),
        ],
        axis=1,
    )
    return joined.astype(jnp.bfloat16)


def grouped_device(
    frames_in,
    phone_len,
    frame_len,
    section,
    norm_gain,
    norm_bias,
    ada_scale,
    ada_shift,
    w_qkv,
    w_out,
    w_up,
    w_down,
    out_grad,
):
    micro_count, local_seqs, local_rows, model_width = frames_in.shape
    seq_length = local_rows * lax.axis_size("tensor")
    block_rows = min(512, seq_length)
    section_count = ada_scale.shape[1]
    qkv_mats = [w_qkv[layer_index].reshape(model_width, -1) for layer_index in range(2)]
    acc_qkv = [jnp.zeros(qkv_mats[layer_index].shape, jnp.float32) for layer_index in range(2)]
    acc_out = [jnp.zeros(w_out.shape[1:], jnp.float32) for layer_index in range(2)]
    acc_up = [jnp.zeros(w_up.shape[1:], jnp.float32) for layer_index in range(2)]
    acc_down = [jnp.zeros(w_down.shape[1:], jnp.float32) for layer_index in range(2)]
    acc_gain = [jnp.zeros((model_width,), jnp.float32) for part_index in range(2)]
    acc_bias = [jnp.zeros((model_width,), jnp.float32) for part_index in range(2)]
    acc_scale = [jnp.zeros((section_count, model_width), jnp.float32) for part_index in range(2)]
    acc_shift = [jnp.zeros((section_count, model_width), jnp.float32) for part_index in range(2)]
    frames_list = []
    grads_list = []
    for micro_index in range(micro_count):
        prefix = phone_len[micro_index, 0]
        valid_count = prefix + frame_len[micro_index, 0]
        picker = (lax.iota(jnp.int32, section_count) == section[micro_index, 0]).astype(
            jnp.float32
        )[None, :]
        residual = frames_in[micro_index, 0].astype(jnp.float32)
        stored = []
        for layer_index in range(2):
            for part_index in range(2):
                if layer_index == 0:
                    normed, norm_back = jax.vjp(
                        fixed_norm, residual, norm_gain[part_index], norm_bias[part_index]
                    )
                else:
                    normed, norm_back = jax.vjp(
                        partial(section_norm, picker=picker),
                        residual,
                        ada_scale[part_index],
                        ada_shift[part_index],
                    )
                normed_low = normed.astype(jnp.bfloat16)
                gathered = gather_normed(normed_low)
                if part_index == 0:
                    projected = jnp.dot(
                        gathered, qkv_mats[layer_index], preferred_element_type=jnp.float32
                    ).astype(jnp.bfloat16)
                    mixture, log_totals = attend_forward(
                        projected, prefix, valid_count, layer_index == 0, block_rows
                    )
                    branch = sum_branch(
                        jnp.dot(mixture, w_out[layer_index], preferred_element_type=jnp.float32)
                    )
                    saved_state = (projected, log_totals, mixture)
                else:
                    hidden = jnp.dot(
                        gathered, w_up[layer_index], preferred_element_type=jnp.float32
                    )
                    active = jax.nn.gelu(hidden, approximate=True).astype(jnp.bfloat16)
                    branch = sum_branch(
                        jnp.dot(active, w_down[layer_index], preferred_element_type=jnp.float32)
                    )
                    saved_state = (hidden, active)
                kept_rows = normed_low
                stored.append((norm_back, kept_rows, saved_state))
                residual = residual + branch
        out_group = [residual]
        grad_rows = out_grad[micro_index, 0].astype(jnp.float32)
        for layer_index in (1, 0):
            for part_index in (1, 0):
                norm_back, kept_rows, saved_state = stored[2 * layer_index + part_index]
                gathered = gather_again(kept_rows)
                grad_whole = gather_grad(grad_rows.astype(jnp.bfloat16))
                if part_index == 1:
                    hidden, active = saved_state
                    acc_down[layer_index] = acc_down[layer_index] + lax.dot_general(
                        active, grad_whole, contract_rows, preferred_element_type=jnp.float32
                    )
                    grad_active = lax.dot_general(
                        grad_whole,
                        w_down[layer_index],
                        contract_cols,
                        preferred_element_type=jnp.float32,
                    )
                    gelu_value, gelu_back = jax.vjp(partial(jax.nn.gelu, approximate=True), hidden)
                    grad_hidden = gelu_back(grad_active)[0].astype(jnp.bfloat16)
                    acc_up[layer_index] = acc_up[layer_index] + lax.dot_general(
                        gathered, grad_hidden, contract_rows, preferred_element_type=jnp.float32
                    )
                    grad_normed = sum_normed(
                        lax.dot_general(
                            grad_hidden,
                            w_up[layer_index],
                            contract_cols,
                            preferred_element_type=jnp.float32,
                        )
                    )
                else:
                    projected, log_totals, mixture = saved_state
                    acc_out[layer_index] = acc_out[layer_index] + lax.dot_general(
                        mixture, grad_whole, contract_rows, preferred_element_type=jnp.float32
                    )
                    grad_mixture = lax.dot_general(
                        grad_whole,
                        w_out[layer_index],
                        contract_cols,
                        preferred_element_type=jnp.float32,
                    ).astype(jnp.bfloat16)
                    grad_projected = attend_backward(
                        projected,
                        log_totals,
                        grad_mixture,
                        prefix,
                        valid_count,
                        layer_index == 0,
                        block_rows,
                    )
                    acc_qkv[layer_index] = acc_qkv[layer_index] + lax.dot_general(
                        gathered, grad_projected, contract_rows, preferred_element_type=jnp.float32
                    )
                    grad_normed = sum_normed(
                        lax.dot_general(
                            grad_projected,
                            qkv_mats[layer_index],
                            contract_cols,
                            preferred_element_type=jnp.float32,
                        )
                    )
                grad_input, grad_first, grad_second = norm_back(grad_normed)
                grad_rows = grad_rows + grad_input
                if layer_index == 0:
                    acc_gain[part_index] = acc_gain[part_index] + grad_first
                    acc_bias[part_index] = acc_bias[part_index] + grad_second
                else:
                    acc_scale[part_index] = acc_scale[part_index] + grad_first
                    acc_shift[part_index] = acc_shift[part_index] + grad_second
        grad_group = [grad_rows]
        frames_list.append(jnp.stack(out_group))
        grads_list.append(jnp.stack(grad_group))
    total_qkv, total_out, total_up, total_down = (
        lax.psum(jnp.stack(acc_qkv).astype(jnp.bfloat16), "dp").astype(jnp.float32),
        lax.psum(jnp.stack(acc_out).astype(jnp.bfloat16), "dp").astype(jnp.float32),
        lax.psum(jnp.stack(acc_up).astype(jnp.bfloat16), "dp").astype(jnp.float32),
        lax.psum(jnp.stack(acc_down).astype(jnp.bfloat16), "dp").astype(jnp.float32),
    )
    norm_totals = lax.psum(
        (jnp.stack(acc_gain), jnp.stack(acc_bias), jnp.stack(acc_scale), jnp.stack(acc_shift)),
        ("dp", "tensor"),
    )
    return (
        jnp.stack(frames_list),
        jnp.stack(grads_list),
        total_qkv.reshape(2, model_width, 3, -1),
        total_out,
        total_up,
        total_down,
        norm_totals[0],
        norm_totals[1],
        norm_totals[2],
        norm_totals[3],
    )


bf16,f32=jnp.bfloat16,jnp.float32
NT=(((1,),(1,)),((),()))
TN=(((0,),(0,)),((),()))

def _limits(lims_ref, start, rows, causal, axis):
    prefix, valid = lims_ref[0], lims_ref[1]
    shape=(rows,1) if axis==0 else (1,rows)
    pos=start+lax.broadcasted_iota(jnp.int32,shape,axis)
    if causal:
        return jnp.minimum(jnp.maximum(pos,prefix-1),valid-1)
    return jnp.zeros(shape,jnp.int32)+(valid-1)

def fwd_kernel(causal, bq, lims_ref, q_ref, k_ref, v_ref, o_ref, l_ref):
    length=q_ref.shape[0]
    lane=lax.broadcasted_iota(jnp.int32,(bq,128),1)
    def block(start, kk):
        q=q_ref[pl.ds(start,bq),:]*jnp.asarray(0.125,bf16)
        lim=_limits(lims_ref,start,bq,causal,0)
        outs=[];rows=[]
        for h in range(2):
            qm=jnp.where((lane<HEAD_DIM)==(h==0),q,jnp.zeros_like(q))
            s=lax.dot_general(qm,k_ref[0:kk,:],NT,preferred_element_type=f32)
            key=lax.broadcasted_iota(jnp.int32,(bq,kk),1)
            s=jnp.where(key<=lim,s,-1e9)
            m=jnp.max(s,axis=1,keepdims=True)
            e=jnp.exp(s-m)
            l=jnp.sum(e,axis=1,keepdims=True)
            o=jnp.dot(e.astype(bf16),v_ref[0:kk,:],preferred_element_type=f32)*(1.0/l)
            outs.append(o); rows.append(m+jnp.log(l))
        o_ref[pl.ds(start,bq),:]=jnp.where(lane<HEAD_DIM,outs[0],outs[1]).astype(bf16)
        both=jnp.where(lane<HEAD_DIM,rows[0],rows[1])
        bt=both.T
        l_ref[0,0:1,pl.ds(start,bq)]=bt[0:1,:]
        l_ref[0,1:2,pl.ds(start,bq)]=bt[HEAD_DIM:HEAD_DIM+1,:]
    nq=length//bq
    if causal:
        for i in range(nq): block(i*bq,(i+1)*bq)
    else:
        def body(i,c):
            block(pl.multiple_of(i*bq,bq),length); return c
        lax.fori_loop(0,nq,body,0)

def attn_fwd(qkv, lims, causal, bq=256):
    length=qkv.shape[0]; width=qkv.shape[1]//3; pairs=width//128
    spec=lambda off: pl.BlockSpec((length,128),lambda i,off=off:(0,off*pairs+i))
    return pl.pallas_call(partial(fwd_kernel,causal,bq),
        grid=(pairs,),
        in_specs=[pl.BlockSpec(memory_space=pltpu.SMEM),spec(0),spec(1),spec(2)],
        out_specs=[pl.BlockSpec((length,128),lambda i:(0,i)),pl.BlockSpec((1,2,length),lambda i:(i,0,0))],
        out_shape=[jax.ShapeDtypeStruct((length,width),bf16),jax.ShapeDtypeStruct((pairs,2,length),f32)],
        compiler_params=pltpu.CompilerParams(vmem_limit_bytes=48*2**20),
        cost_estimate=pl.CostEstimate(flops=pairs*2**20,bytes_accessed=length*width*8,transcendentals=0),
        name="attn_fwd_"+("causal" if causal else "full"),
    )(lims,qkv,qkv,qkv)

def bwd_kernel(causal,bq,lims_ref,q_ref,k_ref,v_ref,l_ref,do_ref,grad_ref,dk_acc,dv_acc):
    length=q_ref.shape[0]
    lane=lax.broadcasted_iota(jnp.int32,(bq,128),1)
    dk_acc[...]=jnp.zeros_like(dk_acc); dv_acc[...]=jnp.zeros_like(dv_acc)
    width=grad_ref.shape[1]//3
    at=[pl.multiple_of(part*width+pl.program_id(0)*128,128) for part in range(3)]
    def block(start,kk):
        q=q_ref[pl.ds(start,bq),:]*jnp.asarray(0.125,bf16)
        do=do_ref[pl.ds(start,bq),:]
        lim=_limits(lims_ref,start,bq,causal,1)
        dqs=[]
        for h in range(2):
            sel=(lane<HEAD_DIM)==(h==0)
            qm=jnp.where(sel,q,jnp.zeros_like(q)); dom=jnp.where(sel,do,jnp.zeros_like(do))
            s=lax.dot_general(k_ref[0:kk,:],qm,NT,preferred_element_type=f32)
            dp=lax.dot_general(v_ref[0:kk,:],dom,NT,preferred_element_type=f32)
            key=lax.broadcasted_iota(jnp.int32,(kk,bq),0)
            lrow=l_ref[0,h:h+1,pl.ds(start,bq)]
            p=jnp.where(key<=lim,jnp.exp(s-lrow),0.0)
            pd=p*dp
            D=jnp.sum(pd,axis=0,keepdims=True)
            ds=(pd-p*D).astype(bf16)
            dv_acc[0:kk,:]+=jnp.dot(p.astype(bf16),dom,preferred_element_type=f32)
            dk_acc[0:kk,:]+=jnp.dot(ds,qm,preferred_element_type=f32)
            dqs.append(lax.dot_general(ds,k_ref[0:kk,:],TN,preferred_element_type=f32))
        grad_ref[pl.ds(start,bq),pl.ds(at[0],128)]=(jnp.where(lane<HEAD_DIM,dqs[0],dqs[1])*0.125).astype(bf16)
    nq=length//bq
    if causal:
        for i in range(nq): block(i*bq,(i+1)*bq)
    else:
        def body(i,c):
            block(pl.multiple_of(i*bq,bq),length); return c
        lax.fori_loop(0,nq,body,0)
    grad_ref[:,pl.ds(at[1],128)]=dk_acc[...].astype(bf16)
    grad_ref[:,pl.ds(at[2],128)]=dv_acc[...].astype(bf16)

def attn_bwd(qkv,L,do,lims,causal,bq=256):
    length=qkv.shape[0]; width=qkv.shape[1]//3; pairs=width//128
    spec=lambda off: pl.BlockSpec((length,128),lambda i,off=off:(0,off*pairs+i))
    one=pl.BlockSpec((length,128),lambda i:(0,i))
    return pl.pallas_call(partial(bwd_kernel,causal,bq),
        grid=(pairs,),
        in_specs=[pl.BlockSpec(memory_space=pltpu.SMEM),spec(0),spec(1),spec(2),pl.BlockSpec((1,2,length),lambda i:(i,0,0)),one],
        out_specs=pl.BlockSpec((length,3*width),lambda i:(0,0)),
        out_shape=jax.ShapeDtypeStruct((length,3*width),bf16),
        scratch_shapes=[pltpu.VMEM((length,128),f32)]*2,
        compiler_params=pltpu.CompilerParams(vmem_limit_bytes=48*2**20),
        cost_estimate=pl.CostEstimate(flops=pairs*2**20,bytes_accessed=length*width*8,transcendentals=0),
        name="attn_bwd_"+("causal" if causal else "full"),
    )(lims,qkv,qkv,qkv,L,do)


def pin(*values):
    return lax.optimization_barrier(values)


def swap_tensor(block):
    return lax.ppermute(block, "tensor", [(0, 1), (1, 0)])


def swap_bit(block, bit, dp_size):
    return lax.ppermute(block, "dp", [(place, place ^ (1 << bit)) for place in range(dp_size)])


def in_order(flag, mine, other):
    first = jnp.where(flag == 0, mine, other)
    second = jnp.where(flag == 0, other, mine)
    return jnp.concatenate([first, second], axis=0)


def add_rounded(left, right):
    return (left.astype(f32) + right.astype(f32)).astype(bf16)


def norm_forward(rows, gain_row, shift_row):
    mean = jnp.mean(rows, axis=-1, keepdims=True)
    centered = rows - mean
    rate = lax.rsqrt(jnp.mean(centered * centered, axis=-1, keepdims=True) + norm_eps)
    normed = centered * rate * gain_row + shift_row
    return normed.astype(bf16), (rows, mean, rate)


def norm_backward(saved, grad_normed, gain_row):
    rows, mean, rate = saved
    unit = (rows - mean) * rate
    grad_unit = grad_normed * gain_row
    grad_rows = rate * (
        grad_unit
        - jnp.mean(grad_unit, axis=-1, keepdims=True)
        - unit * jnp.mean(grad_unit * unit, axis=-1, keepdims=True)
    )
    return grad_rows, jnp.sum(grad_normed * unit, axis=0), jnp.sum(grad_normed, axis=0)


def gelu_pair(hidden):
    square = hidden * hidden
    share = 0.5 + 0.5 * jnp.tanh(hidden * (0.7978845608 + (0.7978845608 * 0.044715) * square))
    value = hidden * share
    rate = 2.0 * 0.7978845608 + (6.0 * 0.7978845608 * 0.044715) * square
    slope = share + (value * rate) * (1.0 - share)
    return value.astype(bf16), slope.astype(bf16)


def dot_sum(pairs, dims):
    total = None
    for left, right in pairs:
        term = lax.dot_general(left, right, dims, preferred_element_type=f32)
        total = term if total is None else total + term
    return total


def dot_low(left, right, dims):
    return lax.dot_general(left, right, dims, preferred_element_type=f32).astype(bf16)


NN = (((1,), (0,)), ((), ()))
SPLIT_AXIS = {"up": 1, "down": 0}
PACK_WIDTH = 512


def quarter_of(kind, half, place):
    axis = SPLIT_AXIS[kind]
    width = half.shape[axis] // 2
    return lax.dynamic_slice_in_dim(half, place * width, width, axis)


def row_half(block, place):
    height = block.shape[0] // 2
    return lax.dynamic_slice_in_dim(block, place * height, height, 0)


def flat_kernel(in_ref, out_ref):
    width = in_ref.shape[3]
    for part in range(3):
        out_ref[:, part * width : (part + 1) * width] = in_ref[0, part]


def flat_qkv(stacked, layer):
    _, _, height, width = stacked.shape
    rows = height // 2
    return pl.pallas_call(
        flat_kernel,
        grid=(2,),
        in_specs=[pl.BlockSpec((1, 3, rows, width), lambda step: (layer, 0, step, 0))],
        out_specs=pl.BlockSpec((rows, 3 * width), lambda step: (step, 0)),
        out_shape=jax.ShapeDtypeStruct((height, 3 * width), bf16),
        cost_estimate=pl.CostEstimate(flops=0, bytes_accessed=12 * height * width, transcendentals=0),
        name="flat_qkv",
    )(stacked)


def pack_kernel(kinds, place_ref, *refs):
    out_ref = refs[-1]
    at = 0
    for kind, ref in zip(kinds, refs):
        if kind == "qkv":
            pieces = [ref[0, part] for part in range(3)]
        else:
            count = ref.shape[2] // PACK_WIDTH
            pieces = [ref[0, :, part * PACK_WIDTH : (part + 1) * PACK_WIDTH] for part in range(count)]
        for piece in pieces:
            out_ref[at : at + piece.shape[0], :] = piece
            at += piece.shape[0]


def pack_pieces(place, layer, dp_size, kinds, arrays):
    specs, total = [], 0
    for kind, array in zip(kinds, arrays):
        height, width = array.shape[-2:]
        rows = height // dp_size
        if kind == "qkv":
            specs.append(pl.BlockSpec((1, 3, rows, width), lambda step, at: (layer, 0, at[0], 0)))
            total += 3 * rows * width // PACK_WIDTH
        else:
            specs.append(pl.BlockSpec((1, rows, width), lambda step, at: (layer, at[0], 0)))
            total += rows * width // PACK_WIDTH
    return pl.pallas_call(
        partial(pack_kernel, kinds),
        grid_spec=pltpu.PrefetchScalarGridSpec(
            num_scalar_prefetch=1,
            grid=(1,),
            in_specs=specs,
            out_specs=pl.BlockSpec((total, PACK_WIDTH), lambda step, at: (0, 0)),
        ),
        out_shape=jax.ShapeDtypeStruct((total, PACK_WIDTH), bf16),
        cost_estimate=pl.CostEstimate(flops=0, bytes_accessed=4 * total * PACK_WIDTH, transcendentals=0),
        name="pack_pieces",
    )(place.reshape(1).astype(jnp.int32), *arrays)


def unpack_kernel(count, side_ref, in_ref, *refs):
    at = 0
    for ref in refs[-count:]:
        rows = ref.shape[0] // in_ref.shape[0]
        for part in range(ref.shape[1] // PACK_WIDTH):
            for block in range(in_ref.shape[0]):
                ref[block * rows : (block + 1) * rows, part * PACK_WIDTH : (part + 1) * PACK_WIDTH] = in_ref[
                    block, at : at + rows, :
                ]
            at += rows


def unpack_halves(side, gathered, shapes, bases=()):
    dp_size, total, _ = gathered.shape
    some = max(1, dp_size // 4)
    steps = dp_size // some
    out_specs, out_shape = [], []
    for index, (height, width) in enumerate(shapes):
        base = index - (len(shapes) - len(bases))
        block = (height // steps, width)
        if base < 0:
            out_specs.append(pl.BlockSpec(block, lambda step, side_ref: (step, 0)))
            out_shape.append(jax.ShapeDtypeStruct((height, width), bf16))
            continue
        if bases[base].shape[0] == height:
            out_specs.append(pl.BlockSpec(block, lambda step, side_ref: (step, 1 - side_ref[0])))
        else:
            out_specs.append(pl.BlockSpec(block, lambda step, side_ref: ((1 - side_ref[0]) * steps + step, 0)))
        out_shape.append(jax.ShapeDtypeStruct(bases[base].shape, bf16))
    return pl.pallas_call(
        partial(unpack_kernel, len(shapes)),
        grid_spec=pltpu.PrefetchScalarGridSpec(
            num_scalar_prefetch=1,
            grid=(steps,),
            in_specs=[pl.BlockSpec((some, total, PACK_WIDTH), lambda step, side_ref: (step, 0, 0))]
            + [pl.BlockSpec(memory_space=pl.ANY)] * len(bases),
            out_specs=out_specs,
        ),
        out_shape=out_shape,
        input_output_aliases={2 + base: len(shapes) - len(bases) + base for base in range(len(bases))},
        compiler_params=pltpu.CompilerParams(vmem_limit_bytes=32 * 2**20),
        cost_estimate=pl.CostEstimate(
            flops=0, bytes_accessed=4 * dp_size * total * PACK_WIDTH, transcendentals=0
        ),
        name="unpack_halves",
    )(side.reshape(1).astype(jnp.int32), gathered, *bases)


def fill_kernel(side_ref, up_ref, down_ref, up_out, down_out):
    up_out[...] = up_ref[0]
    down_out[...] = down_ref[0]


def fill_whole(side, w_up, w_down, layer):
    steps = 4
    _, height, width = w_up.shape
    up_rows, down_rows = height // steps, width // steps
    return pl.pallas_call(
        fill_kernel,
        grid_spec=pltpu.PrefetchScalarGridSpec(
            num_scalar_prefetch=1,
            grid=(steps,),
            in_specs=[
                pl.BlockSpec((1, up_rows, width), lambda step, side_ref: (layer, step, 0)),
                pl.BlockSpec((1, down_rows, height), lambda step, side_ref: (layer, step, 0)),
            ],
            out_specs=[
                pl.BlockSpec((up_rows, width), lambda step, side_ref: (step, side_ref[0])),
                pl.BlockSpec((down_rows, height), lambda step, side_ref: (side_ref[0] * steps + step, 0)),
            ],
        ),
        out_shape=[
            jax.ShapeDtypeStruct((height, 2 * width), bf16),
            jax.ShapeDtypeStruct((2 * width, height), bf16),
        ],
        compiler_params=pltpu.CompilerParams(vmem_limit_bytes=32 * 2**20),
        cost_estimate=pl.CostEstimate(flops=0, bytes_accessed=8 * height * width, transcendentals=0),
        name="fill_whole",
    )(side.reshape(1).astype(jnp.int32), w_up, w_down)


def place_joint_kernel(whole_ref, *refs):
    qkv_out, out_out = refs[-2:]
    for block in range(whole_ref.shape[0]):
        rows = qkv_out.shape[2] // whole_ref.shape[0]
        for part in range(3):
            qkv_out[0, part, block * rows : (block + 1) * rows, :] = whole_ref[
                block, part * rows : (part + 1) * rows, :
            ].astype(f32)
        at, rows = 3 * rows, out_out.shape[1] // whole_ref.shape[0]
        for part in range(out_out.shape[2] // PACK_WIDTH):
            out_out[0, block * rows : (block + 1) * rows, part * PACK_WIDTH : (part + 1) * PACK_WIDTH] = whole_ref[
                block, at + part * rows : at + (part + 1) * rows, :
            ].astype(f32)


def place_joint(whole, layer, qkv_shape, out_shape, bases):
    dp_size, total, _ = whole.shape
    some = dp_size // 4
    operands, in_specs, aliases = [whole], [pl.BlockSpec((some, total, PACK_WIDTH), lambda step: (step, 0, 0))], {}
    if bases is not None:
        operands += bases
        in_specs += [pl.BlockSpec(memory_space=pl.ANY)] * 2
        aliases = {1: 0, 2: 1}
    return pl.pallas_call(
        place_joint_kernel,
        grid=(4,),
        in_specs=in_specs,
        out_specs=[
            pl.BlockSpec((1, 3, qkv_shape[0] // 4, qkv_shape[1] // 3), lambda step: (layer, 0, step, 0)),
            pl.BlockSpec((1, out_shape[0] // 4, out_shape[1]), lambda step: (layer, step, 0)),
        ],
        out_shape=[
            jax.ShapeDtypeStruct((2, 3, qkv_shape[0], qkv_shape[1] // 3), f32),
            jax.ShapeDtypeStruct((2,) + tuple(out_shape), f32),
        ],
        input_output_aliases=aliases,
        compiler_params=pltpu.CompilerParams(vmem_limit_bytes=32 * 2**20),
        cost_estimate=pl.CostEstimate(flops=0, bytes_accessed=6 * dp_size * total * PACK_WIDTH, transcendentals=0),
        name="place_joint",
    )(*operands)


def place_pair_kernel(whole_ref, up_out, down_out):
    for block in range(whole_ref.shape[0]):
        rows = whole_ref.shape[2]
        down_out[0, block * rows : (block + 1) * rows, :] = whole_ref[block, 0].astype(f32)
        up_out[0, :, block * rows : (block + 1) * rows] = whole_ref[block, 1].astype(f32).T


def place_pair(whole, layer):
    dp_size, rows, columns = whole.shape
    rows = rows // 2
    some = dp_size // 4
    return pl.pallas_call(
        place_pair_kernel,
        grid=(4,),
        in_specs=[pl.BlockSpec((some, 2, rows, columns), lambda step: (step, 0, 0, 0))],
        out_specs=[
            pl.BlockSpec((1, columns, some * rows), lambda step: (layer, 0, step)),
            pl.BlockSpec((1, some * rows, columns), lambda step: (layer, step, 0)),
        ],
        out_shape=[
            jax.ShapeDtypeStruct((2, columns, dp_size * rows), f32),
            jax.ShapeDtypeStruct((2, dp_size * rows, columns), f32),
        ],
        compiler_params=pltpu.CompilerParams(vmem_limit_bytes=40 * 2**20),
        cost_estimate=pl.CostEstimate(flops=0, bytes_accessed=12 * dp_size * rows * columns, transcendentals=0),
        name="place_pair",
    )(whole.reshape(dp_size, 2, rows, columns))


def place_kernel(whole_ref, *refs):
    out_ref = refs[-1]
    out_ref[0] = whole_ref[...].reshape(-1, whole_ref.shape[-1]).astype(f32)


def place_quarters(kind, whole, which, layer, base):
    dp_size, rows, columns = whole.shape
    half, some, rows = dp_size // 2, dp_size // 4, rows // 2
    if kind == "down":
        out_spec = pl.BlockSpec((1, some * rows, columns), lambda step: (layer, step, 0))
    else:
        out_spec = pl.BlockSpec((1, some * rows, columns), lambda step: (layer, step % 2, step // 2))
    return pl.pallas_call(
        place_kernel,
        grid=(4,),
        in_specs=[
            pl.BlockSpec(
                (some, None, None, rows, columns), lambda step: (step % 2, step // 2, which, 0, 0)
            ),
            pl.BlockSpec(memory_space=pl.ANY),
        ],
        out_specs=out_spec,
        out_shape=jax.ShapeDtypeStruct(base.shape, f32),
        input_output_aliases={1: 0},
        compiler_params=pltpu.CompilerParams(vmem_limit_bytes=32 * 2**20),
        cost_estimate=pl.CostEstimate(flops=0, bytes_accessed=6 * dp_size * rows * columns, transcendentals=0),
        name="place_" + kind,
    )(whole.reshape(half, 2, 2, rows, columns), base)


def frame_kernel(side_ref, mine_ref, other_ref, out_ref):
    own = pl.program_id(0) == side_ref[0]
    out_ref[0, 0] = jnp.where(own, mine_ref[...], other_ref[...].astype(f32))


def place_frames(side, mine, other):
    height, width = mine.shape
    rows = height // 2
    spec = pl.BlockSpec((rows, width), lambda slot, step, side_ref: (step, 0))
    return pl.pallas_call(
        frame_kernel,
        grid_spec=pltpu.PrefetchScalarGridSpec(
            num_scalar_prefetch=1,
            grid=(2, 2),
            in_specs=[spec, spec],
            out_specs=pl.BlockSpec((1, 1, rows, width), lambda slot, step, side_ref: (slot, 0, step, 0)),
        ),
        out_shape=jax.ShapeDtypeStruct((2, 1, height, width), f32),
        name="place_frames",
    )(side.reshape(1).astype(jnp.int32), mine, other)


def take_axis(block, index):
    return lax.dynamic_index_in_dim(block, index, 1, keepdims=False)


def flat_rows(block):
    return block.reshape(-1, block.shape[-1])


def join_level(here, kept, arrived):
    first = jnp.where(here == 0, kept, arrived)
    second = jnp.where(here == 0, arrived, kept)
    joined = jnp.stack([first, second], axis=1)
    return joined.reshape((-1,) + joined.shape[2:])


class Chain:
    def __init__(self, place, dp_size, rows, columns, kind, gather):
        self.place, self.dp_size, self.kind, self.gather = place, dp_size, kind, gather
        self.rows, self.columns = rows, columns
        self.bit_count = dp_size.bit_length() - 1
        self.flight = []

    def bit(self, index):
        return (self.place >> index) & 1

    def swap(self, block, bit):
        return swap_bit(block, bit, self.dp_size)

    def pair(self, block):
        return block.reshape(-1, 2, self.rows, self.columns)

    def start(self, near, far, ours=None, own_far=None):
        self.near, self.ours = near, ours
        self.flight = [self.swap(far, 0)] + ([] if ours is None else [self.swap(own_far, 0)])
        self.state = "core"

    def start_rows(self, own, other):
        self.start_other(other)
        self.add_own(own)

    def start_other(self, other):
        split, core = self.pair(other), self.bit(0)
        self.start(flat_rows(take_axis(split, core)), flat_rows(take_axis(split, 1 - core)))

    def add_own(self, own):
        split, core = self.pair(own), self.bit(0)
        self.flight = self.flight + [self.swap(flat_rows(take_axis(split, 1 - core)), 0)]
        self.ours = flat_rows(take_axis(split, core))

    def halves(self, block, bit):
        split, here = self.pair(block), self.bit(bit)
        return flat_rows(take_axis(split, here)), flat_rows(take_axis(split, 1 - here))

    def settle(self, arrived):
        self.near_here, self.near_away = self.halves(add_rounded(self.near, arrived[0]), 1)
        if self.ours is not None:
            self.kept_here, self.kept_away = self.halves(add_rounded(self.ours, arrived[1]), 1)
        self.flight, self.state = [], "ready"

    def launch(self):
        self.flight = [swap_tensor(self.near_away) if self.kind == "x" else self.swap(self.near_away, 1)]
        self.state = "first"

    def second(self, arrived):
        if len(arrived) > 1:
            self.kept_here, self.kept_away = self.halves(add_rounded(self.ours, arrived[1]), 1)
        if self.kind == "x":
            self.kept_away = add_rounded(self.kept_away, arrived[0])
        else:
            self.near_here = add_rounded(self.near_here, arrived[0])
        self.flight = [swap_tensor(self.near_here), self.swap(self.kept_away, 1)]
        self.state = "second"

    def next_bit(self, total, index):
        if index == self.bit_count:
            self.kept, self.state = total, "gather"
            if self.gather == "native":
                self.flight = [lax.all_gather(total, "dp", axis=0, tiled=False)]
                return
            if self.gather is None:
                self.flight, self.state = [], "done"
                return
            self.kept, self.level = total[None], index - 1
            self.flight = [self.swap(self.kept, self.level)]
            return
        self.kept, away = self.halves(total, index)
        self.flight, self.index, self.state = [self.swap(away, index)], index, "bits"

    def advance(self, arrived, hold=False):
        if self.state == "done":
            return
        if self.state == "core":
            self.settle(arrived)
            if not hold:
                self.launch()
        elif self.state == "ready":
            self.launch()
        elif self.state == "first":
            self.second(arrived)
        elif self.state == "second":
            total = self.kept_here.astype(f32) + arrived[0].astype(f32) + arrived[1].astype(f32)
            self.next_bit(total.astype(bf16), 2)
        elif self.state == "bits":
            self.next_bit(add_rounded(self.kept, arrived[0]), self.index + 1)
        elif self.gather == "native":
            self.whole, self.flight, self.state = arrived[0], [], "done"
        else:
            self.kept = join_level(self.bit(self.level), self.kept, arrived[0])
            self.level -= 1
            if self.level < 0:
                self.whole, self.flight, self.state = self.kept, [], "done"
            else:
                self.flight = [self.swap(self.kept, self.level)]


class Scatter:
    def __init__(self, block):
        self.flight = [lax.psum_scatter(block, ("tensor", "dp"), scatter_dimension=0, tiled=True)]
        self.state = "sum"

    def advance(self, arrived):
        if self.state == "sum":
            self.flight, self.state = [lax.all_gather(arrived[0], "dp", axis=0, tiled=False)], "gather"
        elif self.state == "gather":
            self.whole, self.flight, self.state = arrived[0], [], "done"


class Gather:
    def __init__(self, qkv, out, width, native):
        assert qkv.state == "done" and out.state == "done"
        pieces = []
        for block in (qkv.kept, out.kept):
            for at in range(0, block.shape[1], width):
                pieces.append(lax.slice_in_dim(block, at, at + width, axis=1))
        self.kept = jnp.concatenate(pieces, axis=0)
        self.native, self.bit, self.swap = native, qkv.bit, qkv.swap
        self.state = "going"
        if native:
            self.flight = [lax.all_gather(self.kept, "dp", axis=0, tiled=False)]
        else:
            self.kept, self.level = self.kept[None], qkv.bit_count - 1
            self.flight = [self.swap(self.kept, self.level)]

    def advance(self, arrived):
        if self.state == "done":
            return
        if self.native:
            self.whole, self.flight, self.state = arrived[0], [], "done"
            return
        self.kept = join_level(self.bit(self.level), self.kept, arrived[0])
        self.level -= 1
        if self.level < 0:
            self.whole, self.flight, self.state = self.kept, [], "done"
        else:
            self.flight = [self.swap(self.kept, self.level)]


class Spread:
    def __init__(self, block, dp_size):
        self.block, self.dp_size = block, dp_size
        self.bits = list(range(dp_size.bit_length() - 1))
        self.flight = [swap_tensor(block)]

    def advance(self, arrived):
        if not arrived:
            return
        self.block = self.block + arrived[0]
        self.flight = [swap_bit(self.block, self.bits.pop(0), self.dp_size)] if self.bits else []


def move(state, *chains, hold=()):
    everyone = chains + tuple(hold)
    state, flights = pin(state, [one.flight for one in everyone])
    for one, flight in zip(everyone, flights):
        if one in hold:
            one.advance(flight, hold=True)
        else:
            one.advance(flight)
    return state


def paired_device(
    dp_size,
    frames_in,
    phone_len,
    frame_len,
    section,
    norm_gain,
    norm_bias,
    ada_scale,
    ada_shift,
    w_qkv,
    w_out,
    w_up,
    w_down,
    out_grad,
):
    model_width = frames_in.shape[3]
    section_count = ada_scale.shape[1]
    side = lax.axis_index("tensor")
    place = lax.axis_index("dp")
    core, near_row = place & 1, (place >> 1) & 1

    def away_rows(halves):
        return lax.dynamic_index_in_dim(halves[:, 0], 1 - side, 0, keepdims=False)

    def whole_rows(halves, other):
        mine = lax.dynamic_index_in_dim(halves[:, 0], side, 0, keepdims=False)
        return in_order(side, mine, other)

    prefix = lax.dynamic_index_in_dim(phone_len[:, 0], side, 0, keepdims=False)
    frames = lax.dynamic_index_in_dim(frame_len[:, 0], side, 0, keepdims=False)
    chosen = lax.dynamic_index_in_dim(section[:, 0], side, 0, keepdims=False)
    limits = jnp.stack([prefix, prefix + frames]).astype(jnp.int32)
    picker = (lax.iota(jnp.int32, section_count) == chosen).astype(f32)[:, None]

    gains = [
        [norm_gain[0], norm_gain[1]],
        [jnp.sum(picker * ada_scale[part], axis=0) for part in range(2)],
    ]
    shifts = [
        [norm_bias[0], norm_bias[1]],
        [jnp.sum(picker * ada_shift[part], axis=0) for part in range(2)],
    ]

    stacked = w_qkv.transpose(0, 2, 1, 3)
    arrays = {"qkv": stacked, "out": w_out, "up": w_up, "down": w_down}
    flat_shape = {
        "qkv": (model_width, 3 * stacked.shape[3]),
        "out": w_out.shape[1:],
        "up": w_up.shape[1:],
        "down": w_down.shape[1:],
    }

    def packed(layer, kinds):
        return pack_pieces(place, layer, dp_size, kinds, [arrays[kind] for kind in kinds])

    def gathered(arrived):
        return lax.all_gather(arrived, "dp", axis=0, tiled=False)

    def unpacked(whole, kinds, bases=()):
        return dict(zip(kinds, unpack_halves(side, whole, [flat_shape[kind] for kind in kinds], bases)))

    attn_kinds, all_kinds = ("qkv", "out"), ("qkv", "out", "up", "down")
    first_pack = swap_tensor(packed(0, attn_kinds))
    other_rows = swap_tensor(away_rows(frames_in))
    first_whole = gathered(first_pack)
    second_send = packed(1, all_kinds)
    up_send = row_half(quarter_of("up", w_up[0], core), near_row)
    down_send = row_half(quarter_of("down", w_down[0], core), near_row)
    own_qkv = [flat_qkv(stacked, layer) for layer in range(2)]
    filled = fill_whole(side, w_up, w_down, 1)
    other_rows, second_send, up_send, down_send, own_qkv, filled = pin(
        other_rows, second_send, up_send, down_send, own_qkv, filled
    )
    second_pack = swap_tensor(second_send)
    rows = whole_rows(frames_in, other_rows).astype(f32)
    normed, norm_kept = norm_forward(rows, gains[0][0], shifts[0][0])
    mine = dot_low(normed, own_qkv[0], NN)
    mine, second_pack, up_send, down_send = pin(mine, second_pack, up_send, down_send)
    second_whole = gathered(second_pack)
    up_piece = swap_tensor(up_send)
    mix_mine = attn_fwd(mine, limits, True, 512)
    mix_mine, up_piece, down_send = pin(mix_mine, up_piece, down_send)
    down_piece = swap_tensor(down_send)
    up_there = swap_bit(up_piece, 1, dp_size)
    first = unpacked(first_whole, attn_kinds)
    theirs = dot_low(normed, first["qkv"], NN)
    mix_theirs = attn_fwd(theirs, limits, True, 512)
    mix_theirs, up_there, down_piece = pin(mix_theirs, up_there, down_piece)
    up_near = in_order(near_row, up_piece, up_there)
    up_far = swap_bit(up_near, 0, dp_size)
    down_there = swap_bit(down_piece, 1, dp_size)
    kept = [(normed, norm_kept, [mine, theirs], [mix_mine, mix_theirs])]
    rows = rows + dot_sum([(mix_mine[0], w_out[0]), (mix_theirs[0], first["out"])], NN)
    normed, norm_kept = norm_forward(rows, gains[0][1], shifts[0][1])
    pair_own = gelu_pair(jnp.dot(normed, w_up[0], preferred_element_type=f32))
    pair_own, up_far, normed, norm_kept, rows = pin(pair_own, up_far, normed, norm_kept, rows)
    pair_near = gelu_pair(jnp.dot(normed, up_near, preferred_element_type=f32))
    pair_far = gelu_pair(jnp.dot(normed, up_far, preferred_element_type=f32))
    rows = rows + dot_sum([(pair_own[0], w_down[0])], NN)
    rows, pair_near, pair_far, down_there = pin(rows, pair_near, pair_far, down_there)
    down_near = in_order(near_row, down_piece, down_there)
    down_far = swap_bit(down_near, 0, dp_size)
    grad_send = away_rows(out_grad)
    rows = rows + dot_sum([(pair_near[0], down_near)], NN)
    rows, grad_send, down_far = pin(rows, grad_send, down_far)
    grad_other = swap_tensor(grad_send)
    rows = rows + dot_sum([(pair_far[0], down_far)], NN)
    kept.append((normed, norm_kept, [pair_own, pair_near, pair_far]))

    normed, norm_kept = norm_forward(rows, gains[1][0], shifts[1][0])
    mine = dot_low(normed, own_qkv[1], NN)
    mix_mine = attn_fwd(mine, limits, False, 512)
    mix_mine, second_whole = pin(mix_mine, second_whole)
    second = unpacked(second_whole, all_kinds, filled)
    weights = [
        {
            "qkv": [own_qkv[0], first["qkv"]],
            "out": [w_out[0], first["out"]],
            "up": [w_up[0], up_near, up_far],
            "down": [w_down[0], down_near, down_far],
        },
        {
            "qkv": [own_qkv[1], second["qkv"]],
            "out": [w_out[1], second["out"]],
            "up": [second["up"]],
            "down": [second["down"]],
        },
    ]
    theirs = dot_low(normed, second["qkv"], NN)
    mix_theirs = attn_fwd(theirs, limits, False, 512)
    mixed = [mix_mine, mix_theirs]
    kept.append((normed, norm_kept, [mine, theirs], mixed))
    rows = rows + dot_sum([(mix[0], part) for mix, part in zip(mixed, weights[1]["out"])], NN)
    normed, norm_kept = norm_forward(rows, gains[1][1], shifts[1][1])
    pairs = [gelu_pair(jnp.dot(normed, part, preferred_element_type=f32)) for part in weights[1]["up"]]
    pairs, rows, normed, norm_kept = pin(pairs, rows, normed, norm_kept)
    rows = rows + dot_sum([(pair[0], part) for pair, part in zip(pairs, weights[1]["down"])], NN)
    kept.append((normed, norm_kept, pairs))
    rows, grad_other = pin(rows, grad_other)

    def halves_of(block):
        height = block.shape[0] // 2
        mine = lax.dynamic_slice_in_dim(block, side * height, height, 0)
        away = lax.dynamic_slice_in_dim(block, (1 - side) * height, height, 0)
        return mine, away.astype(bf16)

    out_mine, out_away = halves_of(rows)

    norm_sums = [[None, None], [None, None]]
    grad_rows = whole_rows(out_grad, grad_other).astype(f32)
    def chain(kind, first, gather, split="rows"):
        height, width = flat_shape[kind]
        if split == "core":
            count = dp_size // 2
            height, width = (height, width // 2) if kind == "up" else (height // 2, width)
        else:
            count = dp_size
        return Chain(place, dp_size, height // count, width, first, gather)

    def start_quarters(one, kind, parts):
        own, near, far = parts
        one.start(near, far, quarter_of(kind, own, core), quarter_of(kind, own, 1 - core))

    def hidden_grads(layer, low):
        pairs = kept[2 * layer + 1][2]
        return [
            (
                lax.dot_general(low, part, NT, preferred_element_type=f32) * pair[1].astype(f32)
            ).astype(bf16)
            for pair, part in zip(pairs, weights[layer]["down"])
        ]

    def down_grads(layer, low):
        return [dot_low(pair[0], low, TN) for pair in kept[2 * layer + 1][2]]

    def up_grads(layer, hidden):
        return [dot_low(kept[2 * layer + 1][0], part, TN) for part in hidden]

    def out_grads(layer, low):
        return [dot_low(mix[0], low, TN) for mix in kept[2 * layer][3]]

    def mixed_grads(layer, low):
        return [dot_low(low, part, NT) for part in weights[layer]["out"]]

    def attention_grad(layer, part, grad_mix):
        _, _, projected, mixed = kept[2 * layer]
        rows = 256 if layer == 0 else 512
        return attn_bwd(projected[part], mixed[part][1], grad_mix, limits, layer == 0, rows)

    def norm_step(layer, part, grad_rows, grad_normed):
        added, grad_gain, grad_shift = norm_backward(
            kept[2 * layer + part][1], grad_normed, gains[layer][part]
        )
        norm_sums[layer][part] = (grad_gain, grad_shift)
        return grad_rows + added

    out1, qkv1 = chain("out", "x", None), chain("qkv", "y", None)
    down0, up0 = chain("down", "x", None, "core"), chain("up", "y", None, "core")
    out0, qkv0 = chain("out", "x", None), chain("qkv", "y", None)

    low = grad_rows.astype(bf16)
    (down_part,) = down_grads(1, low)
    hidden = hidden_grads(1, low)
    down_part, hidden, grad_rows = pin(down_part, hidden, grad_rows)
    up_part = dot_low(hidden[0], kept[3][0], TN)
    both_parts = jnp.concatenate(
        [part.reshape(2 * dp_size, -1, model_width) for part in (down_part, up_part)], axis=1
    )
    both_parts, hidden, grad_rows = pin(both_parts, hidden, grad_rows)
    pair1 = Scatter(flat_rows(both_parts))
    grad_normed = dot_sum(list(zip(hidden, weights[1]["up"])), NT)
    grad_rows = norm_step(1, 1, grad_rows, grad_normed)
    low = grad_rows.astype(bf16)
    out_parts = out_grads(1, low)
    mine, theirs = mixed_grads(1, low)
    theirs = attention_grad(1, 1, theirs)
    out_parts, mine, theirs, grad_rows = pin(out_parts, mine, theirs, grad_rows)
    out1.start_rows(*out_parts)
    mine = attention_grad(1, 0, mine)
    parts = [dot_low(kept[2][0], part, TN) for part in (mine, theirs)]
    parts, mine, theirs, grad_rows = move((parts, mine, theirs, grad_rows), hold=[out1])
    qkv1.start_rows(*parts)
    out_there = swap_tensor(out_away)
    grad_normed = dot_sum(list(zip((mine, theirs), weights[1]["qkv"])), NT)
    grad_rows = norm_step(1, 0, grad_rows, grad_normed)
    low = grad_rows.astype(bf16)
    parts = down_grads(0, low)
    parts, low, grad_rows = move((parts, low, grad_rows), out1, qkv1)
    start_quarters(down0, "down", parts)
    hidden = hidden_grads(0, low)
    hidden, grad_rows, out_there = move((hidden, grad_rows, out_there), qkv1, out1, hold=[down0])
    parts = up_grads(0, hidden)
    grad_normed = dot_sum(list(zip(hidden, weights[0]["up"])), NT)
    parts, grad_normed, grad_rows = move((parts, grad_normed, grad_rows), qkv1, out1, down0, pair1)
    start_quarters(up0, "up", parts)
    grad_rows = norm_step(0, 1, grad_rows, grad_normed)
    low = grad_rows.astype(bf16)
    out_parts = out_grads(0, low)
    mine, theirs = mixed_grads(0, low)
    out_parts, mine, theirs, grad_rows = move((out_parts, mine, theirs, grad_rows), up0, qkv1, out1)
    out0.start_rows(*out_parts)
    theirs = attention_grad(0, 1, theirs)
    part_theirs = dot_low(kept[0][0], theirs, TN)
    part_theirs, mine, theirs, grad_rows = move(
        (part_theirs, mine, theirs, grad_rows), down0, up0, qkv1, out1, hold=[out0]
    )
    joint1 = Gather(qkv1, out1, PACK_WIDTH, True)
    qkv0.start_other(part_theirs)
    mine = attention_grad(0, 0, mine)
    part_mine = dot_low(kept[0][0], mine, TN)
    part_mine, mine, theirs, grad_rows = move(
        (part_mine, mine, theirs, grad_rows), down0, up0, out0, qkv0
    )
    qkv0.add_own(part_mine)
    grad_normed = dot_sum([(mine, weights[0]["qkv"][0]), (theirs, weights[0]["qkv"][1])], NT)
    grad_rows = norm_step(0, 0, grad_rows, grad_normed)
    grad_mine, grad_away = halves_of(grad_rows)
    late = Spread(
        jnp.concatenate(
            [jnp.stack([norm_sums[0][part][which] for which in range(2) for part in range(2)])]
            + [picker * norm_sums[1][part][which][None] for which in range(2) for part in range(2)]
        ),
        dp_size,
    )
    frames_out = place_frames(side, out_mine, out_there)
    grad_away, grad_mine, frames_out = move((grad_away, grad_mine, frames_out), qkv0, up0, down0, out0, pair1, late)
    grad_away, grad_mine = move((grad_away, grad_mine), qkv0, up0, down0, out0, late)
    pair0 = Gather(down0, up0, model_width, True)
    grad_there = swap_tensor(grad_away)
    bases = dict(zip(("up", "down"), place_pair(pair1.whole, 1)))
    bases, grad_mine, grad_there = move((bases, grad_mine, grad_there), qkv0, out0, late)
    (grad_mine,) = move((grad_mine,), qkv0, out0, late, joint1)
    joint0 = Gather(qkv0, out0, PACK_WIDTH, False)
    shapes = (flat_shape["qkv"], flat_shape["out"])
    joint_bases = place_joint(joint1.whole, 1, *shapes, None)
    frames_grad = place_frames(side, grad_mine, grad_there)
    joint_bases, frames_grad = move((joint_bases, frames_grad), joint0, late)
    joint_bases, frames_grad = move((joint_bases, frames_grad), joint0, late)
    (joint_bases,) = move((joint_bases,), joint0, pair0)
    grad_up = place_quarters("up", pair0.whole, 1, 0, bases["up"])
    grad_down = place_quarters("down", pair0.whole, 0, 0, bases["down"])
    while joint0.flight:
        joint0.advance(joint0.flight)
    while late.flight:
        late.advance(late.flight)
    grad_qkv, grad_out = place_joint(joint0.whole, 0, *shapes, list(joint_bases))

    gain_rows = late.block[4:].reshape(4, section_count, model_width)
    return (
        frames_out,
        frames_grad,
        grad_qkv.transpose(0, 2, 1, 3),
        grad_out,
        grad_up,
        grad_down,
        late.block[0:2],
        late.block[2:4],
        gain_rows[0:2],
        gain_rows[2:4],
    )


def per_device(dp_size, tensor_size, *arrays):
    micro_count, local_seqs = arrays[0].shape[:2]
    paired = micro_count == 2 and tensor_size == 2 and local_seqs == 1
    if paired and dp_size >= 4 and dp_size & (dp_size - 1) == 0:
        return paired_device(dp_size, *arrays)
    return grouped_device(*arrays)


def solution(mesh):
    return jax.shard_map(
        partial(per_device, mesh.shape["dp"], mesh.shape["tensor"]),
        mesh=mesh,
        in_specs=(
            P(None, "dp", "tensor", None),
            P(None, "dp"),
            P(None, "dp"),
            P(None, "dp"),
            P(),
            P(),
            P(),
            P(),
            P(None, None, None, "tensor"),
            P(None, "tensor", None),
            P(None, None, "tensor"),
            P(None, "tensor", None),
            P(None, "dp", "tensor", None),
        ),
        out_specs=(
            P(None, "dp", "tensor", None),
            P(None, "dp", "tensor", None),
            P(None, None, None, "tensor"),
            P(None, "tensor", None),
            P(None, None, "tensor"),
            P(None, "tensor", None),
            P(),
            P(),
            P(),
            P(),
        ),
        check_vma=False,
    )
```

```python
from functools import partial

import jax
import jax.numpy as jnp
from jax import lax
from jax.experimental import pallas as pl
from jax.experimental.pallas import tpu as pltpu
from jax.sharding import PartitionSpec as P

HEAD_DIM = 64


norm_eps = 1e-05
masked_score = -1000000000.0
contract_rows = (((0,), (0,)), ((), ()))
contract_cols = (((1,), (1,)), ((), ()))


def plain_norm(inputs):
    centered = inputs - jnp.mean(inputs, axis=-1, keepdims=True)
    variance = jnp.mean(centered * centered, axis=-1, keepdims=True)
    return centered * lax.rsqrt(variance + norm_eps)


def fixed_norm(inputs, gain_row, shift_row):
    return plain_norm(inputs) * gain_row + shift_row


def section_norm(inputs, scale_table, shift_table, picker):
    scale_row = jnp.dot(
        picker, scale_table, precision=lax.Precision.HIGHEST, preferred_element_type=jnp.float32
    )
    shift_row = jnp.dot(
        picker, shift_table, precision=lax.Precision.HIGHEST, preferred_element_type=jnp.float32
    )
    return plain_norm(inputs) * scale_row + shift_row


def gather_normed(normed_low):
    return lax.all_gather(normed_low, "tensor", axis=0, tiled=True)


def gather_again(normed_low):
    return lax.all_gather(normed_low, "tensor", axis=0, tiled=True)


def sum_branch(branch_part):
    return lax.psum_scatter(
        branch_part.astype(jnp.bfloat16), "tensor", scatter_dimension=0, tiled=True
    ).astype(jnp.float32)


def gather_grad(grad_low):
    return lax.all_gather(grad_low, "tensor", axis=0, tiled=True)


def sum_normed(grad_part):
    return lax.psum_scatter(
        grad_part.astype(jnp.bfloat16), "tensor", scatter_dimension=0, tiled=True
    ).astype(jnp.float32)


def key_allowed(query_pos, key_pos, prefix, valid_count, causal):
    allowed = key_pos[None, :] < valid_count
    if causal:
        allowed = allowed & ((key_pos[None, :] < prefix) | (key_pos[None, :] <= query_pos[:, None]))
    return allowed


def split_heads(projected):
    length = projected.shape[0]
    head_width = projected.shape[1] // 3
    head_count = head_width // HEAD_DIM
    query_rows = projected[:, :head_width].reshape(length, head_count, HEAD_DIM)
    key_rows = projected[:, head_width : 2 * head_width].reshape(length, head_count, HEAD_DIM)
    value_rows = projected[:, 2 * head_width :].reshape(length, head_count, HEAD_DIM)
    return (query_rows, key_rows, value_rows)


def block_scores(query_block, key_rows, block_start, prefix, valid_count, causal):
    block_rows = query_block.shape[0]
    length = key_rows.shape[0]
    scores = jnp.einsum(
        "qhd,khd->hqk", query_block, key_rows, preferred_element_type=jnp.float32
    ) * HEAD_DIM ** (-0.5)
    query_pos = block_start + lax.iota(jnp.int32, block_rows)
    key_pos = lax.iota(jnp.int32, length)
    allowed = key_allowed(query_pos, key_pos, prefix, valid_count, causal)
    return jnp.where(allowed[None], scores, masked_score)


def attend_forward(projected, prefix, valid_count, causal, block_rows):
    length = projected.shape[0]
    head_width = projected.shape[1] // 3
    query_rows, key_rows, value_rows = split_heads(projected)

    def one_block(block_start):
        query_block = lax.dynamic_slice_in_dim(query_rows, block_start, block_rows, 0)
        scores = block_scores(query_block, key_rows, block_start, prefix, valid_count, causal)
        highest = jnp.max(scores, axis=-1, keepdims=True)
        row_total = jnp.sum(jnp.exp(scores - highest), axis=-1, keepdims=True)
        log_total = highest + jnp.log(row_total)
        shares = jnp.exp(scores - log_total).astype(jnp.bfloat16)
        mixture = jnp.einsum("hqk,khd->qhd", shares, value_rows, preferred_element_type=jnp.float32)
        return (mixture.astype(jnp.bfloat16), log_total)

    starts = lax.iota(jnp.int32, length // block_rows) * block_rows
    mixture, log_totals = lax.map(one_block, starts)
    return (mixture.reshape(length, head_width), log_totals)


def attend_backward(projected, log_totals, grad_mixture, prefix, valid_count, causal, block_rows):
    length = projected.shape[0]
    head_width = projected.shape[1] // 3
    query_rows, key_rows, value_rows = split_heads(projected)
    grad_rows = grad_mixture.reshape(query_rows.shape)
    score_scale = HEAD_DIM ** (-0.5)

    def one_block(grad_state, block_item):
        block_start, log_total = block_item
        grad_key, grad_value = grad_state
        query_block = lax.dynamic_slice_in_dim(query_rows, block_start, block_rows, 0)
        grad_block = lax.dynamic_slice_in_dim(grad_rows, block_start, block_rows, 0)
        scores = block_scores(query_block, key_rows, block_start, prefix, valid_count, causal)
        shares = jnp.exp(scores - log_total)
        shares_low = shares.astype(jnp.bfloat16)
        grad_shares = jnp.einsum(
            "qhd,khd->hqk", grad_block, value_rows, preferred_element_type=jnp.float32
        )
        inner_sum = jnp.sum(shares * grad_shares, axis=-1, keepdims=True)
        grad_scores = (shares * (grad_shares - inner_sum)).astype(jnp.bfloat16)
        grad_query = (
            jnp.einsum("hqk,khd->qhd", grad_scores, key_rows, preferred_element_type=jnp.float32)
            * score_scale
        )
        grad_key = (
            grad_key
            + jnp.einsum(
                "hqk,qhd->khd", grad_scores, query_block, preferred_element_type=jnp.float32
            )
            * score_scale
        )
        grad_value = grad_value + jnp.einsum(
            "hqk,qhd->khd", shares_low, grad_block, preferred_element_type=jnp.float32
        )
        return ((grad_key, grad_value), grad_query)

    starts = lax.iota(jnp.int32, length // block_rows) * block_rows
    zero_rows = jnp.zeros(query_rows.shape, jnp.float32)
    grad_state, grad_query = lax.scan(one_block, (zero_rows, zero_rows), (starts, log_totals))
    grad_key, grad_value = grad_state
    joined = jnp.concatenate(
        [
            grad_query.reshape(length, head_width),
            grad_key.reshape(length, head_width),
            grad_value.reshape(length, head_width),
        ],
        axis=1,
    )
    return joined.astype(jnp.bfloat16)


def grouped_device(
    frames_in,
    phone_len,
    frame_len,
    section,
    norm_gain,
    norm_bias,
    ada_scale,
    ada_shift,
    w_qkv,
    w_out,
    w_up,
    w_down,
    out_grad,
):
    micro_count, local_seqs, local_rows, model_width = frames_in.shape
    seq_length = local_rows * lax.axis_size("tensor")
    block_rows = min(512, seq_length)
    section_count = ada_scale.shape[1]
    qkv_mats = [w_qkv[layer_index].reshape(model_width, -1) for layer_index in range(2)]
    acc_qkv = [jnp.zeros(qkv_mats[layer_index].shape, jnp.float32) for layer_index in range(2)]
    acc_out = [jnp.zeros(w_out.shape[1:], jnp.float32) for layer_index in range(2)]
    acc_up = [jnp.zeros(w_up.shape[1:], jnp.float32) for layer_index in range(2)]
    acc_down = [jnp.zeros(w_down.shape[1:], jnp.float32) for layer_index in range(2)]
    acc_gain = [jnp.zeros((model_width,), jnp.float32) for part_index in range(2)]
    acc_bias = [jnp.zeros((model_width,), jnp.float32) for part_index in range(2)]
    acc_scale = [jnp.zeros((section_count, model_width), jnp.float32) for part_index in range(2)]
    acc_shift = [jnp.zeros((section_count, model_width), jnp.float32) for part_index in range(2)]
    frames_list = []
    grads_list = []
    for micro_index in range(micro_count):
        prefix = phone_len[micro_index, 0]
        valid_count = prefix + frame_len[micro_index, 0]
        picker = (lax.iota(jnp.int32, section_count) == section[micro_index, 0]).astype(
            jnp.float32
        )[None, :]
        residual = frames_in[micro_index, 0].astype(jnp.float32)
        stored = []
        for layer_index in range(2):
            for part_index in range(2):
                if layer_index == 0:
                    normed, norm_back = jax.vjp(
                        fixed_norm, residual, norm_gain[part_index], norm_bias[part_index]
                    )
                else:
                    normed, norm_back = jax.vjp(
                        partial(section_norm, picker=picker),
                        residual,
                        ada_scale[part_index],
                        ada_shift[part_index],
                    )
                normed_low = normed.astype(jnp.bfloat16)
                gathered = gather_normed(normed_low)
                if part_index == 0:
                    projected = jnp.dot(
                        gathered, qkv_mats[layer_index], preferred_element_type=jnp.float32
                    ).astype(jnp.bfloat16)
                    mixture, log_totals = attend_forward(
                        projected, prefix, valid_count, layer_index == 0, block_rows
                    )
                    branch = sum_branch(
                        jnp.dot(mixture, w_out[layer_index], preferred_element_type=jnp.float32)
                    )
                    saved_state = (projected, log_totals, mixture)
                else:
                    hidden = jnp.dot(
                        gathered, w_up[layer_index], preferred_element_type=jnp.float32
                    )
                    active = jax.nn.gelu(hidden, approximate=True).astype(jnp.bfloat16)
                    branch = sum_branch(
                        jnp.dot(active, w_down[layer_index], preferred_element_type=jnp.float32)
                    )
                    saved_state = (hidden, active)
                kept_rows = normed_low
                stored.append((norm_back, kept_rows, saved_state))
                residual = residual + branch
        out_group = [residual]
        grad_rows = out_grad[micro_index, 0].astype(jnp.float32)
        for layer_index in (1, 0):
            for part_index in (1, 0):
                norm_back, kept_rows, saved_state = stored[2 * layer_index + part_index]
                gathered = gather_again(kept_rows)
                grad_whole = gather_grad(grad_rows.astype(jnp.bfloat16))
                if part_index == 1:
                    hidden, active = saved_state
                    acc_down[layer_index] = acc_down[layer_index] + lax.dot_general(
                        active, grad_whole, contract_rows, preferred_element_type=jnp.float32
                    )
                    grad_active = lax.dot_general(
                        grad_whole,
                        w_down[layer_index],
                        contract_cols,
                        preferred_element_type=jnp.float32,
                    )
                    gelu_value, gelu_back = jax.vjp(partial(jax.nn.gelu, approximate=True), hidden)
                    grad_hidden = gelu_back(grad_active)[0].astype(jnp.bfloat16)
                    acc_up[layer_index] = acc_up[layer_index] + lax.dot_general(
                        gathered, grad_hidden, contract_rows, preferred_element_type=jnp.float32
                    )
                    grad_normed = sum_normed(
                        lax.dot_general(
                            grad_hidden,
                            w_up[layer_index],
                            contract_cols,
                            preferred_element_type=jnp.float32,
                        )
                    )
                else:
                    projected, log_totals, mixture = saved_state
                    acc_out[layer_index] = acc_out[layer_index] + lax.dot_general(
                        mixture, grad_whole, contract_rows, preferred_element_type=jnp.float32
                    )
                    grad_mixture = lax.dot_general(
                        grad_whole,
                        w_out[layer_index],
                        contract_cols,
                        preferred_element_type=jnp.float32,
                    ).astype(jnp.bfloat16)
                    grad_projected = attend_backward(
                        projected,
                        log_totals,
                        grad_mixture,
                        prefix,
                        valid_count,
                        layer_index == 0,
                        block_rows,
                    )
                    acc_qkv[layer_index] = acc_qkv[layer_index] + lax.dot_general(
                        gathered, grad_projected, contract_rows, preferred_element_type=jnp.float32
                    )
                    grad_normed = sum_normed(
                        lax.dot_general(
                            grad_projected,
                            qkv_mats[layer_index],
                            contract_cols,
                            preferred_element_type=jnp.float32,
                        )
                    )
                grad_input, grad_first, grad_second = norm_back(grad_normed)
                grad_rows = grad_rows + grad_input
                if layer_index == 0:
                    acc_gain[part_index] = acc_gain[part_index] + grad_first
                    acc_bias[part_index] = acc_bias[part_index] + grad_second
                else:
                    acc_scale[part_index] = acc_scale[part_index] + grad_first
                    acc_shift[part_index] = acc_shift[part_index] + grad_second
        grad_group = [grad_rows]
        frames_list.append(jnp.stack(out_group))
        grads_list.append(jnp.stack(grad_group))
    total_qkv, total_out, total_up, total_down = (
        lax.psum(jnp.stack(acc_qkv).astype(jnp.bfloat16), "dp").astype(jnp.float32),
        lax.psum(jnp.stack(acc_out).astype(jnp.bfloat16), "dp").astype(jnp.float32),
        lax.psum(jnp.stack(acc_up).astype(jnp.bfloat16), "dp").astype(jnp.float32),
        lax.psum(jnp.stack(acc_down).astype(jnp.bfloat16), "dp").astype(jnp.float32),
    )
    norm_totals = lax.psum(
        (jnp.stack(acc_gain), jnp.stack(acc_bias), jnp.stack(acc_scale), jnp.stack(acc_shift)),
        ("dp", "tensor"),
    )
    return (
        jnp.stack(frames_list),
        jnp.stack(grads_list),
        total_qkv.reshape(2, model_width, 3, -1),
        total_out,
        total_up,
        total_down,
        norm_totals[0],
        norm_totals[1],
        norm_totals[2],
        norm_totals[3],
    )


bf16,f32=jnp.bfloat16,jnp.float32
NT=(((1,),(1,)),((),()))
TN=(((0,),(0,)),((),()))

def _limits(lims_ref, start, rows, causal, axis):
    prefix, valid = lims_ref[0], lims_ref[1]
    shape=(rows,1) if axis==0 else (1,rows)
    pos=start+lax.broadcasted_iota(jnp.int32,shape,axis)
    if causal:
        return jnp.minimum(jnp.maximum(pos,prefix-1),valid-1)
    return jnp.zeros(shape,jnp.int32)+(valid-1)

def fwd_kernel(causal, bq, lims_ref, q_ref, k_ref, v_ref, o_ref, l_ref):
    length=q_ref.shape[0]
    lane=lax.broadcasted_iota(jnp.int32,(bq,128),1)
    def block(start, kk):
        q=q_ref[pl.ds(start,bq),:]*jnp.asarray(0.125,bf16)
        lim=_limits(lims_ref,start,bq,causal,0)
        outs=[];rows=[]
        for h in range(2):
            qm=jnp.where((lane<HEAD_DIM)==(h==0),q,jnp.zeros_like(q))
            s=lax.dot_general(qm,k_ref[0:kk,:],NT,preferred_element_type=f32)
            key=lax.broadcasted_iota(jnp.int32,(bq,kk),1)
            s=jnp.where(key<=lim,s,-1e9)
            m=jnp.max(s,axis=1,keepdims=True)
            e=jnp.exp(s-m)
            l=jnp.sum(e,axis=1,keepdims=True)
            o=jnp.dot(e.astype(bf16),v_ref[0:kk,:],preferred_element_type=f32)*(1.0/l)
            outs.append(o); rows.append(m+jnp.log(l))
        o_ref[pl.ds(start,bq),:]=jnp.where(lane<HEAD_DIM,outs[0],outs[1]).astype(bf16)
        both=jnp.where(lane<HEAD_DIM,rows[0],rows[1])
        bt=both.T
        l_ref[0,0:1,pl.ds(start,bq)]=bt[0:1,:]
        l_ref[0,1:2,pl.ds(start,bq)]=bt[HEAD_DIM:HEAD_DIM+1,:]
    nq=length//bq
    if causal:
        for i in range(nq): block(i*bq,(i+1)*bq)
    else:
        def body(i,c):
            block(pl.multiple_of(i*bq,bq),length); return c
        lax.fori_loop(0,nq,body,0)

def attn_fwd(qkv, lims, causal, bq=256):
    length=qkv.shape[0]; width=qkv.shape[1]//3; pairs=width//128
    spec=lambda off: pl.BlockSpec((length,128),lambda i,off=off:(0,off*pairs+i))
    return pl.pallas_call(partial(fwd_kernel,causal,bq),
        grid=(pairs,),
        in_specs=[pl.BlockSpec(memory_space=pltpu.SMEM),spec(0),spec(1),spec(2)],
        out_specs=[pl.BlockSpec((length,128),lambda i:(0,i)),pl.BlockSpec((1,2,length),lambda i:(i,0,0))],
        out_shape=[jax.ShapeDtypeStruct((length,width),bf16),jax.ShapeDtypeStruct((pairs,2,length),f32)],
        compiler_params=pltpu.CompilerParams(vmem_limit_bytes=48*2**20),
        cost_estimate=pl.CostEstimate(flops=pairs*2**20,bytes_accessed=length*width*8,transcendentals=0),
        name="attn_fwd_"+("causal" if causal else "full"),
    )(lims,qkv,qkv,qkv)

def bwd_kernel(causal,bq,lims_ref,q_ref,k_ref,v_ref,l_ref,do_ref,grad_ref,dk_acc,dv_acc):
    length=q_ref.shape[0]
    lane=lax.broadcasted_iota(jnp.int32,(bq,128),1)
    dk_acc[...]=jnp.zeros_like(dk_acc); dv_acc[...]=jnp.zeros_like(dv_acc)
    width=grad_ref.shape[1]//3
    at=[pl.multiple_of(part*width+pl.program_id(0)*128,128) for part in range(3)]
    def block(start,kk):
        q=q_ref[pl.ds(start,bq),:]*jnp.asarray(0.125,bf16)
        do=do_ref[pl.ds(start,bq),:]
        lim=_limits(lims_ref,start,bq,causal,1)
        dqs=[]
        for h in range(2):
            sel=(lane<HEAD_DIM)==(h==0)
            qm=jnp.where(sel,q,jnp.zeros_like(q)); dom=jnp.where(sel,do,jnp.zeros_like(do))
            s=lax.dot_general(k_ref[0:kk,:],qm,NT,preferred_element_type=f32)
            dp=lax.dot_general(v_ref[0:kk,:],dom,NT,preferred_element_type=f32)
            key=lax.broadcasted_iota(jnp.int32,(kk,bq),0)
            lrow=l_ref[0,h:h+1,pl.ds(start,bq)]
            p=jnp.where(key<=lim,jnp.exp(s-lrow),0.0)
            pd=p*dp
            D=jnp.sum(pd,axis=0,keepdims=True)
            ds=(pd-p*D).astype(bf16)
            dv_acc[0:kk,:]+=jnp.dot(p.astype(bf16),dom,preferred_element_type=f32)
            dk_acc[0:kk,:]+=jnp.dot(ds,qm,preferred_element_type=f32)
            dqs.append(lax.dot_general(ds,k_ref[0:kk,:],TN,preferred_element_type=f32))
        grad_ref[pl.ds(start,bq),pl.ds(at[0],128)]=(jnp.where(lane<HEAD_DIM,dqs[0],dqs[1])*0.125).astype(bf16)
    nq=length//bq
    if causal:
        for i in range(nq): block(i*bq,(i+1)*bq)
    else:
        def body(i,c):
            block(pl.multiple_of(i*bq,bq),length); return c
        lax.fori_loop(0,nq,body,0)
    grad_ref[:,pl.ds(at[1],128)]=dk_acc[...].astype(bf16)
    grad_ref[:,pl.ds(at[2],128)]=dv_acc[...].astype(bf16)

def attn_bwd(qkv,L,do,lims,causal,bq=256):
    length=qkv.shape[0]; width=qkv.shape[1]//3; pairs=width//128
    spec=lambda off: pl.BlockSpec((length,128),lambda i,off=off:(0,off*pairs+i))
    one=pl.BlockSpec((length,128),lambda i:(0,i))
    return pl.pallas_call(partial(bwd_kernel,causal,bq),
        grid=(pairs,),
        in_specs=[pl.BlockSpec(memory_space=pltpu.SMEM),spec(0),spec(1),spec(2),pl.BlockSpec((1,2,length),lambda i:(i,0,0)),one],
        out_specs=pl.BlockSpec((length,3*width),lambda i:(0,0)),
        out_shape=jax.ShapeDtypeStruct((length,3*width),bf16),
        scratch_shapes=[pltpu.VMEM((length,128),f32)]*2,
        compiler_params=pltpu.CompilerParams(vmem_limit_bytes=48*2**20),
        cost_estimate=pl.CostEstimate(flops=pairs*2**20,bytes_accessed=length*width*8,transcendentals=0),
        name="attn_bwd_"+("causal" if causal else "full"),
    )(lims,qkv,qkv,qkv,L,do)


def pin(*values):
    return lax.optimization_barrier(values)


def swap_tensor(block):
    return lax.ppermute(block, "tensor", [(0, 1), (1, 0)])


def swap_bit(block, bit, dp_size):
    return lax.ppermute(block, "dp", [(place, place ^ (1 << bit)) for place in range(dp_size)])


def in_order(flag, mine, other):
    first = jnp.where(flag == 0, mine, other)
    second = jnp.where(flag == 0, other, mine)
    return jnp.concatenate([first, second], axis=0)


def add_rounded(left, right):
    return (left.astype(f32) + right.astype(f32)).astype(bf16)


def norm_forward(rows, gain_row, shift_row):
    mean = jnp.mean(rows, axis=-1, keepdims=True)
    centered = rows - mean
    rate = lax.rsqrt(jnp.mean(centered * centered, axis=-1, keepdims=True) + norm_eps)
    normed = centered * rate * gain_row + shift_row
    return normed.astype(bf16), (rows, mean, rate)


def norm_backward(saved, grad_normed, gain_row):
    rows, mean, rate = saved
    unit = (rows - mean) * rate
    grad_unit = grad_normed * gain_row
    grad_rows = rate * (
        grad_unit
        - jnp.mean(grad_unit, axis=-1, keepdims=True)
        - unit * jnp.mean(grad_unit * unit, axis=-1, keepdims=True)
    )
    return grad_rows, jnp.sum(grad_normed * unit, axis=0), jnp.sum(grad_normed, axis=0)


def gelu_pair(hidden):
    square = hidden * hidden
    share = 0.5 + 0.5 * jnp.tanh(hidden * (0.7978845608 + (0.7978845608 * 0.044715) * square))
    value = hidden * share
    rate = 2.0 * 0.7978845608 + (6.0 * 0.7978845608 * 0.044715) * square
    slope = share + (value * rate) * (1.0 - share)
    return value.astype(bf16), slope.astype(bf16)


def dot_sum(pairs, dims):
    total = None
    for left, right in pairs:
        term = lax.dot_general(left, right, dims, preferred_element_type=f32)
        total = term if total is None else total + term
    return total


def dot_low(left, right, dims):
    return lax.dot_general(left, right, dims, preferred_element_type=f32).astype(bf16)


NN = (((1,), (0,)), ((), ()))
SPLIT_AXIS = {"up": 1, "down": 0}
PACK_WIDTH = 512


def quarter_of(kind, half, place):
    axis = SPLIT_AXIS[kind]
    width = half.shape[axis] // 2
    return lax.dynamic_slice_in_dim(half, place * width, width, axis)


def row_half(block, place):
    height = block.shape[0] // 2
    return lax.dynamic_slice_in_dim(block, place * height, height, 0)


def flat_kernel(in_ref, out_ref):
    width = in_ref.shape[3]
    for part in range(3):
        out_ref[:, part * width : (part + 1) * width] = in_ref[0, part]


def flat_qkv(stacked, layer):
    _, _, height, width = stacked.shape
    rows = height // 2
    return pl.pallas_call(
        flat_kernel,
        grid=(2,),
        in_specs=[pl.BlockSpec((1, 3, rows, width), lambda step: (layer, 0, step, 0))],
        out_specs=pl.BlockSpec((rows, 3 * width), lambda step: (step, 0)),
        out_shape=jax.ShapeDtypeStruct((height, 3 * width), bf16),
        cost_estimate=pl.CostEstimate(flops=0, bytes_accessed=12 * height * width, transcendentals=0),
        name="flat_qkv",
    )(stacked)


def pack_kernel(kinds, place_ref, *refs):
    out_ref = refs[-1]
    at = 0
    for kind, ref in zip(kinds, refs):
        if kind == "qkv":
            pieces = [ref[0, part] for part in range(3)]
        else:
            count = ref.shape[2] // PACK_WIDTH
            pieces = [ref[0, :, part * PACK_WIDTH : (part + 1) * PACK_WIDTH] for part in range(count)]
        for piece in pieces:
            out_ref[at : at + piece.shape[0], :] = piece
            at += piece.shape[0]


def pack_pieces(place, layer, dp_size, kinds, arrays):
    specs, total = [], 0
    for kind, array in zip(kinds, arrays):
        height, width = array.shape[-2:]
        rows = height // dp_size
        if kind == "qkv":
            specs.append(pl.BlockSpec((1, 3, rows, width), lambda step, at: (layer, 0, at[0], 0)))
            total += 3 * rows * width // PACK_WIDTH
        else:
            specs.append(pl.BlockSpec((1, rows, width), lambda step, at: (layer, at[0], 0)))
            total += rows * width // PACK_WIDTH
    return pl.pallas_call(
        partial(pack_kernel, kinds),
        grid_spec=pltpu.PrefetchScalarGridSpec(
            num_scalar_prefetch=1,
            grid=(1,),
            in_specs=specs,
            out_specs=pl.BlockSpec((total, PACK_WIDTH), lambda step, at: (0, 0)),
        ),
        out_shape=jax.ShapeDtypeStruct((total, PACK_WIDTH), bf16),
        cost_estimate=pl.CostEstimate(flops=0, bytes_accessed=4 * total * PACK_WIDTH, transcendentals=0),
        name="pack_pieces",
    )(place.reshape(1).astype(jnp.int32), *arrays)


def unpack_kernel(in_ref, *refs):
    at = 0
    for ref in refs:
        rows = ref.shape[0] // in_ref.shape[0]
        for part in range(ref.shape[1] // PACK_WIDTH):
            for block in range(in_ref.shape[0]):
                ref[block * rows : (block + 1) * rows, part * PACK_WIDTH : (part + 1) * PACK_WIDTH] = in_ref[
                    block, at : at + rows, :
                ]
            at += rows


def unpack_halves(gathered, shapes):
    dp_size, total, _ = gathered.shape
    some = max(1, dp_size // 4)
    return pl.pallas_call(
        unpack_kernel,
        grid=(dp_size // some,),
        in_specs=[pl.BlockSpec((some, total, PACK_WIDTH), lambda step: (step, 0, 0))],
        out_specs=[
            pl.BlockSpec((height // dp_size * some, width), lambda step: (step, 0)) for height, width in shapes
        ],
        out_shape=[jax.ShapeDtypeStruct(shape, bf16) for shape in shapes],
        compiler_params=pltpu.CompilerParams(vmem_limit_bytes=32 * 2**20),
        cost_estimate=pl.CostEstimate(
            flops=0, bytes_accessed=4 * dp_size * total * PACK_WIDTH, transcendentals=0
        ),
        name="unpack_halves",
    )(gathered)


def stack_kernel(steps, side_ref, down_own, up_own, down_other, up_other, out_ref):
    blocks, rows = out_ref.shape[0], out_ref.shape[1] // 2

    def write(down_ref, up_ref):
        for block in range(blocks):
            out_ref[block, :rows] = down_ref[block * rows : (block + 1) * rows]
            out_ref[block, rows:] = up_ref[block * rows : (block + 1) * rows]

    pl.when(pl.program_id(0) < steps)(lambda: write(down_own, up_own))
    pl.when(pl.program_id(0) >= steps)(lambda: write(down_other, up_other))


def stack_pair(side, dp_size, down_parts, up_parts):
    height, width = down_parts[0].shape
    steps = 4
    rows, some = height // dp_size, dp_size // steps
    own = pl.BlockSpec((some * rows, width), lambda step, side_ref: (jnp.minimum(step, steps - 1), 0))
    other = pl.BlockSpec((some * rows, width), lambda step, side_ref: (jnp.maximum(step - steps, 0), 0))

    def target(step, side_ref):
        half = jnp.where(step < steps, side_ref[0], 1 - side_ref[0])
        return (half * steps + step % steps, 0, 0)

    return pl.pallas_call(
        partial(stack_kernel, steps),
        grid_spec=pltpu.PrefetchScalarGridSpec(
            num_scalar_prefetch=1,
            grid=(2 * steps,),
            in_specs=[own, own, other, other],
            out_specs=pl.BlockSpec((some, 2 * rows, width), target),
        ),
        out_shape=jax.ShapeDtypeStruct((2 * dp_size, 2 * rows, width), bf16),
        compiler_params=pltpu.CompilerParams(vmem_limit_bytes=32 * 2**20),
        cost_estimate=pl.CostEstimate(flops=0, bytes_accessed=16 * height * width, transcendentals=0),
        name="stack_pair",
    )(side.reshape(1).astype(jnp.int32), down_parts[0], up_parts[0], down_parts[1], up_parts[1])


def place_joint_kernel(whole_ref, *refs):
    qkv_out, out_out = refs[-2:]
    for block in range(whole_ref.shape[0]):
        rows = qkv_out.shape[2] // whole_ref.shape[0]
        for part in range(3):
            qkv_out[0, part, block * rows : (block + 1) * rows, :] = whole_ref[
                block, part * rows : (part + 1) * rows, :
            ].astype(f32)
        at, rows = 3 * rows, out_out.shape[1] // whole_ref.shape[0]
        for part in range(out_out.shape[2] // PACK_WIDTH):
            out_out[0, block * rows : (block + 1) * rows, part * PACK_WIDTH : (part + 1) * PACK_WIDTH] = whole_ref[
                block, at + part * rows : at + (part + 1) * rows, :
            ].astype(f32)


def place_joint(whole, layer, qkv_shape, out_shape, bases):
    dp_size, total, _ = whole.shape
    some = dp_size // 4
    operands, in_specs, aliases = [whole], [pl.BlockSpec((some, total, PACK_WIDTH), lambda step: (step, 0, 0))], {}
    if bases is not None:
        operands += bases
        in_specs += [pl.BlockSpec(memory_space=pl.ANY)] * 2
        aliases = {1: 0, 2: 1}
    return pl.pallas_call(
        place_joint_kernel,
        grid=(4,),
        in_specs=in_specs,
        out_specs=[
            pl.BlockSpec((1, 3, qkv_shape[0] // 4, qkv_shape[1] // 3), lambda step: (layer, 0, step, 0)),
            pl.BlockSpec((1, out_shape[0] // 4, out_shape[1]), lambda step: (layer, step, 0)),
        ],
        out_shape=[
            jax.ShapeDtypeStruct((2, 3, qkv_shape[0], qkv_shape[1] // 3), f32),
            jax.ShapeDtypeStruct((2,) + tuple(out_shape), f32),
        ],
        input_output_aliases=aliases,
        compiler_params=pltpu.CompilerParams(vmem_limit_bytes=32 * 2**20),
        cost_estimate=pl.CostEstimate(flops=0, bytes_accessed=6 * dp_size * total * PACK_WIDTH, transcendentals=0),
        name="place_joint",
    )(*operands)


def place_pair_kernel(whole_ref, up_out, down_out):
    for block in range(whole_ref.shape[0]):
        rows = whole_ref.shape[2]
        down_out[0, block * rows : (block + 1) * rows, :] = whole_ref[block, 0].astype(f32)
        up_out[0, :, block * rows : (block + 1) * rows] = whole_ref[block, 1].astype(f32).T


def place_pair(whole, layer):
    dp_size, rows, columns = whole.shape
    rows = rows // 2
    some = dp_size // 4
    return pl.pallas_call(
        place_pair_kernel,
        grid=(4,),
        in_specs=[pl.BlockSpec((some, 2, rows, columns), lambda step: (step, 0, 0, 0))],
        out_specs=[
            pl.BlockSpec((1, columns, some * rows), lambda step: (layer, 0, step)),
            pl.BlockSpec((1, some * rows, columns), lambda step: (layer, step, 0)),
        ],
        out_shape=[
            jax.ShapeDtypeStruct((2, columns, dp_size * rows), f32),
            jax.ShapeDtypeStruct((2, dp_size * rows, columns), f32),
        ],
        compiler_params=pltpu.CompilerParams(vmem_limit_bytes=40 * 2**20),
        cost_estimate=pl.CostEstimate(flops=0, bytes_accessed=12 * dp_size * rows * columns, transcendentals=0),
        name="place_pair",
    )(whole.reshape(dp_size, 2, rows, columns))


def place_kernel(whole_ref, *refs):
    out_ref = refs[-1]
    out_ref[0] = whole_ref[...].reshape(-1, whole_ref.shape[-1]).astype(f32)


def place_quarters(kind, whole, which, layer, base):
    dp_size, rows, columns = whole.shape
    half, some, rows = dp_size // 2, dp_size // 4, rows // 2
    if kind == "down":
        out_spec = pl.BlockSpec((1, some * rows, columns), lambda step: (layer, step, 0))
    else:
        out_spec = pl.BlockSpec((1, some * rows, columns), lambda step: (layer, step % 2, step // 2))
    return pl.pallas_call(
        place_kernel,
        grid=(4,),
        in_specs=[
            pl.BlockSpec(
                (some, None, None, rows, columns), lambda step: (step % 2, step // 2, which, 0, 0)
            ),
            pl.BlockSpec(memory_space=pl.ANY),
        ],
        out_specs=out_spec,
        out_shape=jax.ShapeDtypeStruct(base.shape, f32),
        input_output_aliases={1: 0},
        compiler_params=pltpu.CompilerParams(vmem_limit_bytes=32 * 2**20),
        cost_estimate=pl.CostEstimate(flops=0, bytes_accessed=6 * dp_size * rows * columns, transcendentals=0),
        name="place_" + kind,
    )(whole.reshape(half, 2, 2, rows, columns), base)


def frame_kernel(side_ref, mine_ref, other_ref, out_ref):
    own = pl.program_id(0) == side_ref[0]
    out_ref[0, 0] = jnp.where(own, mine_ref[...], other_ref[...].astype(f32))


def place_frames(side, mine, other):
    height, width = mine.shape
    rows = height // 2
    spec = pl.BlockSpec((rows, width), lambda slot, step, side_ref: (step, 0))
    return pl.pallas_call(
        frame_kernel,
        grid_spec=pltpu.PrefetchScalarGridSpec(
            num_scalar_prefetch=1,
            grid=(2, 2),
            in_specs=[spec, spec],
            out_specs=pl.BlockSpec((1, 1, rows, width), lambda slot, step, side_ref: (slot, 0, step, 0)),
        ),
        out_shape=jax.ShapeDtypeStruct((2, 1, height, width), f32),
        name="place_frames",
    )(side.reshape(1).astype(jnp.int32), mine, other)


def take_axis(block, index):
    return lax.dynamic_index_in_dim(block, index, 1, keepdims=False)


def flat_rows(block):
    return block.reshape(-1, block.shape[-1])


def join_level(here, kept, arrived):
    first = jnp.where(here == 0, kept, arrived)
    second = jnp.where(here == 0, arrived, kept)
    joined = jnp.stack([first, second], axis=1)
    return joined.reshape((-1,) + joined.shape[2:])


class Chain:
    def __init__(self, place, dp_size, rows, columns, kind, gather):
        self.place, self.dp_size, self.kind, self.gather = place, dp_size, kind, gather
        self.rows, self.columns = rows, columns
        self.bit_count = dp_size.bit_length() - 1
        self.flight = []

    def bit(self, index):
        return (self.place >> index) & 1

    def swap(self, block, bit):
        return swap_bit(block, bit, self.dp_size)

    def pair(self, block):
        return block.reshape(-1, 2, self.rows, self.columns)

    def start(self, near, far, ours=None, own_far=None):
        self.near, self.ours = near, ours
        self.flight = [self.swap(far, 0)] + ([] if ours is None else [self.swap(own_far, 0)])
        self.state = "core"

    def start_rows(self, own, other):
        self.start_other(other)
        self.add_own(own)

    def start_other(self, other):
        split, core = self.pair(other), self.bit(0)
        self.start(flat_rows(take_axis(split, core)), flat_rows(take_axis(split, 1 - core)))

    def add_own(self, own):
        split, core = self.pair(own), self.bit(0)
        self.flight = self.flight + [self.swap(flat_rows(take_axis(split, 1 - core)), 0)]
        self.ours = flat_rows(take_axis(split, core))

    def halves(self, block, bit):
        split, here = self.pair(block), self.bit(bit)
        return flat_rows(take_axis(split, here)), flat_rows(take_axis(split, 1 - here))

    def settle(self, arrived):
        self.near_here, self.near_away = self.halves(add_rounded(self.near, arrived[0]), 1)
        if self.ours is not None:
            self.kept_here, self.kept_away = self.halves(add_rounded(self.ours, arrived[1]), 1)
        self.flight, self.state = [], "ready"

    def launch(self):
        self.flight = [swap_tensor(self.near_away) if self.kind == "x" else self.swap(self.near_away, 1)]
        self.state = "first"

    def second(self, arrived):
        if len(arrived) > 1:
            self.kept_here, self.kept_away = self.halves(add_rounded(self.ours, arrived[1]), 1)
        if self.kind == "x":
            self.kept_away = add_rounded(self.kept_away, arrived[0])
        else:
            self.near_here = add_rounded(self.near_here, arrived[0])
        self.flight = [swap_tensor(self.near_here), self.swap(self.kept_away, 1)]
        self.state = "second"

    def next_bit(self, total, index):
        if index == self.bit_count:
            self.kept, self.state = total, "gather"
            if self.gather == "native":
                self.flight = [lax.all_gather(total, "dp", axis=0, tiled=False)]
                return
            if self.gather is None:
                self.flight, self.state = [], "done"
                return
            self.kept, self.level = total[None], index - 1
            self.flight = [self.swap(self.kept, self.level)]
            return
        self.kept, away = self.halves(total, index)
        self.flight, self.index, self.state = [self.swap(away, index)], index, "bits"

    def advance(self, arrived, hold=False):
        if self.state == "done":
            return
        if self.state == "core":
            self.settle(arrived)
            if not hold:
                self.launch()
        elif self.state == "ready":
            self.launch()
        elif self.state == "first":
            self.second(arrived)
        elif self.state == "second":
            total = self.kept_here.astype(f32) + arrived[0].astype(f32) + arrived[1].astype(f32)
            self.next_bit(total.astype(bf16), 2)
        elif self.state == "bits":
            self.next_bit(add_rounded(self.kept, arrived[0]), self.index + 1)
        elif self.gather == "native":
            self.whole, self.flight, self.state = arrived[0], [], "done"
        else:
            self.kept = join_level(self.bit(self.level), self.kept, arrived[0])
            self.level -= 1
            if self.level < 0:
                self.whole, self.flight, self.state = self.kept, [], "done"
            else:
                self.flight = [self.swap(self.kept, self.level)]


class Scatter:
    def __init__(self, block):
        self.flight = [lax.psum_scatter(block, ("tensor", "dp"), scatter_dimension=0, tiled=True)]
        self.state = "sum"

    def advance(self, arrived):
        if self.state == "sum":
            self.flight, self.state = [lax.all_gather(arrived[0], "dp", axis=0, tiled=False)], "gather"
        elif self.state == "gather":
            self.whole, self.flight, self.state = arrived[0], [], "done"


class Gather:
    def __init__(self, qkv, out, width, native):
        assert qkv.state == "done" and out.state == "done"
        pieces = []
        for block in (qkv.kept, out.kept):
            for at in range(0, block.shape[1], width):
                pieces.append(lax.slice_in_dim(block, at, at + width, axis=1))
        self.kept = jnp.concatenate(pieces, axis=0)
        self.native, self.bit, self.swap = native, qkv.bit, qkv.swap
        self.state = "going"
        if native:
            self.flight = [lax.all_gather(self.kept, "dp", axis=0, tiled=False)]
        else:
            self.kept, self.level = self.kept[None], qkv.bit_count - 1
            self.flight = [self.swap(self.kept, self.level)]

    def advance(self, arrived):
        if self.state == "done":
            return
        if self.native:
            self.whole, self.flight, self.state = arrived[0], [], "done"
            return
        self.kept = join_level(self.bit(self.level), self.kept, arrived[0])
        self.level -= 1
        if self.level < 0:
            self.whole, self.flight, self.state = self.kept, [], "done"
        else:
            self.flight = [self.swap(self.kept, self.level)]


class Spread:
    def __init__(self, block, dp_size):
        self.block, self.dp_size = block, dp_size
        self.bits = list(range(dp_size.bit_length() - 1))
        self.flight = [swap_tensor(block)]

    def advance(self, arrived):
        if not arrived:
            return
        self.block = self.block + arrived[0]
        self.flight = [swap_bit(self.block, self.bits.pop(0), self.dp_size)] if self.bits else []


def move(state, *chains, hold=()):
    everyone = chains + tuple(hold)
    state, flights = pin(state, [one.flight for one in everyone])
    for one, flight in zip(everyone, flights):
        if one in hold:
            one.advance(flight, hold=True)
        else:
            one.advance(flight)
    return state


def paired_device(
    dp_size,
    frames_in,
    phone_len,
    frame_len,
    section,
    norm_gain,
    norm_bias,
    ada_scale,
    ada_shift,
    w_qkv,
    w_out,
    w_up,
    w_down,
    out_grad,
):
    model_width = frames_in.shape[3]
    section_count = ada_scale.shape[1]
    side = lax.axis_index("tensor")
    place = lax.axis_index("dp")
    core, near_row = place & 1, (place >> 1) & 1

    def away_rows(halves):
        return lax.dynamic_index_in_dim(halves[:, 0], 1 - side, 0, keepdims=False)

    def whole_rows(halves, other):
        mine = lax.dynamic_index_in_dim(halves[:, 0], side, 0, keepdims=False)
        return in_order(side, mine, other)

    prefix = lax.dynamic_index_in_dim(phone_len[:, 0], side, 0, keepdims=False)
    frames = lax.dynamic_index_in_dim(frame_len[:, 0], side, 0, keepdims=False)
    chosen = lax.dynamic_index_in_dim(section[:, 0], side, 0, keepdims=False)
    limits = jnp.stack([prefix, prefix + frames]).astype(jnp.int32)
    picker = (lax.iota(jnp.int32, section_count) == chosen).astype(f32)[:, None]

    gains = [
        [norm_gain[0], norm_gain[1]],
        [jnp.sum(picker * ada_scale[part], axis=0) for part in range(2)],
    ]
    shifts = [
        [norm_bias[0], norm_bias[1]],
        [jnp.sum(picker * ada_shift[part], axis=0) for part in range(2)],
    ]

    stacked = w_qkv.transpose(0, 2, 1, 3)
    arrays = {"qkv": stacked, "out": w_out, "up": w_up, "down": w_down}
    flat_shape = {
        "qkv": (model_width, 3 * stacked.shape[3]),
        "out": w_out.shape[1:],
        "up": w_up.shape[1:],
        "down": w_down.shape[1:],
    }

    def packed(layer, kinds):
        return pack_pieces(place, layer, dp_size, kinds, [arrays[kind] for kind in kinds])

    def gathered(arrived):
        return lax.all_gather(arrived, "dp", axis=0, tiled=False)

    def unpacked(whole, kinds):
        return dict(zip(kinds, unpack_halves(whole, [flat_shape[kind] for kind in kinds])))

    attn_kinds, all_kinds = ("qkv", "out"), ("qkv", "out", "up", "down")
    rows_away, first_send = pin(away_rows(frames_in), packed(0, attn_kinds))
    other_rows = swap_tensor(rows_away)
    first_pack = swap_tensor(first_send)
    own_qkv = [flat_qkv(stacked, layer) for layer in range(2)]
    first_pack, own_qkv = pin(first_pack, own_qkv)
    first_whole = gathered(first_pack)
    second_send = packed(1, all_kinds)
    piece_rows, piece_columns = model_width // 2, w_up.shape[2] // 2
    up_send = lax.dynamic_slice(
        w_up, (0, near_row * piece_rows, core * piece_columns), (1, piece_rows, piece_columns)
    )[0]
    piece_rows = w_down.shape[1] // 4
    down_send = lax.dynamic_slice(
        w_down, (0, (2 * core + near_row) * piece_rows, 0), (1, piece_rows, model_width)
    )[0]
    other_rows, second_send, up_send, down_send, own_qkv = pin(
        other_rows, second_send, up_send, down_send, own_qkv
    )
    second_pack = swap_tensor(second_send)
    rows = whole_rows(frames_in, other_rows).astype(f32)
    normed, norm_kept = norm_forward(rows, gains[0][0], shifts[0][0])
    mine = dot_low(normed, own_qkv[0], NN)
    mine, second_pack, up_send, down_send = pin(mine, second_pack, up_send, down_send)
    second_whole = gathered(second_pack)
    up_piece = swap_tensor(up_send)
    mix_mine = attn_fwd(mine, limits, True, 512)
    mix_mine, up_piece, down_send = pin(mix_mine, up_piece, down_send)
    down_piece = swap_tensor(down_send)
    up_there = swap_bit(up_piece, 1, dp_size)
    first = unpacked(first_whole, attn_kinds)
    theirs = dot_low(normed, first["qkv"], NN)
    mix_theirs = attn_fwd(theirs, limits, True, 512)
    mix_theirs, up_there, down_piece = pin(mix_theirs, up_there, down_piece)
    up_near = in_order(near_row, up_piece, up_there)
    up_far = swap_bit(up_near, 0, dp_size)
    down_there = swap_bit(down_piece, 1, dp_size)
    kept = [(normed, norm_kept, [mine, theirs], [mix_mine, mix_theirs])]
    rows = rows + dot_sum([(mix_mine[0], w_out[0]), (mix_theirs[0], first["out"])], NN)
    normed, norm_kept = norm_forward(rows, gains[0][1], shifts[0][1])
    pair_own = gelu_pair(jnp.dot(normed, w_up[0], preferred_element_type=f32))
    pair_own, up_far, normed, norm_kept, rows = pin(pair_own, up_far, normed, norm_kept, rows)
    pair_near = gelu_pair(jnp.dot(normed, up_near, preferred_element_type=f32))
    pair_far = gelu_pair(jnp.dot(normed, up_far, preferred_element_type=f32))
    rows = rows + dot_sum([(pair_own[0], w_down[0])], NN)
    rows, pair_near, pair_far, down_there = pin(rows, pair_near, pair_far, down_there)
    down_near = in_order(near_row, down_piece, down_there)
    down_far = swap_bit(down_near, 0, dp_size)
    grad_send = away_rows(out_grad)
    rows = rows + dot_sum([(pair_near[0], down_near)], NN)
    rows, grad_send, down_far = pin(rows, grad_send, down_far)
    grad_other = swap_tensor(grad_send)
    rows = rows + dot_sum([(pair_far[0], down_far)], NN)
    kept.append((normed, norm_kept, [pair_own, pair_near, pair_far]))

    normed, norm_kept = norm_forward(rows, gains[1][0], shifts[1][0])
    mine = dot_low(normed, own_qkv[1], NN)
    mix_mine = attn_fwd(mine, limits, False, 512)
    mix_mine, second_whole = pin(mix_mine, second_whole)
    second = unpacked(second_whole, all_kinds)
    weights = [
        {
            "qkv": [own_qkv[0], first["qkv"]],
            "out": [w_out[0], first["out"]],
            "up": [w_up[0], up_near, up_far],
            "down": [w_down[0], down_near, down_far],
        },
        {
            "qkv": [own_qkv[1], second["qkv"]],
            "out": [w_out[1], second["out"]],
            "up": [w_up[1], second["up"]],
            "down": [w_down[1], second["down"]],
        },
    ]
    theirs = dot_low(normed, second["qkv"], NN)
    mix_theirs = attn_fwd(theirs, limits, False, 512)
    mixed = [mix_mine, mix_theirs]
    kept.append((normed, norm_kept, [mine, theirs], mixed))
    rows = rows + dot_sum([(mix[0], part) for mix, part in zip(mixed, weights[1]["out"])], NN)
    normed, norm_kept = norm_forward(rows, gains[1][1], shifts[1][1])
    pairs = [gelu_pair(jnp.dot(normed, part, preferred_element_type=f32)) for part in weights[1]["up"]]
    pairs, rows, normed, norm_kept = pin(pairs, rows, normed, norm_kept)
    rows = rows + dot_sum([(pair[0], part) for pair, part in zip(pairs, weights[1]["down"])], NN)
    kept.append((normed, norm_kept, pairs))
    rows, grad_other = pin(rows, grad_other)

    def halves_of(block):
        height = block.shape[0] // 2
        mine = lax.dynamic_slice_in_dim(block, side * height, height, 0)
        away = lax.dynamic_slice_in_dim(block, (1 - side) * height, height, 0)
        return mine, away.astype(bf16)

    out_mine, out_away = halves_of(rows)

    norm_sums = [[None, None], [None, None]]
    grad_rows = whole_rows(out_grad, grad_other).astype(f32)
    def chain(kind, first, gather, split="rows"):
        height, width = flat_shape[kind]
        if split == "core":
            count = dp_size // 2
            height, width = (height, width // 2) if kind == "up" else (height // 2, width)
        else:
            count = dp_size
        return Chain(place, dp_size, height // count, width, first, gather)

    def start_quarters(one, kind, parts):
        own, near, far = parts
        one.start(near, far, quarter_of(kind, own, core), quarter_of(kind, own, 1 - core))

    def hidden_grads(layer, low):
        pairs = kept[2 * layer + 1][2]
        return [
            (
                lax.dot_general(low, part, NT, preferred_element_type=f32) * pair[1].astype(f32)
            ).astype(bf16)
            for pair, part in zip(pairs, weights[layer]["down"])
        ]

    def down_grads(layer, low):
        return [dot_low(pair[0], low, TN) for pair in kept[2 * layer + 1][2]]

    def up_grads(layer, hidden):
        return [dot_low(kept[2 * layer + 1][0], part, TN) for part in hidden]

    def out_grads(layer, low):
        return [dot_low(mix[0], low, TN) for mix in kept[2 * layer][3]]

    def mixed_grads(layer, low):
        return [dot_low(low, part, NT) for part in weights[layer]["out"]]

    def attention_grad(layer, part, grad_mix):
        _, _, projected, mixed = kept[2 * layer]
        rows = 256 if layer == 0 else 512
        return attn_bwd(projected[part], mixed[part][1], grad_mix, limits, layer == 0, rows)

    def norm_step(layer, part, grad_rows, grad_normed):
        added, grad_gain, grad_shift = norm_backward(
            kept[2 * layer + part][1], grad_normed, gains[layer][part]
        )
        norm_sums[layer][part] = (grad_gain, grad_shift)
        return grad_rows + added

    out1, qkv1 = chain("out", "x", None), chain("qkv", "y", None)
    down0, up0 = chain("down", "x", None, "core"), chain("up", "y", None, "core")
    out0, qkv0 = chain("out", "x", None), chain("qkv", "y", None)

    low = grad_rows.astype(bf16)
    down_parts = down_grads(1, low)
    hidden = hidden_grads(1, low)
    down_parts, hidden, grad_rows = pin(down_parts, hidden, grad_rows)
    up_parts = [dot_low(part, kept[3][0], TN) for part in hidden]
    both_parts = stack_pair(side, dp_size, down_parts, up_parts)
    both_parts, hidden, grad_rows = pin(both_parts, hidden, grad_rows)
    pair1 = Scatter(flat_rows(both_parts))
    grad_normed = dot_sum(list(zip(hidden, weights[1]["up"])), NT)
    grad_rows = norm_step(1, 1, grad_rows, grad_normed)
    low = grad_rows.astype(bf16)
    out_parts = out_grads(1, low)
    mine, theirs = mixed_grads(1, low)
    theirs = attention_grad(1, 1, theirs)
    out_parts, mine, theirs, grad_rows = pin(out_parts, mine, theirs, grad_rows)
    out1.start_rows(*out_parts)
    mine = attention_grad(1, 0, mine)
    parts = [dot_low(kept[2][0], part, TN) for part in (mine, theirs)]
    parts, mine, theirs, grad_rows = move((parts, mine, theirs, grad_rows), hold=[out1])
    qkv1.start_rows(*parts)
    out_there = swap_tensor(out_away)
    grad_normed = dot_sum(list(zip((mine, theirs), weights[1]["qkv"])), NT)
    grad_rows = norm_step(1, 0, grad_rows, grad_normed)
    low = grad_rows.astype(bf16)
    parts = down_grads(0, low)
    parts, low, grad_rows = move((parts, low, grad_rows), out1, qkv1)
    start_quarters(down0, "down", parts)
    hidden = hidden_grads(0, low)
    hidden, grad_rows, out_there = move((hidden, grad_rows, out_there), qkv1, out1, hold=[down0])
    parts = up_grads(0, hidden)
    grad_normed = dot_sum(list(zip(hidden, weights[0]["up"])), NT)
    parts, grad_normed, grad_rows = move((parts, grad_normed, grad_rows), qkv1, out1, down0, pair1)
    start_quarters(up0, "up", parts)
    grad_rows = norm_step(0, 1, grad_rows, grad_normed)
    low = grad_rows.astype(bf16)
    out_parts = out_grads(0, low)
    mine, theirs = mixed_grads(0, low)
    out_parts, mine, theirs, grad_rows = move((out_parts, mine, theirs, grad_rows), up0, qkv1, out1)
    out0.start_rows(*out_parts)
    theirs = attention_grad(0, 1, theirs)
    part_theirs = dot_low(kept[0][0], theirs, TN)
    part_theirs, mine, theirs, grad_rows = move(
        (part_theirs, mine, theirs, grad_rows), down0, up0, qkv1, out1, hold=[out0]
    )
    joint1 = Gather(qkv1, out1, PACK_WIDTH, True)
    qkv0.start_other(part_theirs)
    mine = attention_grad(0, 0, mine)
    part_mine = dot_low(kept[0][0], mine, TN)
    part_mine, mine, theirs, grad_rows = move(
        (part_mine, mine, theirs, grad_rows), down0, up0, out0, qkv0
    )
    qkv0.add_own(part_mine)
    grad_normed = dot_sum([(mine, weights[0]["qkv"][0]), (theirs, weights[0]["qkv"][1])], NT)
    grad_rows = norm_step(0, 0, grad_rows, grad_normed)
    grad_mine, grad_away = halves_of(grad_rows)
    late = Spread(
        jnp.concatenate(
            [jnp.stack([norm_sums[0][part][which] for which in range(2) for part in range(2)])]
            + [picker * norm_sums[1][part][which][None] for which in range(2) for part in range(2)]
        ),
        dp_size,
    )
    frames_out = place_frames(side, out_mine, out_there)
    grad_away, grad_mine, frames_out = move((grad_away, grad_mine, frames_out), qkv0, up0, down0, out0, pair1, late)
    grad_away, grad_mine = move((grad_away, grad_mine), qkv0, up0, down0, out0, late)
    pair0 = Gather(down0, up0, model_width, True)
    grad_there = swap_tensor(grad_away)
    bases = dict(zip(("up", "down"), place_pair(pair1.whole, 1)))
    bases, grad_mine, grad_there = move((bases, grad_mine, grad_there), qkv0, out0, late)
    (grad_mine,) = move((grad_mine,), qkv0, out0, late, joint1)
    joint0 = Gather(qkv0, out0, PACK_WIDTH, False)
    shapes = (flat_shape["qkv"], flat_shape["out"])
    joint_bases = place_joint(joint1.whole, 1, *shapes, None)
    frames_grad = place_frames(side, grad_mine, grad_there)
    joint_bases, frames_grad = move((joint_bases, frames_grad), joint0, late)
    joint_bases, frames_grad = move((joint_bases, frames_grad), joint0, late)
    (joint_bases,) = move((joint_bases,), joint0, pair0)
    grad_up = place_quarters("up", pair0.whole, 1, 0, bases["up"])
    grad_down = place_quarters("down", pair0.whole, 0, 0, bases["down"])
    while joint0.flight:
        joint0.advance(joint0.flight)
    while late.flight:
        late.advance(late.flight)
    grad_qkv, grad_out = place_joint(joint0.whole, 0, *shapes, list(joint_bases))

    gain_rows = late.block[4:].reshape(4, section_count, model_width)
    return (
        frames_out,
        frames_grad,
        grad_qkv.transpose(0, 2, 1, 3),
        grad_out,
        grad_up,
        grad_down,
        late.block[0:2],
        late.block[2:4],
        gain_rows[0:2],
        gain_rows[2:4],
    )


def per_device(dp_size, tensor_size, *arrays):
    micro_count, local_seqs = arrays[0].shape[:2]
    paired = micro_count == 2 and tensor_size == 2 and local_seqs == 1
    if paired and dp_size >= 4 and dp_size & (dp_size - 1) == 0:
        return paired_device(dp_size, *arrays)
    return grouped_device(*arrays)


def solution(mesh):
    return jax.shard_map(
        partial(per_device, mesh.shape["dp"], mesh.shape["tensor"]),
        mesh=mesh,
        in_specs=(
            P(None, "dp", "tensor", None),
            P(None, "dp"),
            P(None, "dp"),
            P(None, "dp"),
            P(),
            P(),
            P(),
            P(),
            P(None, None, None, "tensor"),
            P(None, "tensor", None),
            P(None, None, "tensor"),
            P(None, "tensor", None),
            P(None, "dp", "tensor", None),
        ),
        out_specs=(
            P(None, "dp", "tensor", None),
            P(None, "dp", "tensor", None),
            P(None, None, None, "tensor"),
            P(None, "tensor", None),
            P(None, None, "tensor"),
            P(None, "tensor", None),
            P(),
            P(),
            P(),
            P(),
        ),
        check_vma=False,
    )
```

```python
from functools import partial

import jax
import jax.numpy as jnp
from jax import lax
from jax.experimental import pallas as pl
from jax.experimental.pallas import tpu as pltpu
from jax.sharding import PartitionSpec as P

HEAD_DIM = 64


norm_eps = 1e-05
masked_score = -1000000000.0
contract_rows = (((0,), (0,)), ((), ()))
contract_cols = (((1,), (1,)), ((), ()))


def plain_norm(inputs):
    centered = inputs - jnp.mean(inputs, axis=-1, keepdims=True)
    variance = jnp.mean(centered * centered, axis=-1, keepdims=True)
    return centered * lax.rsqrt(variance + norm_eps)


def fixed_norm(inputs, gain_row, shift_row):
    return plain_norm(inputs) * gain_row + shift_row


def section_norm(inputs, scale_table, shift_table, picker):
    scale_row = jnp.dot(
        picker, scale_table, precision=lax.Precision.HIGHEST, preferred_element_type=jnp.float32
    )
    shift_row = jnp.dot(
        picker, shift_table, precision=lax.Precision.HIGHEST, preferred_element_type=jnp.float32
    )
    return plain_norm(inputs) * scale_row + shift_row


def gather_normed(normed_low):
    return lax.all_gather(normed_low, "tensor", axis=0, tiled=True)


def gather_again(normed_low):
    return lax.all_gather(normed_low, "tensor", axis=0, tiled=True)


def sum_branch(branch_part):
    return lax.psum_scatter(
        branch_part.astype(jnp.bfloat16), "tensor", scatter_dimension=0, tiled=True
    ).astype(jnp.float32)


def gather_grad(grad_low):
    return lax.all_gather(grad_low, "tensor", axis=0, tiled=True)


def sum_normed(grad_part):
    return lax.psum_scatter(
        grad_part.astype(jnp.bfloat16), "tensor", scatter_dimension=0, tiled=True
    ).astype(jnp.float32)


def key_allowed(query_pos, key_pos, prefix, valid_count, causal):
    allowed = key_pos[None, :] < valid_count
    if causal:
        allowed = allowed & ((key_pos[None, :] < prefix) | (key_pos[None, :] <= query_pos[:, None]))
    return allowed


def split_heads(projected):
    length = projected.shape[0]
    head_width = projected.shape[1] // 3
    head_count = head_width // HEAD_DIM
    query_rows = projected[:, :head_width].reshape(length, head_count, HEAD_DIM)
    key_rows = projected[:, head_width : 2 * head_width].reshape(length, head_count, HEAD_DIM)
    value_rows = projected[:, 2 * head_width :].reshape(length, head_count, HEAD_DIM)
    return (query_rows, key_rows, value_rows)


def block_scores(query_block, key_rows, block_start, prefix, valid_count, causal):
    block_rows = query_block.shape[0]
    length = key_rows.shape[0]
    scores = jnp.einsum(
        "qhd,khd->hqk", query_block, key_rows, preferred_element_type=jnp.float32
    ) * HEAD_DIM ** (-0.5)
    query_pos = block_start + lax.iota(jnp.int32, block_rows)
    key_pos = lax.iota(jnp.int32, length)
    allowed = key_allowed(query_pos, key_pos, prefix, valid_count, causal)
    return jnp.where(allowed[None], scores, masked_score)


def attend_forward(projected, prefix, valid_count, causal, block_rows):
    length = projected.shape[0]
    head_width = projected.shape[1] // 3
    query_rows, key_rows, value_rows = split_heads(projected)

    def one_block(block_start):
        query_block = lax.dynamic_slice_in_dim(query_rows, block_start, block_rows, 0)
        scores = block_scores(query_block, key_rows, block_start, prefix, valid_count, causal)
        highest = jnp.max(scores, axis=-1, keepdims=True)
        row_total = jnp.sum(jnp.exp(scores - highest), axis=-1, keepdims=True)
        log_total = highest + jnp.log(row_total)
        shares = jnp.exp(scores - log_total).astype(jnp.bfloat16)
        mixture = jnp.einsum("hqk,khd->qhd", shares, value_rows, preferred_element_type=jnp.float32)
        return (mixture.astype(jnp.bfloat16), log_total)

    starts = lax.iota(jnp.int32, length // block_rows) * block_rows
    mixture, log_totals = lax.map(one_block, starts)
    return (mixture.reshape(length, head_width), log_totals)


def attend_backward(projected, log_totals, grad_mixture, prefix, valid_count, causal, block_rows):
    length = projected.shape[0]
    head_width = projected.shape[1] // 3
    query_rows, key_rows, value_rows = split_heads(projected)
    grad_rows = grad_mixture.reshape(query_rows.shape)
    score_scale = HEAD_DIM ** (-0.5)

    def one_block(grad_state, block_item):
        block_start, log_total = block_item
        grad_key, grad_value = grad_state
        query_block = lax.dynamic_slice_in_dim(query_rows, block_start, block_rows, 0)
        grad_block = lax.dynamic_slice_in_dim(grad_rows, block_start, block_rows, 0)
        scores = block_scores(query_block, key_rows, block_start, prefix, valid_count, causal)
        shares = jnp.exp(scores - log_total)
        shares_low = shares.astype(jnp.bfloat16)
        grad_shares = jnp.einsum(
            "qhd,khd->hqk", grad_block, value_rows, preferred_element_type=jnp.float32
        )
        inner_sum = jnp.sum(shares * grad_shares, axis=-1, keepdims=True)
        grad_scores = (shares * (grad_shares - inner_sum)).astype(jnp.bfloat16)
        grad_query = (
            jnp.einsum("hqk,khd->qhd", grad_scores, key_rows, preferred_element_type=jnp.float32)
            * score_scale
        )
        grad_key = (
            grad_key
            + jnp.einsum(
                "hqk,qhd->khd", grad_scores, query_block, preferred_element_type=jnp.float32
            )
            * score_scale
        )
        grad_value = grad_value + jnp.einsum(
            "hqk,qhd->khd", shares_low, grad_block, preferred_element_type=jnp.float32
        )
        return ((grad_key, grad_value), grad_query)

    starts = lax.iota(jnp.int32, length // block_rows) * block_rows
    zero_rows = jnp.zeros(query_rows.shape, jnp.float32)
    grad_state, grad_query = lax.scan(one_block, (zero_rows, zero_rows), (starts, log_totals))
    grad_key, grad_value = grad_state
    joined = jnp.concatenate(
        [
            grad_query.reshape(length, head_width),
            grad_key.reshape(length, head_width),
            grad_value.reshape(length, head_width),
        ],
        axis=1,
    )
    return joined.astype(jnp.bfloat16)


def grouped_device(
    frames_in,
    phone_len,
    frame_len,
    section,
    norm_gain,
    norm_bias,
    ada_scale,
    ada_shift,
    w_qkv,
    w_out,
    w_up,
    w_down,
    out_grad,
):
    micro_count, local_seqs, local_rows, model_width = frames_in.shape
    seq_length = local_rows * lax.axis_size("tensor")
    block_rows = min(512, seq_length)
    section_count = ada_scale.shape[1]
    qkv_mats = [w_qkv[layer_index].reshape(model_width, -1) for layer_index in range(2)]
    acc_qkv = [jnp.zeros(qkv_mats[layer_index].shape, jnp.float32) for layer_index in range(2)]
    acc_out = [jnp.zeros(w_out.shape[1:], jnp.float32) for layer_index in range(2)]
    acc_up = [jnp.zeros(w_up.shape[1:], jnp.float32) for layer_index in range(2)]
    acc_down = [jnp.zeros(w_down.shape[1:], jnp.float32) for layer_index in range(2)]
    acc_gain = [jnp.zeros((model_width,), jnp.float32) for part_index in range(2)]
    acc_bias = [jnp.zeros((model_width,), jnp.float32) for part_index in range(2)]
    acc_scale = [jnp.zeros((section_count, model_width), jnp.float32) for part_index in range(2)]
    acc_shift = [jnp.zeros((section_count, model_width), jnp.float32) for part_index in range(2)]
    frames_list = []
    grads_list = []
    for micro_index in range(micro_count):
        prefix = phone_len[micro_index, 0]
        valid_count = prefix + frame_len[micro_index, 0]
        picker = (lax.iota(jnp.int32, section_count) == section[micro_index, 0]).astype(
            jnp.float32
        )[None, :]
        residual = frames_in[micro_index, 0].astype(jnp.float32)
        stored = []
        for layer_index in range(2):
            for part_index in range(2):
                if layer_index == 0:
                    normed, norm_back = jax.vjp(
                        fixed_norm, residual, norm_gain[part_index], norm_bias[part_index]
                    )
                else:
                    normed, norm_back = jax.vjp(
                        partial(section_norm, picker=picker),
                        residual,
                        ada_scale[part_index],
                        ada_shift[part_index],
                    )
                normed_low = normed.astype(jnp.bfloat16)
                gathered = gather_normed(normed_low)
                if part_index == 0:
                    projected = jnp.dot(
                        gathered, qkv_mats[layer_index], preferred_element_type=jnp.float32
                    ).astype(jnp.bfloat16)
                    mixture, log_totals = attend_forward(
                        projected, prefix, valid_count, layer_index == 0, block_rows
                    )
                    branch = sum_branch(
                        jnp.dot(mixture, w_out[layer_index], preferred_element_type=jnp.float32)
                    )
                    saved_state = (projected, log_totals, mixture)
                else:
                    hidden = jnp.dot(
                        gathered, w_up[layer_index], preferred_element_type=jnp.float32
                    )
                    active = jax.nn.gelu(hidden, approximate=True).astype(jnp.bfloat16)
                    branch = sum_branch(
                        jnp.dot(active, w_down[layer_index], preferred_element_type=jnp.float32)
                    )
                    saved_state = (hidden, active)
                kept_rows = normed_low
                stored.append((norm_back, kept_rows, saved_state))
                residual = residual + branch
        out_group = [residual]
        grad_rows = out_grad[micro_index, 0].astype(jnp.float32)
        for layer_index in (1, 0):
            for part_index in (1, 0):
                norm_back, kept_rows, saved_state = stored[2 * layer_index + part_index]
                gathered = gather_again(kept_rows)
                grad_whole = gather_grad(grad_rows.astype(jnp.bfloat16))
                if part_index == 1:
                    hidden, active = saved_state
                    acc_down[layer_index] = acc_down[layer_index] + lax.dot_general(
                        active, grad_whole, contract_rows, preferred_element_type=jnp.float32
                    )
                    grad_active = lax.dot_general(
                        grad_whole,
                        w_down[layer_index],
                        contract_cols,
                        preferred_element_type=jnp.float32,
                    )
                    gelu_value, gelu_back = jax.vjp(partial(jax.nn.gelu, approximate=True), hidden)
                    grad_hidden = gelu_back(grad_active)[0].astype(jnp.bfloat16)
                    acc_up[layer_index] = acc_up[layer_index] + lax.dot_general(
                        gathered, grad_hidden, contract_rows, preferred_element_type=jnp.float32
                    )
                    grad_normed = sum_normed(
                        lax.dot_general(
                            grad_hidden,
                            w_up[layer_index],
                            contract_cols,
                            preferred_element_type=jnp.float32,
                        )
                    )
                else:
                    projected, log_totals, mixture = saved_state
                    acc_out[layer_index] = acc_out[layer_index] + lax.dot_general(
                        mixture, grad_whole, contract_rows, preferred_element_type=jnp.float32
                    )
                    grad_mixture = lax.dot_general(
                        grad_whole,
                        w_out[layer_index],
                        contract_cols,
                        preferred_element_type=jnp.float32,
                    ).astype(jnp.bfloat16)
                    grad_projected = attend_backward(
                        projected,
                        log_totals,
                        grad_mixture,
                        prefix,
                        valid_count,
                        layer_index == 0,
                        block_rows,
                    )
                    acc_qkv[layer_index] = acc_qkv[layer_index] + lax.dot_general(
                        gathered, grad_projected, contract_rows, preferred_element_type=jnp.float32
                    )
                    grad_normed = sum_normed(
                        lax.dot_general(
                            grad_projected,
                            qkv_mats[layer_index],
                            contract_cols,
                            preferred_element_type=jnp.float32,
                        )
                    )
                grad_input, grad_first, grad_second = norm_back(grad_normed)
                grad_rows = grad_rows + grad_input
                if layer_index == 0:
                    acc_gain[part_index] = acc_gain[part_index] + grad_first
                    acc_bias[part_index] = acc_bias[part_index] + grad_second
                else:
                    acc_scale[part_index] = acc_scale[part_index] + grad_first
                    acc_shift[part_index] = acc_shift[part_index] + grad_second
        grad_group = [grad_rows]
        frames_list.append(jnp.stack(out_group))
        grads_list.append(jnp.stack(grad_group))
    total_qkv, total_out, total_up, total_down = (
        lax.psum(jnp.stack(acc_qkv).astype(jnp.bfloat16), "dp").astype(jnp.float32),
        lax.psum(jnp.stack(acc_out).astype(jnp.bfloat16), "dp").astype(jnp.float32),
        lax.psum(jnp.stack(acc_up).astype(jnp.bfloat16), "dp").astype(jnp.float32),
        lax.psum(jnp.stack(acc_down).astype(jnp.bfloat16), "dp").astype(jnp.float32),
    )
    norm_totals = lax.psum(
        (jnp.stack(acc_gain), jnp.stack(acc_bias), jnp.stack(acc_scale), jnp.stack(acc_shift)),
        ("dp", "tensor"),
    )
    return (
        jnp.stack(frames_list),
        jnp.stack(grads_list),
        total_qkv.reshape(2, model_width, 3, -1),
        total_out,
        total_up,
        total_down,
        norm_totals[0],
        norm_totals[1],
        norm_totals[2],
        norm_totals[3],
    )


bf16,f32=jnp.bfloat16,jnp.float32
NT=(((1,),(1,)),((),()))
TN=(((0,),(0,)),((),()))

def _limits(lims_ref, start, rows, causal, axis):
    prefix, valid = lims_ref[0], lims_ref[1]
    shape=(rows,1) if axis==0 else (1,rows)
    pos=start+lax.broadcasted_iota(jnp.int32,shape,axis)
    if causal:
        return jnp.minimum(jnp.maximum(pos,prefix-1),valid-1)
    return jnp.zeros(shape,jnp.int32)+(valid-1)

def fwd_kernel(causal, bq, lims_ref, q_ref, k_ref, v_ref, o_ref, l_ref):
    length=q_ref.shape[0]
    lane=lax.broadcasted_iota(jnp.int32,(bq,128),1)
    def block(start, kk):
        q=q_ref[pl.ds(start,bq),:]*jnp.asarray(0.125,bf16)
        lim=_limits(lims_ref,start,bq,causal,0)
        outs=[];rows=[]
        for h in range(2):
            qm=jnp.where((lane<HEAD_DIM)==(h==0),q,jnp.zeros_like(q))
            s=lax.dot_general(qm,k_ref[0:kk,:],NT,preferred_element_type=f32)
            key=lax.broadcasted_iota(jnp.int32,(bq,kk),1)
            s=jnp.where(key<=lim,s,-1e9)
            m=jnp.max(s,axis=1,keepdims=True)
            e=jnp.exp(s-m)
            l=jnp.sum(e,axis=1,keepdims=True)
            o=jnp.dot(e.astype(bf16),v_ref[0:kk,:],preferred_element_type=f32)*(1.0/l)
            outs.append(o); rows.append(m+jnp.log(l))
        o_ref[pl.ds(start,bq),:]=jnp.where(lane<HEAD_DIM,outs[0],outs[1]).astype(bf16)
        both=jnp.where(lane<HEAD_DIM,rows[0],rows[1])
        bt=both.T
        l_ref[0,0:1,pl.ds(start,bq)]=bt[0:1,:]
        l_ref[0,1:2,pl.ds(start,bq)]=bt[HEAD_DIM:HEAD_DIM+1,:]
    nq=length//bq
    if causal:
        for i in range(nq): block(i*bq,(i+1)*bq)
    else:
        def body(i,c):
            block(pl.multiple_of(i*bq,bq),length); return c
        lax.fori_loop(0,nq,body,0)

def attn_fwd(qkv, lims, causal, bq=256):
    length=qkv.shape[0]; width=qkv.shape[1]//3; pairs=width//128
    spec=lambda off: pl.BlockSpec((length,128),lambda i,off=off:(0,off*pairs+i))
    return pl.pallas_call(partial(fwd_kernel,causal,bq),
        grid=(pairs,),
        in_specs=[pl.BlockSpec(memory_space=pltpu.SMEM),spec(0),spec(1),spec(2)],
        out_specs=[pl.BlockSpec((length,128),lambda i:(0,i)),pl.BlockSpec((1,2,length),lambda i:(i,0,0))],
        out_shape=[jax.ShapeDtypeStruct((length,width),bf16),jax.ShapeDtypeStruct((pairs,2,length),f32)],
        compiler_params=pltpu.CompilerParams(vmem_limit_bytes=48*2**20),
        cost_estimate=pl.CostEstimate(flops=pairs*2**20,bytes_accessed=length*width*8,transcendentals=0),
        name="attn_fwd_"+("causal" if causal else "full"),
    )(lims,qkv,qkv,qkv)

def bwd_kernel(causal,bq,lims_ref,q_ref,k_ref,v_ref,l_ref,do_ref,grad_ref,dk_acc,dv_acc):
    length=q_ref.shape[0]
    lane=lax.broadcasted_iota(jnp.int32,(bq,128),1)
    dk_acc[...]=jnp.zeros_like(dk_acc); dv_acc[...]=jnp.zeros_like(dv_acc)
    width=grad_ref.shape[1]//3
    at=[pl.multiple_of(part*width+pl.program_id(0)*128,128) for part in range(3)]
    def block(start,kk):
        q=q_ref[pl.ds(start,bq),:]*jnp.asarray(0.125,bf16)
        do=do_ref[pl.ds(start,bq),:]
        lim=_limits(lims_ref,start,bq,causal,1)
        dqs=[]
        for h in range(2):
            sel=(lane<HEAD_DIM)==(h==0)
            qm=jnp.where(sel,q,jnp.zeros_like(q)); dom=jnp.where(sel,do,jnp.zeros_like(do))
            s=lax.dot_general(k_ref[0:kk,:],qm,NT,preferred_element_type=f32)
            dp=lax.dot_general(v_ref[0:kk,:],dom,NT,preferred_element_type=f32)
            key=lax.broadcasted_iota(jnp.int32,(kk,bq),0)
            lrow=l_ref[0,h:h+1,pl.ds(start,bq)]
            p=jnp.where(key<=lim,jnp.exp(s-lrow),0.0)
            pd=p*dp
            D=jnp.sum(pd,axis=0,keepdims=True)
            ds=(pd-p*D).astype(bf16)
            dv_acc[0:kk,:]+=jnp.dot(p.astype(bf16),dom,preferred_element_type=f32)
            dk_acc[0:kk,:]+=jnp.dot(ds,qm,preferred_element_type=f32)
            dqs.append(lax.dot_general(ds,k_ref[0:kk,:],TN,preferred_element_type=f32))
        grad_ref[pl.ds(start,bq),pl.ds(at[0],128)]=(jnp.where(lane<HEAD_DIM,dqs[0],dqs[1])*0.125).astype(bf16)
    nq=length//bq
    if causal:
        for i in range(nq): block(i*bq,(i+1)*bq)
    else:
        def body(i,c):
            block(pl.multiple_of(i*bq,bq),length); return c
        lax.fori_loop(0,nq,body,0)
    grad_ref[:,pl.ds(at[1],128)]=dk_acc[...].astype(bf16)
    grad_ref[:,pl.ds(at[2],128)]=dv_acc[...].astype(bf16)

def attn_bwd(qkv,L,do,lims,causal,bq=256):
    length=qkv.shape[0]; width=qkv.shape[1]//3; pairs=width//128
    spec=lambda off: pl.BlockSpec((length,128),lambda i,off=off:(0,off*pairs+i))
    one=pl.BlockSpec((length,128),lambda i:(0,i))
    return pl.pallas_call(partial(bwd_kernel,causal,bq),
        grid=(pairs,),
        in_specs=[pl.BlockSpec(memory_space=pltpu.SMEM),spec(0),spec(1),spec(2),pl.BlockSpec((1,2,length),lambda i:(i,0,0)),one],
        out_specs=pl.BlockSpec((length,3*width),lambda i:(0,0)),
        out_shape=jax.ShapeDtypeStruct((length,3*width),bf16),
        scratch_shapes=[pltpu.VMEM((length,128),f32)]*2,
        compiler_params=pltpu.CompilerParams(vmem_limit_bytes=48*2**20),
        cost_estimate=pl.CostEstimate(flops=pairs*2**20,bytes_accessed=length*width*8,transcendentals=0),
        name="attn_bwd_"+("causal" if causal else "full"),
    )(lims,qkv,qkv,qkv,L,do)


def pin(*values):
    return lax.optimization_barrier(values)


def swap_tensor(block):
    return lax.ppermute(block, "tensor", [(0, 1), (1, 0)])


def swap_bit(block, bit, dp_size):
    return lax.ppermute(block, "dp", [(place, place ^ (1 << bit)) for place in range(dp_size)])


def in_order(flag, mine, other):
    first = jnp.where(flag == 0, mine, other)
    second = jnp.where(flag == 0, other, mine)
    return jnp.concatenate([first, second], axis=0)


def add_rounded(left, right):
    return (left.astype(f32) + right.astype(f32)).astype(bf16)


def norm_forward(rows, gain_row, shift_row):
    mean = jnp.mean(rows, axis=-1, keepdims=True)
    centered = rows - mean
    rate = lax.rsqrt(jnp.mean(centered * centered, axis=-1, keepdims=True) + norm_eps)
    normed = centered * rate * gain_row + shift_row
    return normed.astype(bf16), (rows, mean, rate)


def norm_backward(saved, grad_normed, gain_row):
    rows, mean, rate = saved
    unit = (rows - mean) * rate
    grad_unit = grad_normed * gain_row
    grad_rows = rate * (
        grad_unit
        - jnp.mean(grad_unit, axis=-1, keepdims=True)
        - unit * jnp.mean(grad_unit * unit, axis=-1, keepdims=True)
    )
    return grad_rows, jnp.sum(grad_normed * unit, axis=0), jnp.sum(grad_normed, axis=0)


def gelu_pair(hidden):
    square = hidden * hidden
    share = 0.5 + 0.5 * jnp.tanh(hidden * (0.7978845608 + (0.7978845608 * 0.044715) * square))
    value = hidden * share
    rate = 2.0 * 0.7978845608 + (6.0 * 0.7978845608 * 0.044715) * square
    slope = share + (value * rate) * (1.0 - share)
    return value.astype(bf16), slope.astype(bf16)


def dot_sum(pairs, dims):
    total = None
    for left, right in pairs:
        term = lax.dot_general(left, right, dims, preferred_element_type=f32)
        total = term if total is None else total + term
    return total


def dot_low(left, right, dims):
    return lax.dot_general(left, right, dims, preferred_element_type=f32).astype(bf16)


NN = (((1,), (0,)), ((), ()))
SPLIT_AXIS = {"up": 1, "down": 0}
PACK_WIDTH = 512


def quarter_of(kind, half, place):
    axis = SPLIT_AXIS[kind]
    width = half.shape[axis] // 2
    return lax.dynamic_slice_in_dim(half, place * width, width, axis)


def row_half(block, place):
    height = block.shape[0] // 2
    return lax.dynamic_slice_in_dim(block, place * height, height, 0)


def flat_kernel(in_ref, out_ref):
    width = in_ref.shape[3]
    for part in range(3):
        out_ref[:, part * width : (part + 1) * width] = in_ref[0, part]


def flat_qkv(stacked, layer):
    _, _, height, width = stacked.shape
    rows = height // 2
    return pl.pallas_call(
        flat_kernel,
        grid=(2,),
        in_specs=[pl.BlockSpec((1, 3, rows, width), lambda step: (layer, 0, step, 0))],
        out_specs=pl.BlockSpec((rows, 3 * width), lambda step: (step, 0)),
        out_shape=jax.ShapeDtypeStruct((height, 3 * width), bf16),
        cost_estimate=pl.CostEstimate(flops=0, bytes_accessed=12 * height * width, transcendentals=0),
        name="flat_qkv",
    )(stacked)


def pack_kernel(kinds, place_ref, *refs):
    out_ref = refs[-1]
    at = 0
    for kind, ref in zip(kinds, refs):
        if kind == "qkv":
            pieces = [ref[0, part] for part in range(3)]
        else:
            count = ref.shape[2] // PACK_WIDTH
            pieces = [ref[0, :, part * PACK_WIDTH : (part + 1) * PACK_WIDTH] for part in range(count)]
        for piece in pieces:
            out_ref[at : at + piece.shape[0], :] = piece
            at += piece.shape[0]


def pack_pieces(place, layer, dp_size, kinds, arrays):
    specs, total = [], 0
    for kind, array in zip(kinds, arrays):
        height, width = array.shape[-2:]
        rows = height // dp_size
        if kind == "qkv":
            specs.append(pl.BlockSpec((1, 3, rows, width), lambda step, at: (layer, 0, at[0], 0)))
            total += 3 * rows * width // PACK_WIDTH
        else:
            specs.append(pl.BlockSpec((1, rows, width), lambda step, at: (layer, at[0], 0)))
            total += rows * width // PACK_WIDTH
    return pl.pallas_call(
        partial(pack_kernel, kinds),
        grid_spec=pltpu.PrefetchScalarGridSpec(
            num_scalar_prefetch=1,
            grid=(1,),
            in_specs=specs,
            out_specs=pl.BlockSpec((total, PACK_WIDTH), lambda step, at: (0, 0)),
        ),
        out_shape=jax.ShapeDtypeStruct((total, PACK_WIDTH), bf16),
        cost_estimate=pl.CostEstimate(flops=0, bytes_accessed=4 * total * PACK_WIDTH, transcendentals=0),
        name="pack_pieces",
    )(place.reshape(1).astype(jnp.int32), *arrays)


def unpack_kernel(in_ref, *refs):
    at = 0
    for ref in refs:
        rows = ref.shape[0] // in_ref.shape[0]
        for part in range(ref.shape[1] // PACK_WIDTH):
            for block in range(in_ref.shape[0]):
                ref[block * rows : (block + 1) * rows, part * PACK_WIDTH : (part + 1) * PACK_WIDTH] = in_ref[
                    block, at : at + rows, :
                ]
            at += rows


def unpack_halves(gathered, shapes):
    dp_size, total, _ = gathered.shape
    some = max(1, dp_size // 4)
    return pl.pallas_call(
        unpack_kernel,
        grid=(dp_size // some,),
        in_specs=[pl.BlockSpec((some, total, PACK_WIDTH), lambda step: (step, 0, 0))],
        out_specs=[
            pl.BlockSpec((height // dp_size * some, width), lambda step: (step, 0)) for height, width in shapes
        ],
        out_shape=[jax.ShapeDtypeStruct(shape, bf16) for shape in shapes],
        compiler_params=pltpu.CompilerParams(vmem_limit_bytes=32 * 2**20),
        cost_estimate=pl.CostEstimate(
            flops=0, bytes_accessed=4 * dp_size * total * PACK_WIDTH, transcendentals=0
        ),
        name="unpack_halves",
    )(gathered)


def stack_kernel(steps, side_ref, down_own, up_own, down_other, up_other, out_ref):
    blocks, rows = out_ref.shape[0], out_ref.shape[1] // 2

    def write(down_ref, up_ref):
        for block in range(blocks):
            out_ref[block, :rows] = down_ref[block * rows : (block + 1) * rows]
            out_ref[block, rows:] = up_ref[block * rows : (block + 1) * rows]

    pl.when(pl.program_id(0) < steps)(lambda: write(down_own, up_own))
    pl.when(pl.program_id(0) >= steps)(lambda: write(down_other, up_other))


def stack_pair(side, dp_size, down_parts, up_parts):
    height, width = down_parts[0].shape
    steps = 4
    rows, some = height // dp_size, dp_size // steps
    own = pl.BlockSpec((some * rows, width), lambda step, side_ref: (jnp.minimum(step, steps - 1), 0))
    other = pl.BlockSpec((some * rows, width), lambda step, side_ref: (jnp.maximum(step - steps, 0), 0))

    def target(step, side_ref):
        half = jnp.where(step < steps, side_ref[0], 1 - side_ref[0])
        return (half * steps + step % steps, 0, 0)

    return pl.pallas_call(
        partial(stack_kernel, steps),
        grid_spec=pltpu.PrefetchScalarGridSpec(
            num_scalar_prefetch=1,
            grid=(2 * steps,),
            in_specs=[own, own, other, other],
            out_specs=pl.BlockSpec((some, 2 * rows, width), target),
        ),
        out_shape=jax.ShapeDtypeStruct((2 * dp_size, 2 * rows, width), bf16),
        compiler_params=pltpu.CompilerParams(vmem_limit_bytes=32 * 2**20),
        cost_estimate=pl.CostEstimate(flops=0, bytes_accessed=16 * height * width, transcendentals=0),
        name="stack_pair",
    )(side.reshape(1).astype(jnp.int32), down_parts[0], up_parts[0], down_parts[1], up_parts[1])


def place_joint_kernel(whole_ref, *refs):
    qkv_out, out_out = refs[-2:]
    for block in range(whole_ref.shape[0]):
        rows = qkv_out.shape[2] // whole_ref.shape[0]
        for part in range(3):
            qkv_out[0, part, block * rows : (block + 1) * rows, :] = whole_ref[
                block, part * rows : (part + 1) * rows, :
            ].astype(f32)
        at, rows = 3 * rows, out_out.shape[1] // whole_ref.shape[0]
        for part in range(out_out.shape[2] // PACK_WIDTH):
            out_out[0, block * rows : (block + 1) * rows, part * PACK_WIDTH : (part + 1) * PACK_WIDTH] = whole_ref[
                block, at + part * rows : at + (part + 1) * rows, :
            ].astype(f32)


def place_joint(whole, layer, qkv_shape, out_shape, bases):
    dp_size, total, _ = whole.shape
    some = dp_size // 4
    operands, in_specs, aliases = [whole], [pl.BlockSpec((some, total, PACK_WIDTH), lambda step: (step, 0, 0))], {}
    if bases is not None:
        operands += bases
        in_specs += [pl.BlockSpec(memory_space=pl.ANY)] * 2
        aliases = {1: 0, 2: 1}
    return pl.pallas_call(
        place_joint_kernel,
        grid=(4,),
        in_specs=in_specs,
        out_specs=[
            pl.BlockSpec((1, 3, qkv_shape[0] // 4, qkv_shape[1] // 3), lambda step: (layer, 0, step, 0)),
            pl.BlockSpec((1, out_shape[0] // 4, out_shape[1]), lambda step: (layer, step, 0)),
        ],
        out_shape=[
            jax.ShapeDtypeStruct((2, 3, qkv_shape[0], qkv_shape[1] // 3), f32),
            jax.ShapeDtypeStruct((2,) + tuple(out_shape), f32),
        ],
        input_output_aliases=aliases,
        compiler_params=pltpu.CompilerParams(vmem_limit_bytes=32 * 2**20),
        cost_estimate=pl.CostEstimate(flops=0, bytes_accessed=6 * dp_size * total * PACK_WIDTH, transcendentals=0),
        name="place_joint",
    )(*operands)


def place_pair_kernel(whole_ref, up_out, down_out):
    for block in range(whole_ref.shape[0]):
        rows = whole_ref.shape[2]
        down_out[0, block * rows : (block + 1) * rows, :] = whole_ref[block, 0].astype(f32)
        up_out[0, :, block * rows : (block + 1) * rows] = whole_ref[block, 1].astype(f32).T


def place_pair(whole, layer):
    dp_size, rows, columns = whole.shape
    rows = rows // 2
    some = dp_size // 4
    return pl.pallas_call(
        place_pair_kernel,
        grid=(4,),
        in_specs=[pl.BlockSpec((some, 2, rows, columns), lambda step: (step, 0, 0, 0))],
        out_specs=[
            pl.BlockSpec((1, columns, some * rows), lambda step: (layer, 0, step)),
            pl.BlockSpec((1, some * rows, columns), lambda step: (layer, step, 0)),
        ],
        out_shape=[
            jax.ShapeDtypeStruct((2, columns, dp_size * rows), f32),
            jax.ShapeDtypeStruct((2, dp_size * rows, columns), f32),
        ],
        compiler_params=pltpu.CompilerParams(vmem_limit_bytes=40 * 2**20),
        cost_estimate=pl.CostEstimate(flops=0, bytes_accessed=12 * dp_size * rows * columns, transcendentals=0),
        name="place_pair",
    )(whole.reshape(dp_size, 2, rows, columns))


def place_kernel(whole_ref, *refs):
    out_ref = refs[-1]
    out_ref[0] = whole_ref[...].reshape(-1, whole_ref.shape[-1]).astype(f32)


def place_quarters(kind, whole, which, layer, base):
    dp_size, rows, columns = whole.shape
    half, some, rows = dp_size // 2, dp_size // 4, rows // 2
    if kind == "down":
        out_spec = pl.BlockSpec((1, some * rows, columns), lambda step: (layer, step, 0))
    else:
        out_spec = pl.BlockSpec((1, some * rows, columns), lambda step: (layer, step % 2, step // 2))
    return pl.pallas_call(
        place_kernel,
        grid=(4,),
        in_specs=[
            pl.BlockSpec(
                (some, None, None, rows, columns), lambda step: (step % 2, step // 2, which, 0, 0)
            ),
            pl.BlockSpec(memory_space=pl.ANY),
        ],
        out_specs=out_spec,
        out_shape=jax.ShapeDtypeStruct(base.shape, f32),
        input_output_aliases={1: 0},
        compiler_params=pltpu.CompilerParams(vmem_limit_bytes=32 * 2**20),
        cost_estimate=pl.CostEstimate(flops=0, bytes_accessed=6 * dp_size * rows * columns, transcendentals=0),
        name="place_" + kind,
    )(whole.reshape(half, 2, 2, rows, columns), base)


def frame_kernel(side_ref, mine_ref, other_ref, out_ref):
    own = pl.program_id(0) == side_ref[0]
    out_ref[0, 0] = jnp.where(own, mine_ref[...], other_ref[...].astype(f32))


def place_frames(side, mine, other):
    height, width = mine.shape
    rows = height // 2
    spec = pl.BlockSpec((rows, width), lambda slot, step, side_ref: (step, 0))
    return pl.pallas_call(
        frame_kernel,
        grid_spec=pltpu.PrefetchScalarGridSpec(
            num_scalar_prefetch=1,
            grid=(2, 2),
            in_specs=[spec, spec],
            out_specs=pl.BlockSpec((1, 1, rows, width), lambda slot, step, side_ref: (slot, 0, step, 0)),
        ),
        out_shape=jax.ShapeDtypeStruct((2, 1, height, width), f32),
        name="place_frames",
    )(side.reshape(1).astype(jnp.int32), mine, other)


def take_axis(block, index):
    return lax.dynamic_index_in_dim(block, index, 1, keepdims=False)


def flat_rows(block):
    return block.reshape(-1, block.shape[-1])


def join_level(here, kept, arrived):
    first = jnp.where(here == 0, kept, arrived)
    second = jnp.where(here == 0, arrived, kept)
    joined = jnp.stack([first, second], axis=1)
    return joined.reshape((-1,) + joined.shape[2:])


class Chain:
    def __init__(self, place, dp_size, rows, columns, kind, gather):
        self.place, self.dp_size, self.kind, self.gather = place, dp_size, kind, gather
        self.rows, self.columns = rows, columns
        self.bit_count = dp_size.bit_length() - 1
        self.flight = []

    def bit(self, index):
        return (self.place >> index) & 1

    def swap(self, block, bit):
        return swap_bit(block, bit, self.dp_size)

    def pair(self, block):
        return block.reshape(-1, 2, self.rows, self.columns)

    def start(self, near, far, ours=None, own_far=None):
        self.near, self.ours = near, ours
        self.flight = [self.swap(far, 0)] + ([] if ours is None else [self.swap(own_far, 0)])
        self.state = "core"

    def start_rows(self, own, other):
        self.start_other(other)
        self.add_own(own)

    def start_other(self, other):
        split, core = self.pair(other), self.bit(0)
        self.start(flat_rows(take_axis(split, core)), flat_rows(take_axis(split, 1 - core)))

    def add_own(self, own):
        split, core = self.pair(own), self.bit(0)
        self.flight = self.flight + [self.swap(flat_rows(take_axis(split, 1 - core)), 0)]
        self.ours = flat_rows(take_axis(split, core))

    def halves(self, block, bit):
        split, here = self.pair(block), self.bit(bit)
        return flat_rows(take_axis(split, here)), flat_rows(take_axis(split, 1 - here))

    def settle(self, arrived):
        self.near_here, self.near_away = self.halves(add_rounded(self.near, arrived[0]), 1)
        if self.ours is not None:
            self.kept_here, self.kept_away = self.halves(add_rounded(self.ours, arrived[1]), 1)
        self.flight, self.state = [], "ready"

    def launch(self):
        self.flight = [swap_tensor(self.near_away) if self.kind == "x" else self.swap(self.near_away, 1)]
        self.state = "first"

    def second(self, arrived):
        if len(arrived) > 1:
            self.kept_here, self.kept_away = self.halves(add_rounded(self.ours, arrived[1]), 1)
        if self.kind == "x":
            self.kept_away = add_rounded(self.kept_away, arrived[0])
        else:
            self.near_here = add_rounded(self.near_here, arrived[0])
        self.flight = [swap_tensor(self.near_here), self.swap(self.kept_away, 1)]
        self.state = "second"

    def next_bit(self, total, index):
        if index == self.bit_count:
            self.kept, self.state = total, "gather"
            if self.gather == "native":
                self.flight = [lax.all_gather(total, "dp", axis=0, tiled=False)]
                return
            if self.gather is None:
                self.flight, self.state = [], "done"
                return
            self.kept, self.level = total[None], index - 1
            self.flight = [self.swap(self.kept, self.level)]
            return
        self.kept, away = self.halves(total, index)
        self.flight, self.index, self.state = [self.swap(away, index)], index, "bits"

    def advance(self, arrived, hold=False):
        if self.state == "done":
            return
        if self.state == "core":
            self.settle(arrived)
            if not hold:
                self.launch()
        elif self.state == "ready":
            self.launch()
        elif self.state == "first":
            self.second(arrived)
        elif self.state == "second":
            total = self.kept_here.astype(f32) + arrived[0].astype(f32) + arrived[1].astype(f32)
            self.next_bit(total.astype(bf16), 2)
        elif self.state == "bits":
            self.next_bit(add_rounded(self.kept, arrived[0]), self.index + 1)
        elif self.gather == "native":
            self.whole, self.flight, self.state = arrived[0], [], "done"
        else:
            self.kept = join_level(self.bit(self.level), self.kept, arrived[0])
            self.level -= 1
            if self.level < 0:
                self.whole, self.flight, self.state = self.kept, [], "done"
            else:
                self.flight = [self.swap(self.kept, self.level)]


class Scatter:
    def __init__(self, block):
        self.flight = [lax.psum_scatter(block, ("tensor", "dp"), scatter_dimension=0, tiled=True)]
        self.state = "sum"

    def advance(self, arrived):
        if self.state == "sum":
            self.flight, self.state = [lax.all_gather(arrived[0], "dp", axis=0, tiled=False)], "gather"
        elif self.state == "gather":
            self.whole, self.flight, self.state = arrived[0], [], "done"


class Gather:
    def __init__(self, qkv, out, width, native):
        assert qkv.state == "done" and out.state == "done"
        pieces = []
        for block in (qkv.kept, out.kept):
            for at in range(0, block.shape[1], width):
                pieces.append(lax.slice_in_dim(block, at, at + width, axis=1))
        self.kept = jnp.concatenate(pieces, axis=0)
        self.native, self.bit, self.swap = native, qkv.bit, qkv.swap
        self.state = "going"
        if native:
            self.flight = [lax.all_gather(self.kept, "dp", axis=0, tiled=False)]
        else:
            self.kept, self.level = self.kept[None], qkv.bit_count - 1
            self.flight = [self.swap(self.kept, self.level)]

    def advance(self, arrived):
        if self.state == "done":
            return
        if self.native:
            self.whole, self.flight, self.state = arrived[0], [], "done"
            return
        self.kept = join_level(self.bit(self.level), self.kept, arrived[0])
        self.level -= 1
        if self.level < 0:
            self.whole, self.flight, self.state = self.kept, [], "done"
        else:
            self.flight = [self.swap(self.kept, self.level)]


class Spread:
    def __init__(self, block, dp_size):
        self.block, self.dp_size = block, dp_size
        self.bits = list(range(dp_size.bit_length() - 1))
        self.flight = [swap_tensor(block)]

    def advance(self, arrived):
        if not arrived:
            return
        self.block = self.block + arrived[0]
        self.flight = [swap_bit(self.block, self.bits.pop(0), self.dp_size)] if self.bits else []


def move(state, *chains, hold=()):
    everyone = chains + tuple(hold)
    state, flights = pin(state, [one.flight for one in everyone])
    for one, flight in zip(everyone, flights):
        if one in hold:
            one.advance(flight, hold=True)
        else:
            one.advance(flight)
    return state


def paired_device(
    dp_size,
    frames_in,
    phone_len,
    frame_len,
    section,
    norm_gain,
    norm_bias,
    ada_scale,
    ada_shift,
    w_qkv,
    w_out,
    w_up,
    w_down,
    out_grad,
):
    model_width = frames_in.shape[3]
    section_count = ada_scale.shape[1]
    side = lax.axis_index("tensor")
    place = lax.axis_index("dp")
    core, near_row = place & 1, (place >> 1) & 1

    def away_rows(halves):
        return lax.dynamic_index_in_dim(halves[:, 0], 1 - side, 0, keepdims=False)

    def whole_rows(halves, other):
        mine = lax.dynamic_index_in_dim(halves[:, 0], side, 0, keepdims=False)
        return in_order(side, mine, other)

    prefix = lax.dynamic_index_in_dim(phone_len[:, 0], side, 0, keepdims=False)
    frames = lax.dynamic_index_in_dim(frame_len[:, 0], side, 0, keepdims=False)
    chosen = lax.dynamic_index_in_dim(section[:, 0], side, 0, keepdims=False)
    limits = jnp.stack([prefix, prefix + frames]).astype(jnp.int32)
    picker = (lax.iota(jnp.int32, section_count) == chosen).astype(f32)[:, None]

    gains = [
        [norm_gain[0], norm_gain[1]],
        [jnp.sum(picker * ada_scale[part], axis=0) for part in range(2)],
    ]
    shifts = [
        [norm_bias[0], norm_bias[1]],
        [jnp.sum(picker * ada_shift[part], axis=0) for part in range(2)],
    ]

    stacked = w_qkv.transpose(0, 2, 1, 3)
    arrays = {"qkv": stacked, "out": w_out, "up": w_up, "down": w_down}
    flat_shape = {
        "qkv": (model_width, 3 * stacked.shape[3]),
        "out": w_out.shape[1:],
        "up": w_up.shape[1:],
        "down": w_down.shape[1:],
    }

    def packed(layer, kinds):
        return pack_pieces(place, layer, dp_size, kinds, [arrays[kind] for kind in kinds])

    def gathered(arrived):
        return lax.all_gather(arrived, "dp", axis=0, tiled=False)

    def unpacked(whole, kinds):
        return dict(zip(kinds, unpack_halves(whole, [flat_shape[kind] for kind in kinds])))

    attn_kinds, hidden_kinds = ("qkv", "out"), ("up", "down")
    rows_away, first_send = pin(away_rows(frames_in), packed(0, attn_kinds))
    other_rows = swap_tensor(rows_away)
    first_pack = swap_tensor(first_send)
    own_qkv = [flat_qkv(stacked, layer) for layer in range(2)]
    first_pack, own_qkv = pin(first_pack, own_qkv)
    first_whole = gathered(first_pack)
    attn_send, hidden_send = packed(1, attn_kinds), packed(1, hidden_kinds)
    piece_rows, piece_columns = model_width // 2, w_up.shape[2] // 2
    up_send = lax.dynamic_slice(
        w_up, (0, near_row * piece_rows, core * piece_columns), (1, piece_rows, piece_columns)
    )[0]
    piece_rows = w_down.shape[1] // 4
    down_send = lax.dynamic_slice(
        w_down, (0, (2 * core + near_row) * piece_rows, 0), (1, piece_rows, model_width)
    )[0]
    other_rows, attn_send, hidden_send, up_send, down_send, own_qkv = pin(
        other_rows, attn_send, hidden_send, up_send, down_send, own_qkv
    )
    up_piece = swap_tensor(up_send)
    rows = whole_rows(frames_in, other_rows).astype(f32)
    normed, norm_kept = norm_forward(rows, gains[0][0], shifts[0][0])
    mine = dot_low(normed, own_qkv[0], NN)
    mix_mine = attn_fwd(mine, limits, True, 512)
    mix_mine, up_piece, attn_send, down_send = pin(mix_mine, up_piece, attn_send, down_send)
    attn_pack = swap_tensor(attn_send)
    up_there = swap_bit(up_piece, 1, dp_size)
    down_piece = swap_tensor(down_send)
    first = unpacked(first_whole, attn_kinds)
    theirs = dot_low(normed, first["qkv"], NN)
    mix_theirs = attn_fwd(theirs, limits, True, 512)
    mix_theirs, up_there, down_piece, hidden_send, attn_pack = pin(
        mix_theirs, up_there, down_piece, hidden_send, attn_pack
    )
    attn_whole = gathered(attn_pack)
    up_near = in_order(near_row, up_piece, up_there)
    up_far = swap_bit(up_near, 0, dp_size)
    down_there = swap_bit(down_piece, 1, dp_size)
    hidden_pack = swap_tensor(hidden_send)
    kept = [(normed, norm_kept, [mine, theirs], [mix_mine, mix_theirs])]
    rows = rows + dot_sum([(mix_mine[0], w_out[0]), (mix_theirs[0], first["out"])], NN)
    normed, norm_kept = norm_forward(rows, gains[0][1], shifts[0][1])
    pair_own = gelu_pair(jnp.dot(normed, w_up[0], preferred_element_type=f32))
    pair_own, up_far, normed, norm_kept, rows, hidden_pack = pin(
        pair_own, up_far, normed, norm_kept, rows, hidden_pack
    )
    hidden_whole = gathered(hidden_pack)
    pair_near = gelu_pair(jnp.dot(normed, up_near, preferred_element_type=f32))
    pair_far = gelu_pair(jnp.dot(normed, up_far, preferred_element_type=f32))
    rows = rows + dot_sum([(pair_own[0], w_down[0])], NN)
    rows, pair_near, pair_far, down_there = pin(rows, pair_near, pair_far, down_there)
    down_near = in_order(near_row, down_piece, down_there)
    down_far = swap_bit(down_near, 0, dp_size)
    grad_send = away_rows(out_grad)
    rows = rows + dot_sum([(pair_near[0], down_near)], NN)
    rows, grad_send, down_far = pin(rows, grad_send, down_far)
    grad_other = swap_tensor(grad_send)
    rows = rows + dot_sum([(pair_far[0], down_far)], NN)
    kept.append((normed, norm_kept, [pair_own, pair_near, pair_far]))

    normed, norm_kept = norm_forward(rows, gains[1][0], shifts[1][0])
    mine = dot_low(normed, own_qkv[1], NN)
    mix_mine = attn_fwd(mine, limits, False, 512)
    mix_mine, attn_whole = pin(mix_mine, attn_whole)
    second = unpacked(attn_whole, attn_kinds)
    theirs = dot_low(normed, second["qkv"], NN)
    mix_theirs = attn_fwd(theirs, limits, False, 512)
    mixed = [mix_mine, mix_theirs]
    kept.append((normed, norm_kept, [mine, theirs], mixed))
    rows = rows + dot_sum([(mix_mine[0], w_out[1]), (mix_theirs[0], second["out"])], NN)
    normed, norm_kept = norm_forward(rows, gains[1][1], shifts[1][1])
    pair_own = gelu_pair(jnp.dot(normed, w_up[1], preferred_element_type=f32))
    pair_own, rows, normed, norm_kept = pin(pair_own, rows, normed, norm_kept)
    rows = rows + dot_sum([(pair_own[0], w_down[1])], NN)
    rows, hidden_whole = pin(rows, hidden_whole)
    second.update(unpacked(hidden_whole, hidden_kinds))
    pair_other = gelu_pair(jnp.dot(normed, second["up"], preferred_element_type=f32))
    pair_other, rows = pin(pair_other, rows)
    rows = rows + dot_sum([(pair_other[0], second["down"])], NN)
    pairs = [pair_own, pair_other]
    kept.append((normed, norm_kept, pairs))
    weights = [
        {
            "qkv": [own_qkv[0], first["qkv"]],
            "out": [w_out[0], first["out"]],
            "up": [w_up[0], up_near, up_far],
            "down": [w_down[0], down_near, down_far],
        },
        {
            "qkv": [own_qkv[1], second["qkv"]],
            "out": [w_out[1], second["out"]],
            "up": [w_up[1], second["up"]],
            "down": [w_down[1], second["down"]],
        },
    ]
    rows, grad_other = pin(rows, grad_other)

    def halves_of(block):
        height = block.shape[0] // 2
        mine = lax.dynamic_slice_in_dim(block, side * height, height, 0)
        away = lax.dynamic_slice_in_dim(block, (1 - side) * height, height, 0)
        return mine, away.astype(bf16)

    out_mine, out_away = halves_of(rows)

    norm_sums = [[None, None], [None, None]]
    grad_rows = whole_rows(out_grad, grad_other).astype(f32)
    def chain(kind, first, gather, split="rows"):
        height, width = flat_shape[kind]
        if split == "core":
            count = dp_size // 2
            height, width = (height, width // 2) if kind == "up" else (height // 2, width)
        else:
            count = dp_size
        return Chain(place, dp_size, height // count, width, first, gather)

    def start_quarters(one, kind, parts):
        own, near, far = parts
        one.start(near, far, quarter_of(kind, own, core), quarter_of(kind, own, 1 - core))

    def hidden_grads(layer, low):
        pairs = kept[2 * layer + 1][2]
        return [
            (
                lax.dot_general(low, part, NT, preferred_element_type=f32) * pair[1].astype(f32)
            ).astype(bf16)
            for pair, part in zip(pairs, weights[layer]["down"])
        ]

    def down_grads(layer, low):
        return [dot_low(pair[0], low, TN) for pair in kept[2 * layer + 1][2]]

    def up_grads(layer, hidden):
        return [dot_low(kept[2 * layer + 1][0], part, TN) for part in hidden]

    def out_grads(layer, low):
        return [dot_low(mix[0], low, TN) for mix in kept[2 * layer][3]]

    def mixed_grads(layer, low):
        return [dot_low(low, part, NT) for part in weights[layer]["out"]]

    def attention_grad(layer, part, grad_mix):
        _, _, projected, mixed = kept[2 * layer]
        rows = 256 if layer == 0 else 512
        return attn_bwd(projected[part], mixed[part][1], grad_mix, limits, layer == 0, rows)

    def norm_step(layer, part, grad_rows, grad_normed):
        added, grad_gain, grad_shift = norm_backward(
            kept[2 * layer + part][1], grad_normed, gains[layer][part]
        )
        norm_sums[layer][part] = (grad_gain, grad_shift)
        return grad_rows + added

    out1, qkv1 = chain("out", "x", None), chain("qkv", "y", None)
    down0, up0 = chain("down", "x", None, "core"), chain("up", "y", None, "core")
    out0, qkv0 = chain("out", "x", None), chain("qkv", "y", None)

    low = grad_rows.astype(bf16)
    down_parts = down_grads(1, low)
    hidden = hidden_grads(1, low)
    down_parts, hidden, grad_rows = pin(down_parts, hidden, grad_rows)
    up_parts = [dot_low(part, kept[3][0], TN) for part in hidden]
    both_parts = stack_pair(side, dp_size, down_parts, up_parts)
    both_parts, hidden, grad_rows = pin(both_parts, hidden, grad_rows)
    pair1 = Scatter(flat_rows(both_parts))
    grad_normed = dot_sum(list(zip(hidden, weights[1]["up"])), NT)
    grad_rows = norm_step(1, 1, grad_rows, grad_normed)
    low = grad_rows.astype(bf16)
    out_parts = out_grads(1, low)
    mine, theirs = mixed_grads(1, low)
    theirs = attention_grad(1, 1, theirs)
    out_parts, mine, theirs, grad_rows = pin(out_parts, mine, theirs, grad_rows)
    out1.start_rows(*out_parts)
    mine = attention_grad(1, 0, mine)
    parts = [dot_low(kept[2][0], part, TN) for part in (mine, theirs)]
    parts, mine, theirs, grad_rows = move((parts, mine, theirs, grad_rows), hold=[out1])
    qkv1.start_rows(*parts)
    out_there = swap_tensor(out_away)
    grad_normed = dot_sum(list(zip((mine, theirs), weights[1]["qkv"])), NT)
    grad_rows = norm_step(1, 0, grad_rows, grad_normed)
    low = grad_rows.astype(bf16)
    parts = down_grads(0, low)
    parts, low, grad_rows = move((parts, low, grad_rows), out1, qkv1)
    start_quarters(down0, "down", parts)
    hidden = hidden_grads(0, low)
    hidden, grad_rows, out_there = move((hidden, grad_rows, out_there), hold=[down0])
    parts = up_grads(0, hidden)
    grad_normed = dot_sum(list(zip(hidden, weights[0]["up"])), NT)
    parts, grad_normed, grad_rows = move((parts, grad_normed, grad_rows), qkv1, out1, down0, pair1)
    start_quarters(up0, "up", parts)
    grad_rows = norm_step(0, 1, grad_rows, grad_normed)
    low = grad_rows.astype(bf16)
    out_parts = out_grads(0, low)
    mine, theirs = mixed_grads(0, low)
    out_parts, mine, theirs, grad_rows = move((out_parts, mine, theirs, grad_rows), up0, qkv1, out1)
    out0.start_rows(*out_parts)
    theirs = attention_grad(0, 1, theirs)
    part_theirs = dot_low(kept[0][0], theirs, TN)
    part_theirs, mine, theirs, grad_rows = move(
        (part_theirs, mine, theirs, grad_rows), down0, up0, qkv1, out1, hold=[out0]
    )
    qkv0.start_other(part_theirs)
    mine = attention_grad(0, 0, mine)
    part_mine = dot_low(kept[0][0], mine, TN)
    part_mine, mine, theirs, grad_rows = move(
        (part_mine, mine, theirs, grad_rows), down0, up0, out0, qkv0, qkv1, out1
    )
    joint1 = Gather(qkv1, out1, PACK_WIDTH, True)
    qkv0.add_own(part_mine)
    grad_normed = dot_sum([(mine, weights[0]["qkv"][0]), (theirs, weights[0]["qkv"][1])], NT)
    grad_rows = norm_step(0, 0, grad_rows, grad_normed)
    grad_mine, grad_away = halves_of(grad_rows)
    late = Spread(
        jnp.concatenate(
            [jnp.stack([norm_sums[0][part][which] for which in range(2) for part in range(2)])]
            + [picker * norm_sums[1][part][which][None] for which in range(2) for part in range(2)]
        ),
        dp_size,
    )
    frames_out = place_frames(side, out_mine, out_there)
    grad_away, grad_mine, frames_out = move((grad_away, grad_mine, frames_out), qkv0, up0, down0, out0, pair1, late)
    grad_away, grad_mine = move((grad_away, grad_mine), qkv0, up0, down0, out0, late)
    pair0 = Gather(down0, up0, model_width, True)
    grad_there = swap_tensor(grad_away)
    bases = dict(zip(("up", "down"), place_pair(pair1.whole, 1)))
    bases, grad_mine, grad_there = move((bases, grad_mine, grad_there), qkv0, out0, late)
    (grad_mine,) = move((grad_mine,), qkv0, out0, late, joint1)
    joint0 = Gather(qkv0, out0, PACK_WIDTH, False)
    shapes = (flat_shape["qkv"], flat_shape["out"])
    joint_bases = place_joint(joint1.whole, 1, *shapes, None)
    frames_grad = place_frames(side, grad_mine, grad_there)
    joint_bases, frames_grad = move((joint_bases, frames_grad), joint0, late)
    joint_bases, frames_grad = move((joint_bases, frames_grad), joint0, pair0)
    grad_up = place_quarters("up", pair0.whole, 1, 0, bases["up"])
    grad_down = place_quarters("down", pair0.whole, 0, 0, bases["down"])
    joint_bases, grad_up, grad_down = move((joint_bases, grad_up, grad_down), joint0, late)
    while joint0.flight:
        joint0.advance(joint0.flight)
    while late.flight:
        late.advance(late.flight)
    grad_qkv, grad_out = place_joint(joint0.whole, 0, *shapes, list(joint_bases))

    gain_rows = late.block[4:].reshape(4, section_count, model_width)
    return (
        frames_out,
        frames_grad,
        grad_qkv.transpose(0, 2, 1, 3),
        grad_out,
        grad_up,
        grad_down,
        late.block[0:2],
        late.block[2:4],
        gain_rows[0:2],
        gain_rows[2:4],
    )


def per_device(dp_size, tensor_size, *arrays):
    micro_count, local_seqs = arrays[0].shape[:2]
    paired = micro_count == 2 and tensor_size == 2 and local_seqs == 1
    if paired and dp_size >= 4 and dp_size & (dp_size - 1) == 0:
        return paired_device(dp_size, *arrays)
    return grouped_device(*arrays)


def solution(mesh):
    return jax.shard_map(
        partial(per_device, mesh.shape["dp"], mesh.shape["tensor"]),
        mesh=mesh,
        in_specs=(
            P(None, "dp", "tensor", None),
            P(None, "dp"),
            P(None, "dp"),
            P(None, "dp"),
            P(),
            P(),
            P(),
            P(),
            P(None, None, None, "tensor"),
            P(None, "tensor", None),
            P(None, None, "tensor"),
            P(None, "tensor", None),
            P(None, "dp", "tensor", None),
        ),
        out_specs=(
            P(None, "dp", "tensor", None),
            P(None, "dp", "tensor", None),
            P(None, None, None, "tensor"),
            P(None, "tensor", None),
            P(None, None, "tensor"),
            P(None, "tensor", None),
            P(),
            P(),
            P(),
            P(),
        ),
        check_vma=False,
    )
```

```python
from functools import partial

import jax
import jax.numpy as jnp
from jax import lax
from jax.experimental import pallas as pl
from jax.experimental.pallas import tpu as pltpu
from jax.sharding import PartitionSpec as P

HEAD_DIM = 64


norm_eps = 1e-05
masked_score = -1000000000.0
contract_rows = (((0,), (0,)), ((), ()))
contract_cols = (((1,), (1,)), ((), ()))


def plain_norm(inputs):
    centered = inputs - jnp.mean(inputs, axis=-1, keepdims=True)
    variance = jnp.mean(centered * centered, axis=-1, keepdims=True)
    return centered * lax.rsqrt(variance + norm_eps)


def fixed_norm(inputs, gain_row, shift_row):
    return plain_norm(inputs) * gain_row + shift_row


def section_norm(inputs, scale_table, shift_table, picker):
    scale_row = jnp.dot(
        picker, scale_table, precision=lax.Precision.HIGHEST, preferred_element_type=jnp.float32
    )
    shift_row = jnp.dot(
        picker, shift_table, precision=lax.Precision.HIGHEST, preferred_element_type=jnp.float32
    )
    return plain_norm(inputs) * scale_row + shift_row


def gather_normed(normed_low):
    return lax.all_gather(normed_low, "tensor", axis=0, tiled=True)


def gather_again(normed_low):
    return lax.all_gather(normed_low, "tensor", axis=0, tiled=True)


def sum_branch(branch_part):
    return lax.psum_scatter(
        branch_part.astype(jnp.bfloat16), "tensor", scatter_dimension=0, tiled=True
    ).astype(jnp.float32)


def gather_grad(grad_low):
    return lax.all_gather(grad_low, "tensor", axis=0, tiled=True)


def sum_normed(grad_part):
    return lax.psum_scatter(
        grad_part.astype(jnp.bfloat16), "tensor", scatter_dimension=0, tiled=True
    ).astype(jnp.float32)


def key_allowed(query_pos, key_pos, prefix, valid_count, causal):
    allowed = key_pos[None, :] < valid_count
    if causal:
        allowed = allowed & ((key_pos[None, :] < prefix) | (key_pos[None, :] <= query_pos[:, None]))
    return allowed


def split_heads(projected):
    length = projected.shape[0]
    head_width = projected.shape[1] // 3
    head_count = head_width // HEAD_DIM
    query_rows = projected[:, :head_width].reshape(length, head_count, HEAD_DIM)
    key_rows = projected[:, head_width : 2 * head_width].reshape(length, head_count, HEAD_DIM)
    value_rows = projected[:, 2 * head_width :].reshape(length, head_count, HEAD_DIM)
    return (query_rows, key_rows, value_rows)


def block_scores(query_block, key_rows, block_start, prefix, valid_count, causal):
    block_rows = query_block.shape[0]
    length = key_rows.shape[0]
    scores = jnp.einsum(
        "qhd,khd->hqk", query_block, key_rows, preferred_element_type=jnp.float32
    ) * HEAD_DIM ** (-0.5)
    query_pos = block_start + lax.iota(jnp.int32, block_rows)
    key_pos = lax.iota(jnp.int32, length)
    allowed = key_allowed(query_pos, key_pos, prefix, valid_count, causal)
    return jnp.where(allowed[None], scores, masked_score)


def attend_forward(projected, prefix, valid_count, causal, block_rows):
    length = projected.shape[0]
    head_width = projected.shape[1] // 3
    query_rows, key_rows, value_rows = split_heads(projected)

    def one_block(block_start):
        query_block = lax.dynamic_slice_in_dim(query_rows, block_start, block_rows, 0)
        scores = block_scores(query_block, key_rows, block_start, prefix, valid_count, causal)
        highest = jnp.max(scores, axis=-1, keepdims=True)
        row_total = jnp.sum(jnp.exp(scores - highest), axis=-1, keepdims=True)
        log_total = highest + jnp.log(row_total)
        shares = jnp.exp(scores - log_total).astype(jnp.bfloat16)
        mixture = jnp.einsum("hqk,khd->qhd", shares, value_rows, preferred_element_type=jnp.float32)
        return (mixture.astype(jnp.bfloat16), log_total)

    starts = lax.iota(jnp.int32, length // block_rows) * block_rows
    mixture, log_totals = lax.map(one_block, starts)
    return (mixture.reshape(length, head_width), log_totals)


def attend_backward(projected, log_totals, grad_mixture, prefix, valid_count, causal, block_rows):
    length = projected.shape[0]
    head_width = projected.shape[1] // 3
    query_rows, key_rows, value_rows = split_heads(projected)
    grad_rows = grad_mixture.reshape(query_rows.shape)
    score_scale = HEAD_DIM ** (-0.5)

    def one_block(grad_state, block_item):
        block_start, log_total = block_item
        grad_key, grad_value = grad_state
        query_block = lax.dynamic_slice_in_dim(query_rows, block_start, block_rows, 0)
        grad_block = lax.dynamic_slice_in_dim(grad_rows, block_start, block_rows, 0)
        scores = block_scores(query_block, key_rows, block_start, prefix, valid_count, causal)
        shares = jnp.exp(scores - log_total)
        shares_low = shares.astype(jnp.bfloat16)
        grad_shares = jnp.einsum(
            "qhd,khd->hqk", grad_block, value_rows, preferred_element_type=jnp.float32
        )
        inner_sum = jnp.sum(shares * grad_shares, axis=-1, keepdims=True)
        grad_scores = (shares * (grad_shares - inner_sum)).astype(jnp.bfloat16)
        grad_query = (
            jnp.einsum("hqk,khd->qhd", grad_scores, key_rows, preferred_element_type=jnp.float32)
            * score_scale
        )
        grad_key = (
            grad_key
            + jnp.einsum(
                "hqk,qhd->khd", grad_scores, query_block, preferred_element_type=jnp.float32
            )
            * score_scale
        )
        grad_value = grad_value + jnp.einsum(
            "hqk,qhd->khd", shares_low, grad_block, preferred_element_type=jnp.float32
        )
        return ((grad_key, grad_value), grad_query)

    starts = lax.iota(jnp.int32, length // block_rows) * block_rows
    zero_rows = jnp.zeros(query_rows.shape, jnp.float32)
    grad_state, grad_query = lax.scan(one_block, (zero_rows, zero_rows), (starts, log_totals))
    grad_key, grad_value = grad_state
    joined = jnp.concatenate(
        [
            grad_query.reshape(length, head_width),
            grad_key.reshape(length, head_width),
            grad_value.reshape(length, head_width),
        ],
        axis=1,
    )
    return joined.astype(jnp.bfloat16)


def grouped_device(
    frames_in,
    phone_len,
    frame_len,
    section,
    norm_gain,
    norm_bias,
    ada_scale,
    ada_shift,
    w_qkv,
    w_out,
    w_up,
    w_down,
    out_grad,
):
    micro_count, local_seqs, local_rows, model_width = frames_in.shape
    seq_length = local_rows * lax.axis_size("tensor")
    block_rows = min(512, seq_length)
    section_count = ada_scale.shape[1]
    qkv_mats = [w_qkv[layer_index].reshape(model_width, -1) for layer_index in range(2)]
    acc_qkv = [jnp.zeros(qkv_mats[layer_index].shape, jnp.float32) for layer_index in range(2)]
    acc_out = [jnp.zeros(w_out.shape[1:], jnp.float32) for layer_index in range(2)]
    acc_up = [jnp.zeros(w_up.shape[1:], jnp.float32) for layer_index in range(2)]
    acc_down = [jnp.zeros(w_down.shape[1:], jnp.float32) for layer_index in range(2)]
    acc_gain = [jnp.zeros((model_width,), jnp.float32) for part_index in range(2)]
    acc_bias = [jnp.zeros((model_width,), jnp.float32) for part_index in range(2)]
    acc_scale = [jnp.zeros((section_count, model_width), jnp.float32) for part_index in range(2)]
    acc_shift = [jnp.zeros((section_count, model_width), jnp.float32) for part_index in range(2)]
    frames_list = []
    grads_list = []
    for micro_index in range(micro_count):
        prefix = phone_len[micro_index, 0]
        valid_count = prefix + frame_len[micro_index, 0]
        picker = (lax.iota(jnp.int32, section_count) == section[micro_index, 0]).astype(
            jnp.float32
        )[None, :]
        residual = frames_in[micro_index, 0].astype(jnp.float32)
        stored = []
        for layer_index in range(2):
            for part_index in range(2):
                if layer_index == 0:
                    normed, norm_back = jax.vjp(
                        fixed_norm, residual, norm_gain[part_index], norm_bias[part_index]
                    )
                else:
                    normed, norm_back = jax.vjp(
                        partial(section_norm, picker=picker),
                        residual,
                        ada_scale[part_index],
                        ada_shift[part_index],
                    )
                normed_low = normed.astype(jnp.bfloat16)
                gathered = gather_normed(normed_low)
                if part_index == 0:
                    projected = jnp.dot(
                        gathered, qkv_mats[layer_index], preferred_element_type=jnp.float32
                    ).astype(jnp.bfloat16)
                    mixture, log_totals = attend_forward(
                        projected, prefix, valid_count, layer_index == 0, block_rows
                    )
                    branch = sum_branch(
                        jnp.dot(mixture, w_out[layer_index], preferred_element_type=jnp.float32)
                    )
                    saved_state = (projected, log_totals, mixture)
                else:
                    hidden = jnp.dot(
                        gathered, w_up[layer_index], preferred_element_type=jnp.float32
                    )
                    active = jax.nn.gelu(hidden, approximate=True).astype(jnp.bfloat16)
                    branch = sum_branch(
                        jnp.dot(active, w_down[layer_index], preferred_element_type=jnp.float32)
                    )
                    saved_state = (hidden, active)
                kept_rows = normed_low
                stored.append((norm_back, kept_rows, saved_state))
                residual = residual + branch
        out_group = [residual]
        grad_rows = out_grad[micro_index, 0].astype(jnp.float32)
        for layer_index in (1, 0):
            for part_index in (1, 0):
                norm_back, kept_rows, saved_state = stored[2 * layer_index + part_index]
                gathered = gather_again(kept_rows)
                grad_whole = gather_grad(grad_rows.astype(jnp.bfloat16))
                if part_index == 1:
                    hidden, active = saved_state
                    acc_down[layer_index] = acc_down[layer_index] + lax.dot_general(
                        active, grad_whole, contract_rows, preferred_element_type=jnp.float32
                    )
                    grad_active = lax.dot_general(
                        grad_whole,
                        w_down[layer_index],
                        contract_cols,
                        preferred_element_type=jnp.float32,
                    )
                    gelu_value, gelu_back = jax.vjp(partial(jax.nn.gelu, approximate=True), hidden)
                    grad_hidden = gelu_back(grad_active)[0].astype(jnp.bfloat16)
                    acc_up[layer_index] = acc_up[layer_index] + lax.dot_general(
                        gathered, grad_hidden, contract_rows, preferred_element_type=jnp.float32
                    )
                    grad_normed = sum_normed(
                        lax.dot_general(
                            grad_hidden,
                            w_up[layer_index],
                            contract_cols,
                            preferred_element_type=jnp.float32,
                        )
                    )
                else:
                    projected, log_totals, mixture = saved_state
                    acc_out[layer_index] = acc_out[layer_index] + lax.dot_general(
                        mixture, grad_whole, contract_rows, preferred_element_type=jnp.float32
                    )
                    grad_mixture = lax.dot_general(
                        grad_whole,
                        w_out[layer_index],
                        contract_cols,
                        preferred_element_type=jnp.float32,
                    ).astype(jnp.bfloat16)
                    grad_projected = attend_backward(
                        projected,
                        log_totals,
                        grad_mixture,
                        prefix,
                        valid_count,
                        layer_index == 0,
                        block_rows,
                    )
                    acc_qkv[layer_index] = acc_qkv[layer_index] + lax.dot_general(
                        gathered, grad_projected, contract_rows, preferred_element_type=jnp.float32
                    )
                    grad_normed = sum_normed(
                        lax.dot_general(
                            grad_projected,
                            qkv_mats[layer_index],
                            contract_cols,
                            preferred_element_type=jnp.float32,
                        )
                    )
                grad_input, grad_first, grad_second = norm_back(grad_normed)
                grad_rows = grad_rows + grad_input
                if layer_index == 0:
                    acc_gain[part_index] = acc_gain[part_index] + grad_first
                    acc_bias[part_index] = acc_bias[part_index] + grad_second
                else:
                    acc_scale[part_index] = acc_scale[part_index] + grad_first
                    acc_shift[part_index] = acc_shift[part_index] + grad_second
        grad_group = [grad_rows]
        frames_list.append(jnp.stack(out_group))
        grads_list.append(jnp.stack(grad_group))
    total_qkv, total_out, total_up, total_down = (
        lax.psum(jnp.stack(acc_qkv).astype(jnp.bfloat16), "dp").astype(jnp.float32),
        lax.psum(jnp.stack(acc_out).astype(jnp.bfloat16), "dp").astype(jnp.float32),
        lax.psum(jnp.stack(acc_up).astype(jnp.bfloat16), "dp").astype(jnp.float32),
        lax.psum(jnp.stack(acc_down).astype(jnp.bfloat16), "dp").astype(jnp.float32),
    )
    norm_totals = lax.psum(
        (jnp.stack(acc_gain), jnp.stack(acc_bias), jnp.stack(acc_scale), jnp.stack(acc_shift)),
        ("dp", "tensor"),
    )
    return (
        jnp.stack(frames_list),
        jnp.stack(grads_list),
        total_qkv.reshape(2, model_width, 3, -1),
        total_out,
        total_up,
        total_down,
        norm_totals[0],
        norm_totals[1],
        norm_totals[2],
        norm_totals[3],
    )


bf16,f32=jnp.bfloat16,jnp.float32
NT=(((1,),(1,)),((),()))
TN=(((0,),(0,)),((),()))

def _limits(lims_ref, start, rows, causal, axis):
    prefix, valid = lims_ref[0], lims_ref[1]
    shape=(rows,1) if axis==0 else (1,rows)
    pos=start+lax.broadcasted_iota(jnp.int32,shape,axis)
    if causal:
        return jnp.minimum(jnp.maximum(pos,prefix-1),valid-1)
    return jnp.zeros(shape,jnp.int32)+(valid-1)

def fwd_kernel(causal, bq, lims_ref, q_ref, k_ref, v_ref, o_ref, l_ref):
    length=q_ref.shape[0]
    lane=lax.broadcasted_iota(jnp.int32,(bq,128),1)
    def block(start, kk):
        q=q_ref[pl.ds(start,bq),:]*jnp.asarray(0.125,bf16)
        lim=_limits(lims_ref,start,bq,causal,0)
        outs=[];rows=[]
        for h in range(2):
            qm=jnp.where((lane<HEAD_DIM)==(h==0),q,jnp.zeros_like(q))
            s=lax.dot_general(qm,k_ref[0:kk,:],NT,preferred_element_type=f32)
            key=lax.broadcasted_iota(jnp.int32,(bq,kk),1)
            s=jnp.where(key<=lim,s,-1e9)
            m=jnp.max(s,axis=1,keepdims=True)
            e=jnp.exp(s-m)
            l=jnp.sum(e,axis=1,keepdims=True)
            o=jnp.dot(e.astype(bf16),v_ref[0:kk,:],preferred_element_type=f32)*(1.0/l)
            outs.append(o); rows.append(m+jnp.log(l))
        o_ref[pl.ds(start,bq),:]=jnp.where(lane<HEAD_DIM,outs[0],outs[1]).astype(bf16)
        both=jnp.where(lane<HEAD_DIM,rows[0],rows[1])
        bt=both.T
        l_ref[0,0:1,pl.ds(start,bq)]=bt[0:1,:]
        l_ref[0,1:2,pl.ds(start,bq)]=bt[HEAD_DIM:HEAD_DIM+1,:]
    nq=length//bq
    if causal:
        for i in range(nq): block(i*bq,(i+1)*bq)
    else:
        def body(i,c):
            block(pl.multiple_of(i*bq,bq),length); return c
        lax.fori_loop(0,nq,body,0)

def attn_fwd(qkv, lims, causal, bq=256):
    length=qkv.shape[0]; width=qkv.shape[1]//3; pairs=width//128
    spec=lambda off: pl.BlockSpec((length,128),lambda i,off=off:(0,off*pairs+i))
    return pl.pallas_call(partial(fwd_kernel,causal,bq),
        grid=(pairs,),
        in_specs=[pl.BlockSpec(memory_space=pltpu.SMEM),spec(0),spec(1),spec(2)],
        out_specs=[pl.BlockSpec((length,128),lambda i:(0,i)),pl.BlockSpec((1,2,length),lambda i:(i,0,0))],
        out_shape=[jax.ShapeDtypeStruct((length,width),bf16),jax.ShapeDtypeStruct((pairs,2,length),f32)],
        compiler_params=pltpu.CompilerParams(vmem_limit_bytes=48*2**20),
        cost_estimate=pl.CostEstimate(flops=pairs*2**20,bytes_accessed=length*width*8,transcendentals=0),
        name="attn_fwd_"+("causal" if causal else "full"),
    )(lims,qkv,qkv,qkv)

def bwd_kernel(causal,bq,lims_ref,q_ref,k_ref,v_ref,l_ref,do_ref,grad_ref,dk_acc,dv_acc):
    length=q_ref.shape[0]
    lane=lax.broadcasted_iota(jnp.int32,(bq,128),1)
    dk_acc[...]=jnp.zeros_like(dk_acc); dv_acc[...]=jnp.zeros_like(dv_acc)
    width=grad_ref.shape[1]//3
    at=[pl.multiple_of(part*width+pl.program_id(0)*128,128) for part in range(3)]
    def block(start,kk):
        q=q_ref[pl.ds(start,bq),:]*jnp.asarray(0.125,bf16)
        do=do_ref[pl.ds(start,bq),:]
        lim=_limits(lims_ref,start,bq,causal,1)
        dqs=[]
        for h in range(2):
            sel=(lane<HEAD_DIM)==(h==0)
            qm=jnp.where(sel,q,jnp.zeros_like(q)); dom=jnp.where(sel,do,jnp.zeros_like(do))
            s=lax.dot_general(k_ref[0:kk,:],qm,NT,preferred_element_type=f32)
            dp=lax.dot_general(v_ref[0:kk,:],dom,NT,preferred_element_type=f32)
            key=lax.broadcasted_iota(jnp.int32,(kk,bq),0)
            lrow=l_ref[0,h:h+1,pl.ds(start,bq)]
            p=jnp.where(key<=lim,jnp.exp(s-lrow),0.0)
            pd=p*dp
            D=jnp.sum(pd,axis=0,keepdims=True)
            ds=(pd-p*D).astype(bf16)
            dv_acc[0:kk,:]+=jnp.dot(p.astype(bf16),dom,preferred_element_type=f32)
            dk_acc[0:kk,:]+=jnp.dot(ds,qm,preferred_element_type=f32)
            dqs.append(lax.dot_general(ds,k_ref[0:kk,:],TN,preferred_element_type=f32))
        grad_ref[pl.ds(start,bq),pl.ds(at[0],128)]=(jnp.where(lane<HEAD_DIM,dqs[0],dqs[1])*0.125).astype(bf16)
    nq=length//bq
    if causal:
        for i in range(nq): block(i*bq,(i+1)*bq)
    else:
        def body(i,c):
            block(pl.multiple_of(i*bq,bq),length); return c
        lax.fori_loop(0,nq,body,0)
    grad_ref[:,pl.ds(at[1],128)]=dk_acc[...].astype(bf16)
    grad_ref[:,pl.ds(at[2],128)]=dv_acc[...].astype(bf16)

def attn_bwd(qkv,L,do,lims,causal,bq=256):
    length=qkv.shape[0]; width=qkv.shape[1]//3; pairs=width//128
    spec=lambda off: pl.BlockSpec((length,128),lambda i,off=off:(0,off*pairs+i))
    one=pl.BlockSpec((length,128),lambda i:(0,i))
    return pl.pallas_call(partial(bwd_kernel,causal,bq),
        grid=(pairs,),
        in_specs=[pl.BlockSpec(memory_space=pltpu.SMEM),spec(0),spec(1),spec(2),pl.BlockSpec((1,2,length),lambda i:(i,0,0)),one],
        out_specs=pl.BlockSpec((length,3*width),lambda i:(0,0)),
        out_shape=jax.ShapeDtypeStruct((length,3*width),bf16),
        scratch_shapes=[pltpu.VMEM((length,128),f32)]*2,
        compiler_params=pltpu.CompilerParams(vmem_limit_bytes=48*2**20),
        cost_estimate=pl.CostEstimate(flops=pairs*2**20,bytes_accessed=length*width*8,transcendentals=0),
        name="attn_bwd_"+("causal" if causal else "full"),
    )(lims,qkv,qkv,qkv,L,do)


def pin(*values):
    return lax.optimization_barrier(values)


def swap_tensor(block):
    return lax.ppermute(block, "tensor", [(0, 1), (1, 0)])


def swap_bit(block, bit, dp_size):
    return lax.ppermute(block, "dp", [(place, place ^ (1 << bit)) for place in range(dp_size)])


def in_order(flag, mine, other):
    first = jnp.where(flag == 0, mine, other)
    second = jnp.where(flag == 0, other, mine)
    return jnp.concatenate([first, second], axis=0)


def add_rounded(left, right):
    return (left.astype(f32) + right.astype(f32)).astype(bf16)


def norm_forward(rows, gain_row, shift_row):
    mean = jnp.mean(rows, axis=-1, keepdims=True)
    centered = rows - mean
    rate = lax.rsqrt(jnp.mean(centered * centered, axis=-1, keepdims=True) + norm_eps)
    normed = centered * rate * gain_row + shift_row
    return normed.astype(bf16), (rows, mean, rate)


def norm_backward(saved, grad_normed, gain_row):
    rows, mean, rate = saved
    unit = (rows - mean) * rate
    grad_unit = grad_normed * gain_row
    grad_rows = rate * (
        grad_unit
        - jnp.mean(grad_unit, axis=-1, keepdims=True)
        - unit * jnp.mean(grad_unit * unit, axis=-1, keepdims=True)
    )
    return grad_rows, jnp.sum(grad_normed * unit, axis=0), jnp.sum(grad_normed, axis=0)


def gelu_pair(hidden):
    square = hidden * hidden
    share = 0.5 + 0.5 * jnp.tanh(hidden * (0.7978845608 + (0.7978845608 * 0.044715) * square))
    value = hidden * share
    rate = 2.0 * 0.7978845608 + (6.0 * 0.7978845608 * 0.044715) * square
    slope = share + (value * rate) * (1.0 - share)
    return value.astype(bf16), slope.astype(bf16)


def dot_sum(pairs, dims):
    total = None
    for left, right in pairs:
        term = lax.dot_general(left, right, dims, preferred_element_type=f32)
        total = term if total is None else total + term
    return total


def dot_low(left, right, dims):
    return lax.dot_general(left, right, dims, preferred_element_type=f32).astype(bf16)


NN = (((1,), (0,)), ((), ()))
SPLIT_AXIS = {"up": 1, "down": 0}
PACK_WIDTH = 512
LIGHT = pl.CostEstimate(flops=0, bytes_accessed=2**16, transcendentals=0)


def quarter_of(kind, half, place):
    axis = SPLIT_AXIS[kind]
    width = half.shape[axis] // 2
    return lax.dynamic_slice_in_dim(half, place * width, width, axis)


def row_half(block, place):
    height = block.shape[0] // 2
    return lax.dynamic_slice_in_dim(block, place * height, height, 0)


def flat_kernel(in_ref, out_ref):
    width = in_ref.shape[3]
    for part in range(3):
        out_ref[:, part * width : (part + 1) * width] = in_ref[0, part]


def flat_qkv(stacked, layer):
    _, _, height, width = stacked.shape
    rows = height // 2
    return pl.pallas_call(
        flat_kernel,
        grid=(2,),
        in_specs=[pl.BlockSpec((1, 3, rows, width), lambda step: (layer, 0, step, 0))],
        out_specs=pl.BlockSpec((rows, 3 * width), lambda step: (step, 0)),
        out_shape=jax.ShapeDtypeStruct((height, 3 * width), bf16),
        cost_estimate=LIGHT,
        name="flat_qkv",
    )(stacked)


def pack_kernel(kinds, place_ref, *refs):
    out_ref = refs[-1]
    at = 0
    for kind, ref in zip(kinds, refs):
        if kind == "qkv":
            pieces = [ref[0, part] for part in range(3)]
        else:
            count = ref.shape[2] // PACK_WIDTH
            pieces = [ref[0, :, part * PACK_WIDTH : (part + 1) * PACK_WIDTH] for part in range(count)]
        for piece in pieces:
            out_ref[at : at + piece.shape[0], :] = piece
            at += piece.shape[0]


def pack_pieces(place, layer, dp_size, kinds, arrays):
    specs, total = [], 0
    for kind, array in zip(kinds, arrays):
        height, width = array.shape[-2:]
        rows = height // dp_size
        if kind == "qkv":
            specs.append(pl.BlockSpec((1, 3, rows, width), lambda step, at: (layer, 0, at[0], 0)))
            total += 3 * rows * width // PACK_WIDTH
        else:
            specs.append(pl.BlockSpec((1, rows, width), lambda step, at: (layer, at[0], 0)))
            total += rows * width // PACK_WIDTH
    return pl.pallas_call(
        partial(pack_kernel, kinds),
        grid_spec=pltpu.PrefetchScalarGridSpec(
            num_scalar_prefetch=1,
            grid=(1,),
            in_specs=specs,
            out_specs=pl.BlockSpec((total, PACK_WIDTH), lambda step, at: (0, 0)),
        ),
        out_shape=jax.ShapeDtypeStruct((total, PACK_WIDTH), bf16),
        cost_estimate=LIGHT,
        name="pack_pieces",
    )(place.reshape(1).astype(jnp.int32), *arrays)


def unpack_kernel(in_ref, *refs):
    at = 0
    for ref in refs:
        rows = ref.shape[0] // in_ref.shape[0]
        for part in range(ref.shape[1] // PACK_WIDTH):
            for block in range(in_ref.shape[0]):
                ref[block * rows : (block + 1) * rows, part * PACK_WIDTH : (part + 1) * PACK_WIDTH] = in_ref[
                    block, at : at + rows, :
                ]
            at += rows


def unpack_halves(gathered, shapes):
    dp_size, total, _ = gathered.shape
    some = max(1, dp_size // 4)
    return pl.pallas_call(
        unpack_kernel,
        grid=(dp_size // some,),
        in_specs=[pl.BlockSpec((some, total, PACK_WIDTH), lambda step: (step, 0, 0))],
        out_specs=[
            pl.BlockSpec((height // dp_size * some, width), lambda step: (step, 0)) for height, width in shapes
        ],
        out_shape=[jax.ShapeDtypeStruct(shape, bf16) for shape in shapes],
        compiler_params=pltpu.CompilerParams(vmem_limit_bytes=32 * 2**20),
        cost_estimate=LIGHT,
        name="unpack_halves",
    )(gathered)


def stack_kernel(steps, side_ref, down_own, up_own, down_other, up_other, out_ref):
    blocks, rows = out_ref.shape[0], out_ref.shape[1] // 2

    def write(down_ref, up_ref):
        for block in range(blocks):
            out_ref[block, :rows] = down_ref[block * rows : (block + 1) * rows]
            out_ref[block, rows:] = up_ref[block * rows : (block + 1) * rows]

    pl.when(pl.program_id(0) < steps)(lambda: write(down_own, up_own))
    pl.when(pl.program_id(0) >= steps)(lambda: write(down_other, up_other))


def stack_pair(side, dp_size, down_parts, up_parts):
    height, width = down_parts[0].shape
    steps = 4
    rows, some = height // dp_size, dp_size // steps
    own = pl.BlockSpec((some * rows, width), lambda step, side_ref: (jnp.minimum(step, steps - 1), 0))
    other = pl.BlockSpec((some * rows, width), lambda step, side_ref: (jnp.maximum(step - steps, 0), 0))

    def target(step, side_ref):
        half = jnp.where(step < steps, side_ref[0], 1 - side_ref[0])
        return (half * steps + step % steps, 0, 0)

    return pl.pallas_call(
        partial(stack_kernel, steps),
        grid_spec=pltpu.PrefetchScalarGridSpec(
            num_scalar_prefetch=1,
            grid=(2 * steps,),
            in_specs=[own, own, other, other],
            out_specs=pl.BlockSpec((some, 2 * rows, width), target),
        ),
        out_shape=jax.ShapeDtypeStruct((2 * dp_size, 2 * rows, width), bf16),
        compiler_params=pltpu.CompilerParams(vmem_limit_bytes=32 * 2**20),
        cost_estimate=LIGHT,
        name="stack_pair",
    )(side.reshape(1).astype(jnp.int32), down_parts[0], up_parts[0], down_parts[1], up_parts[1])


def place_joint_kernel(whole_ref, *refs):
    qkv_out, out_out = refs[-2:]
    for block in range(whole_ref.shape[0]):
        rows = qkv_out.shape[2] // whole_ref.shape[0]
        for part in range(3):
            qkv_out[0, part, block * rows : (block + 1) * rows, :] = whole_ref[
                block, part * rows : (part + 1) * rows, :
            ].astype(f32)
        at, rows = 3 * rows, out_out.shape[1] // whole_ref.shape[0]
        for part in range(out_out.shape[2] // PACK_WIDTH):
            out_out[0, block * rows : (block + 1) * rows, part * PACK_WIDTH : (part + 1) * PACK_WIDTH] = whole_ref[
                block, at + part * rows : at + (part + 1) * rows, :
            ].astype(f32)


def place_joint(whole, layer, qkv_shape, out_shape, bases):
    dp_size, total, _ = whole.shape
    some = dp_size // 4
    operands, in_specs, aliases = [whole], [pl.BlockSpec((some, total, PACK_WIDTH), lambda step: (step, 0, 0))], {}
    if bases is not None:
        operands += bases
        in_specs += [pl.BlockSpec(memory_space=pl.ANY)] * 2
        aliases = {1: 0, 2: 1}
    return pl.pallas_call(
        place_joint_kernel,
        grid=(4,),
        in_specs=in_specs,
        out_specs=[
            pl.BlockSpec((1, 3, qkv_shape[0] // 4, qkv_shape[1] // 3), lambda step: (layer, 0, step, 0)),
            pl.BlockSpec((1, out_shape[0] // 4, out_shape[1]), lambda step: (layer, step, 0)),
        ],
        out_shape=[
            jax.ShapeDtypeStruct((2, 3, qkv_shape[0], qkv_shape[1] // 3), f32),
            jax.ShapeDtypeStruct((2,) + tuple(out_shape), f32),
        ],
        input_output_aliases=aliases,
        compiler_params=pltpu.CompilerParams(vmem_limit_bytes=32 * 2**20),
        cost_estimate=LIGHT,
        name="place_joint",
    )(*operands)


def place_pair_kernel(whole_ref, up_out, down_out):
    for block in range(whole_ref.shape[0]):
        rows = whole_ref.shape[2]
        down_out[0, block * rows : (block + 1) * rows, :] = whole_ref[block, 0].astype(f32)
        up_out[0, :, block * rows : (block + 1) * rows] = whole_ref[block, 1].astype(f32).T


def place_pair(whole, layer):
    dp_size, rows, columns = whole.shape
    rows = rows // 2
    some = dp_size // 4
    return pl.pallas_call(
        place_pair_kernel,
        grid=(4,),
        in_specs=[pl.BlockSpec((some, 2, rows, columns), lambda step: (step, 0, 0, 0))],
        out_specs=[
            pl.BlockSpec((1, columns, some * rows), lambda step: (layer, 0, step)),
            pl.BlockSpec((1, some * rows, columns), lambda step: (layer, step, 0)),
        ],
        out_shape=[
            jax.ShapeDtypeStruct((2, columns, dp_size * rows), f32),
            jax.ShapeDtypeStruct((2, dp_size * rows, columns), f32),
        ],
        compiler_params=pltpu.CompilerParams(vmem_limit_bytes=40 * 2**20),
        cost_estimate=LIGHT,
        name="place_pair",
    )(whole.reshape(dp_size, 2, rows, columns))


def place_kernel(whole_ref, *refs):
    out_ref = refs[-1]
    out_ref[0] = whole_ref[...].reshape(-1, whole_ref.shape[-1]).astype(f32)


def place_quarters(kind, whole, which, layer, base):
    dp_size, rows, columns = whole.shape
    half, some, rows = dp_size // 2, dp_size // 4, rows // 2
    if kind == "down":
        out_spec = pl.BlockSpec((1, some * rows, columns), lambda step: (layer, step, 0))
    else:
        out_spec = pl.BlockSpec((1, some * rows, columns), lambda step: (layer, step % 2, step // 2))
    return pl.pallas_call(
        place_kernel,
        grid=(4,),
        in_specs=[
            pl.BlockSpec(
                (some, None, None, rows, columns), lambda step: (step % 2, step // 2, which, 0, 0)
            ),
            pl.BlockSpec(memory_space=pl.ANY),
        ],
        out_specs=out_spec,
        out_shape=jax.ShapeDtypeStruct(base.shape, f32),
        input_output_aliases={1: 0},
        compiler_params=pltpu.CompilerParams(vmem_limit_bytes=32 * 2**20),
        cost_estimate=LIGHT,
        name="place_" + kind,
    )(whole.reshape(half, 2, 2, rows, columns), base)


def frame_kernel(side_ref, mine_ref, other_ref, out_ref):
    own = pl.program_id(0) == side_ref[0]
    out_ref[0, 0] = jnp.where(own, mine_ref[...], other_ref[...].astype(f32))


def place_frames(side, mine, other):
    height, width = mine.shape
    rows = height // 2
    spec = pl.BlockSpec((rows, width), lambda slot, step, side_ref: (step, 0))
    return pl.pallas_call(
        frame_kernel,
        grid_spec=pltpu.PrefetchScalarGridSpec(
            num_scalar_prefetch=1,
            grid=(2, 2),
            in_specs=[spec, spec],
            out_specs=pl.BlockSpec((1, 1, rows, width), lambda slot, step, side_ref: (slot, 0, step, 0)),
        ),
        out_shape=jax.ShapeDtypeStruct((2, 1, height, width), f32),
        cost_estimate=LIGHT,
        name="place_frames",
    )(side.reshape(1).astype(jnp.int32), mine, other)


def take_axis(block, index):
    return lax.dynamic_index_in_dim(block, index, 1, keepdims=False)


def flat_rows(block):
    return block.reshape(-1, block.shape[-1])


def join_level(here, kept, arrived):
    first = jnp.where(here == 0, kept, arrived)
    second = jnp.where(here == 0, arrived, kept)
    joined = jnp.stack([first, second], axis=1)
    return joined.reshape((-1,) + joined.shape[2:])


class Chain:
    def __init__(self, place, dp_size, rows, columns, kind, gather):
        self.place, self.dp_size, self.kind, self.gather = place, dp_size, kind, gather
        self.rows, self.columns = rows, columns
        self.bit_count = dp_size.bit_length() - 1
        self.flight = []

    def bit(self, index):
        return (self.place >> index) & 1

    def swap(self, block, bit):
        return swap_bit(block, bit, self.dp_size)

    def pair(self, block):
        return block.reshape(-1, 2, self.rows, self.columns)

    def start(self, near, far, ours=None, own_far=None):
        self.near, self.ours = near, ours
        self.flight = [self.swap(far, 0)] + ([] if ours is None else [self.swap(own_far, 0)])
        self.state = "core"

    def start_rows(self, own, other):
        self.start_other(other)
        self.add_own(own)

    def start_other(self, other):
        split, core = self.pair(other), self.bit(0)
        self.start(flat_rows(take_axis(split, core)), flat_rows(take_axis(split, 1 - core)))

    def add_own(self, own):
        split, core = self.pair(own), self.bit(0)
        self.flight = self.flight + [self.swap(flat_rows(take_axis(split, 1 - core)), 0)]
        self.ours = flat_rows(take_axis(split, core))

    def halves(self, block, bit):
        split, here = self.pair(block), self.bit(bit)
        return flat_rows(take_axis(split, here)), flat_rows(take_axis(split, 1 - here))

    def settle(self, arrived):
        self.near_here, self.near_away = self.halves(add_rounded(self.near, arrived[0]), 1)
        if self.ours is not None:
            self.kept_here, self.kept_away = self.halves(add_rounded(self.ours, arrived[1]), 1)
        self.flight, self.state = [], "ready"

    def launch(self):
        self.flight = [swap_tensor(self.near_away) if self.kind == "x" else self.swap(self.near_away, 1)]
        self.state = "first"

    def second(self, arrived):
        if len(arrived) > 1:
            self.kept_here, self.kept_away = self.halves(add_rounded(self.ours, arrived[1]), 1)
        if self.kind == "x":
            self.kept_away = add_rounded(self.kept_away, arrived[0])
        else:
            self.near_here = add_rounded(self.near_here, arrived[0])
        self.flight = [swap_tensor(self.near_here), self.swap(self.kept_away, 1)]
        self.state = "second"

    def next_bit(self, total, index):
        if index == self.bit_count:
            self.kept, self.state = total, "gather"
            if self.gather == "native":
                self.flight = [lax.all_gather(total, "dp", axis=0, tiled=False)]
                return
            if self.gather is None:
                self.flight, self.state = [], "done"
                return
            self.kept, self.level = total[None], index - 1
            self.flight = [self.swap(self.kept, self.level)]
            return
        self.kept, away = self.halves(total, index)
        self.flight, self.index, self.state = [self.swap(away, index)], index, "bits"

    def advance(self, arrived, hold=False):
        if self.state == "done":
            return
        if self.state == "core":
            self.settle(arrived)
            if not hold:
                self.launch()
        elif self.state == "ready":
            self.launch()
        elif self.state == "first":
            self.second(arrived)
        elif self.state == "second":
            total = self.kept_here.astype(f32) + arrived[0].astype(f32) + arrived[1].astype(f32)
            self.next_bit(total.astype(bf16), 2)
        elif self.state == "bits":
            self.next_bit(add_rounded(self.kept, arrived[0]), self.index + 1)
        elif self.gather == "native":
            self.whole, self.flight, self.state = arrived[0], [], "done"
        else:
            self.kept = join_level(self.bit(self.level), self.kept, arrived[0])
            self.level -= 1
            if self.level < 0:
                self.whole, self.flight, self.state = self.kept, [], "done"
            else:
                self.flight = [self.swap(self.kept, self.level)]


class Scatter:
    def __init__(self, block):
        self.flight = [lax.psum_scatter(block, ("tensor", "dp"), scatter_dimension=0, tiled=True)]
        self.state = "sum"

    def advance(self, arrived):
        if self.state == "sum":
            self.flight, self.state = [lax.all_gather(arrived[0], "dp", axis=0, tiled=False)], "gather"
        elif self.state == "gather":
            self.whole, self.flight, self.state = arrived[0], [], "done"


class Gather:
    def __init__(self, qkv, out, width, native):
        assert qkv.state == "done" and out.state == "done"
        pieces = []
        for block in (qkv.kept, out.kept):
            for at in range(0, block.shape[1], width):
                pieces.append(lax.slice_in_dim(block, at, at + width, axis=1))
        self.kept = jnp.concatenate(pieces, axis=0)
        self.native, self.bit, self.swap = native, qkv.bit, qkv.swap
        self.state = "going"
        if native:
            self.flight = [lax.all_gather(self.kept, "dp", axis=0, tiled=False)]
        else:
            self.kept, self.level = self.kept[None], qkv.bit_count - 1
            self.flight = [self.swap(self.kept, self.level)]

    def advance(self, arrived):
        if self.state == "done":
            return
        if self.native:
            self.whole, self.flight, self.state = arrived[0], [], "done"
            return
        self.kept = join_level(self.bit(self.level), self.kept, arrived[0])
        self.level -= 1
        if self.level < 0:
            self.whole, self.flight, self.state = self.kept, [], "done"
        else:
            self.flight = [self.swap(self.kept, self.level)]


class Spread:
    def __init__(self, block, dp_size):
        self.block, self.dp_size = block, dp_size
        self.bits = list(range(dp_size.bit_length() - 1))
        self.flight = [swap_tensor(block)]

    def advance(self, arrived):
        if not arrived:
            return
        self.block = self.block + arrived[0]
        self.flight = [swap_bit(self.block, self.bits.pop(0), self.dp_size)] if self.bits else []


def move(state, *chains, hold=()):
    everyone = chains + tuple(hold)
    state, flights = pin(state, [one.flight for one in everyone])
    for one, flight in zip(everyone, flights):
        if one in hold:
            one.advance(flight, hold=True)
        else:
            one.advance(flight)
    return state


def paired_device(
    dp_size,
    frames_in,
    phone_len,
    frame_len,
    section,
    norm_gain,
    norm_bias,
    ada_scale,
    ada_shift,
    w_qkv,
    w_out,
    w_up,
    w_down,
    out_grad,
):
    model_width = frames_in.shape[3]
    section_count = ada_scale.shape[1]
    side = lax.axis_index("tensor")
    place = lax.axis_index("dp")
    core, near_row = place & 1, (place >> 1) & 1

    def away_rows(halves):
        return lax.dynamic_index_in_dim(halves[:, 0], 1 - side, 0, keepdims=False)

    def whole_rows(halves, other):
        mine = lax.dynamic_index_in_dim(halves[:, 0], side, 0, keepdims=False)
        return in_order(side, mine, other)

    prefix = lax.dynamic_index_in_dim(phone_len[:, 0], side, 0, keepdims=False)
    frames = lax.dynamic_index_in_dim(frame_len[:, 0], side, 0, keepdims=False)
    chosen = lax.dynamic_index_in_dim(section[:, 0], side, 0, keepdims=False)
    limits = jnp.stack([prefix, prefix + frames]).astype(jnp.int32)
    picker = (lax.iota(jnp.int32, section_count) == chosen).astype(f32)[:, None]

    gains = [
        [norm_gain[0], norm_gain[1]],
        [jnp.sum(picker * ada_scale[part], axis=0) for part in range(2)],
    ]
    shifts = [
        [norm_bias[0], norm_bias[1]],
        [jnp.sum(picker * ada_shift[part], axis=0) for part in range(2)],
    ]

    stacked = w_qkv.transpose(0, 2, 1, 3)
    arrays = {"qkv": stacked, "out": w_out, "up": w_up, "down": w_down}
    flat_shape = {
        "qkv": (model_width, 3 * stacked.shape[3]),
        "out": w_out.shape[1:],
        "up": w_up.shape[1:],
        "down": w_down.shape[1:],
    }

    def packed(layer, kinds):
        return pack_pieces(place, layer, dp_size, kinds, [arrays[kind] for kind in kinds])

    def gathered(arrived):
        return lax.all_gather(arrived, "dp", axis=0, tiled=False)

    def unpacked(whole, kinds):
        return dict(zip(kinds, unpack_halves(whole, [flat_shape[kind] for kind in kinds])))

    attn_kinds, hidden_kinds = ("qkv", "out"), ("up", "down")
    rows_away, first_send = pin(away_rows(frames_in), packed(0, attn_kinds))
    other_rows = swap_tensor(rows_away)
    first_pack = swap_tensor(first_send)
    own_qkv = [flat_qkv(stacked, layer) for layer in range(2)]
    (first_pack,) = pin(first_pack)
    first_whole = gathered(first_pack)
    attn_send, hidden_send = packed(1, attn_kinds), packed(1, hidden_kinds)
    piece_rows, piece_columns = model_width // 2, w_up.shape[2] // 2
    up_send = lax.dynamic_slice(
        w_up, (0, near_row * piece_rows, core * piece_columns), (1, piece_rows, piece_columns)
    )[0]
    piece_rows = w_down.shape[1] // 4
    down_send = lax.dynamic_slice(
        w_down, (0, (2 * core + near_row) * piece_rows, 0), (1, piece_rows, model_width)
    )[0]
    other_rows, attn_send, hidden_send, up_send, down_send, own_qkv = pin(
        other_rows, attn_send, hidden_send, up_send, down_send, own_qkv
    )
    up_piece = swap_tensor(up_send)
    rows = whole_rows(frames_in, other_rows).astype(f32)
    normed, norm_kept = norm_forward(rows, gains[0][0], shifts[0][0])
    mine = dot_low(normed, own_qkv[0], NN)
    mix_mine = attn_fwd(mine, limits, True, 512)
    mix_mine, up_piece, attn_send, down_send = pin(mix_mine, up_piece, attn_send, down_send)
    attn_pack = swap_tensor(attn_send)
    up_there = swap_bit(up_piece, 1, dp_size)
    down_piece = swap_tensor(down_send)
    first = unpacked(first_whole, attn_kinds)
    theirs = dot_low(normed, first["qkv"], NN)
    mix_theirs = attn_fwd(theirs, limits, True, 512)
    mix_theirs, up_there, down_piece, hidden_send, attn_pack = pin(
        mix_theirs, up_there, down_piece, hidden_send, attn_pack
    )
    attn_whole = gathered(attn_pack)
    up_near = in_order(near_row, up_piece, up_there)
    up_far = swap_bit(up_near, 0, dp_size)
    down_there = swap_bit(down_piece, 1, dp_size)
    hidden_pack = swap_tensor(hidden_send)
    kept = [(normed, norm_kept, [mine, theirs], [mix_mine, mix_theirs])]
    rows = rows + dot_sum([(mix_mine[0], w_out[0]), (mix_theirs[0], first["out"])], NN)
    normed, norm_kept = norm_forward(rows, gains[0][1], shifts[0][1])
    pair_own = gelu_pair(jnp.dot(normed, w_up[0], preferred_element_type=f32))
    pair_own, up_far, normed, norm_kept, rows, hidden_pack = pin(
        pair_own, up_far, normed, norm_kept, rows, hidden_pack
    )
    hidden_whole = gathered(hidden_pack)
    pair_near = gelu_pair(jnp.dot(normed, up_near, preferred_element_type=f32))
    pair_far = gelu_pair(jnp.dot(normed, up_far, preferred_element_type=f32))
    rows = rows + dot_sum([(pair_own[0], w_down[0])], NN)
    rows, pair_near, pair_far, down_there = pin(rows, pair_near, pair_far, down_there)
    down_near = in_order(near_row, down_piece, down_there)
    down_far = swap_bit(down_near, 0, dp_size)
    grad_send = away_rows(out_grad)
    rows = rows + dot_sum([(pair_near[0], down_near)], NN)
    rows, grad_send, down_far = pin(rows, grad_send, down_far)
    grad_other = swap_tensor(grad_send)
    rows = rows + dot_sum([(pair_far[0], down_far)], NN)
    kept.append((normed, norm_kept, [pair_own, pair_near, pair_far]))

    normed, norm_kept = norm_forward(rows, gains[1][0], shifts[1][0])
    mine = dot_low(normed, own_qkv[1], NN)
    mix_mine = attn_fwd(mine, limits, False, 512)
    mix_mine, attn_whole = pin(mix_mine, attn_whole)
    second = unpacked(attn_whole, attn_kinds)
    theirs = dot_low(normed, second["qkv"], NN)
    mix_theirs = attn_fwd(theirs, limits, False, 512)
    mixed = [mix_mine, mix_theirs]
    kept.append((normed, norm_kept, [mine, theirs], mixed))
    rows = rows + dot_sum([(mix_mine[0], w_out[1]), (mix_theirs[0], second["out"])], NN)
    normed, norm_kept = norm_forward(rows, gains[1][1], shifts[1][1])
    pair_own = gelu_pair(jnp.dot(normed, w_up[1], preferred_element_type=f32))
    pair_own, rows, normed, norm_kept = pin(pair_own, rows, normed, norm_kept)
    rows = rows + dot_sum([(pair_own[0], w_down[1])], NN)
    rows, hidden_whole = pin(rows, hidden_whole)
    second.update(unpacked(hidden_whole, hidden_kinds))
    pair_other = gelu_pair(jnp.dot(normed, second["up"], preferred_element_type=f32))
    pair_other, rows = pin(pair_other, rows)
    rows = rows + dot_sum([(pair_other[0], second["down"])], NN)
    pairs = [pair_own, pair_other]
    kept.append((normed, norm_kept, pairs))
    weights = [
        {
            "qkv": [own_qkv[0], first["qkv"]],
            "out": [w_out[0], first["out"]],
            "up": [w_up[0], up_near, up_far],
            "down": [w_down[0], down_near, down_far],
        },
        {
            "qkv": [own_qkv[1], second["qkv"]],
            "out": [w_out[1], second["out"]],
            "up": [w_up[1], second["up"]],
            "down": [w_down[1], second["down"]],
        },
    ]
    rows, grad_other = pin(rows, grad_other)

    def halves_of(block):
        height = block.shape[0] // 2
        mine = lax.dynamic_slice_in_dim(block, side * height, height, 0)
        away = lax.dynamic_slice_in_dim(block, (1 - side) * height, height, 0)
        return mine, away.astype(bf16)

    out_mine, out_away = halves_of(rows)

    norm_sums = [[None, None], [None, None]]
    grad_rows = whole_rows(out_grad, grad_other).astype(f32)
    def chain(kind, first, gather, split="rows"):
        height, width = flat_shape[kind]
        if split == "core":
            count = dp_size // 2
            height, width = (height, width // 2) if kind == "up" else (height // 2, width)
        else:
            count = dp_size
        return Chain(place, dp_size, height // count, width, first, gather)

    def start_quarters(one, kind, parts):
        own, near, far = parts
        one.start(near, far, quarter_of(kind, own, core), quarter_of(kind, own, 1 - core))

    def hidden_grads(layer, low):
        pairs = kept[2 * layer + 1][2]
        return [
            (
                lax.dot_general(low, part, NT, preferred_element_type=f32) * pair[1].astype(f32)
            ).astype(bf16)
            for pair, part in zip(pairs, weights[layer]["down"])
        ]

    def down_grads(layer, low):
        return [dot_low(pair[0], low, TN) for pair in kept[2 * layer + 1][2]]

    def up_grads(layer, hidden):
        return [dot_low(kept[2 * layer + 1][0], part, TN) for part in hidden]

    def out_grads(layer, low):
        return [dot_low(mix[0], low, TN) for mix in kept[2 * layer][3]]

    def mixed_grads(layer, low):
        return [dot_low(low, part, NT) for part in weights[layer]["out"]]

    def attention_grad(layer, part, grad_mix):
        _, _, projected, mixed = kept[2 * layer]
        rows = 256 if layer == 0 else 512
        return attn_bwd(projected[part], mixed[part][1], grad_mix, limits, layer == 0, rows)

    def norm_step(layer, part, grad_rows, grad_normed):
        added, grad_gain, grad_shift = norm_backward(
            kept[2 * layer + part][1], grad_normed, gains[layer][part]
        )
        norm_sums[layer][part] = (grad_gain, grad_shift)
        return grad_rows + added

    out1, qkv1 = chain("out", "y", None), chain("qkv", "x", None)
    down0, up0 = chain("down", "x", None, "core"), chain("up", "y", None, "core")
    out0, qkv0 = chain("out", "x", None), chain("qkv", "y", None)

    low = grad_rows.astype(bf16)
    down_parts = down_grads(1, low)
    hidden = hidden_grads(1, low)
    down_parts, hidden, grad_rows = pin(down_parts, hidden, grad_rows)
    up_parts = [dot_low(part, kept[3][0], TN) for part in hidden]
    both_parts = stack_pair(side, dp_size, down_parts, up_parts)
    both_parts, hidden, grad_rows = pin(both_parts, hidden, grad_rows)
    pair1 = Scatter(flat_rows(both_parts))
    grad_normed = dot_sum(list(zip(hidden, weights[1]["up"])), NT)
    grad_rows = norm_step(1, 1, grad_rows, grad_normed)
    low = grad_rows.astype(bf16)
    out_parts = out_grads(1, low)
    mine, theirs = mixed_grads(1, low)
    theirs = attention_grad(1, 1, theirs)
    out_parts, mine, theirs, grad_rows = pin(out_parts, mine, theirs, grad_rows)
    out1.start_rows(*out_parts)
    mine = attention_grad(1, 0, mine)
    parts = [dot_low(kept[2][0], part, TN) for part in (mine, theirs)]
    parts, mine, theirs, grad_rows = move((parts, mine, theirs, grad_rows), hold=[out1])
    qkv1.start_rows(*parts)
    out_there = swap_tensor(out_away)
    grad_normed = dot_sum(list(zip((mine, theirs), weights[1]["qkv"])), NT)
    grad_rows = norm_step(1, 0, grad_rows, grad_normed)
    low = grad_rows.astype(bf16)
    low, grad_rows = move((low, grad_rows), out1, qkv1)
    parts = down_grads(0, low)
    parts, low, grad_rows = pin(parts, low, grad_rows)
    start_quarters(down0, "down", parts)
    hidden = hidden_grads(0, low)
    hidden, grad_rows, out_there = move((hidden, grad_rows, out_there), qkv1, out1, hold=[down0])
    parts = up_grads(0, hidden)
    grad_normed = dot_sum(list(zip(hidden, weights[0]["up"])), NT)
    parts, grad_normed, grad_rows = move((parts, grad_normed, grad_rows), qkv1, out1, down0, pair1)
    start_quarters(up0, "up", parts)
    grad_rows = norm_step(0, 1, grad_rows, grad_normed)
    low = grad_rows.astype(bf16)
    out_parts = out_grads(0, low)
    mine, theirs = mixed_grads(0, low)
    out_parts, mine, theirs, grad_rows = move((out_parts, mine, theirs, grad_rows), up0, qkv1, out1)
    out0.start_rows(*out_parts)
    theirs = attention_grad(0, 1, theirs)
    part_theirs = dot_low(kept[0][0], theirs, TN)
    part_theirs, mine, theirs, grad_rows = move(
        (part_theirs, mine, theirs, grad_rows), down0, up0, qkv1, out1, hold=[out0]
    )
    joint1 = Gather(qkv1, out1, PACK_WIDTH, True)
    qkv0.start_other(part_theirs)
    mine = attention_grad(0, 0, mine)
    part_mine = dot_low(kept[0][0], mine, TN)
    part_mine, mine, theirs, grad_rows = move(
        (part_mine, mine, theirs, grad_rows), down0, up0, out0, qkv0
    )
    qkv0.add_own(part_mine)
    grad_normed = dot_sum([(mine, weights[0]["qkv"][0]), (theirs, weights[0]["qkv"][1])], NT)
    grad_rows = norm_step(0, 0, grad_rows, grad_normed)
    grad_mine, grad_away = halves_of(grad_rows)
    late = Spread(
        jnp.concatenate(
            [jnp.stack([norm_sums[0][part][which] for which in range(2) for part in range(2)])]
            + [picker * norm_sums[1][part][which][None] for which in range(2) for part in range(2)]
        ),
        dp_size,
    )
    frames_out = place_frames(side, out_mine, out_there)
    grad_away, grad_mine, frames_out = move((grad_away, grad_mine, frames_out), qkv0, up0, down0, out0, pair1, late)
    grad_away, grad_mine = move((grad_away, grad_mine), qkv0, up0, down0, out0, late)
    pair0 = Gather(down0, up0, model_width, True)
    grad_there = swap_tensor(grad_away)
    bases = dict(zip(("up", "down"), place_pair(pair1.whole, 1)))
    bases, grad_mine, grad_there = move((bases, grad_mine, grad_there), qkv0, out0, late)
    (grad_mine,) = move((grad_mine,), qkv0, out0, late, joint1)
    joint0 = Gather(qkv0, out0, PACK_WIDTH, False)
    shapes = (flat_shape["qkv"], flat_shape["out"])
    joint_bases = place_joint(joint1.whole, 1, *shapes, None)
    frames_grad = place_frames(side, grad_mine, grad_there)
    joint_bases, frames_grad = move((joint_bases, frames_grad), joint0, late)
    joint_bases, frames_grad = move((joint_bases, frames_grad), joint0, pair0)
    grad_up = place_quarters("up", pair0.whole, 1, 0, bases["up"])
    grad_down = place_quarters("down", pair0.whole, 0, 0, bases["down"])
    joint_bases, grad_up, grad_down = move((joint_bases, grad_up, grad_down), joint0, late)
    while joint0.flight:
        joint0.advance(joint0.flight)
    while late.flight:
        late.advance(late.flight)
    grad_qkv, grad_out = place_joint(joint0.whole, 0, *shapes, list(joint_bases))

    gain_rows = late.block[4:].reshape(4, section_count, model_width)
    return (
        frames_out,
        frames_grad,
        grad_qkv.transpose(0, 2, 1, 3),
        grad_out,
        grad_up,
        grad_down,
        late.block[0:2],
        late.block[2:4],
        gain_rows[0:2],
        gain_rows[2:4],
    )


def per_device(dp_size, tensor_size, *arrays):
    micro_count, local_seqs = arrays[0].shape[:2]
    paired = micro_count == 2 and tensor_size == 2 and local_seqs == 1
    if paired and dp_size >= 4 and dp_size & (dp_size - 1) == 0:
        return paired_device(dp_size, *arrays)
    return grouped_device(*arrays)


def solution(mesh):
    return jax.shard_map(
        partial(per_device, mesh.shape["dp"], mesh.shape["tensor"]),
        mesh=mesh,
        in_specs=(
            P(None, "dp", "tensor", None),
            P(None, "dp"),
            P(None, "dp"),
            P(None, "dp"),
            P(),
            P(),
            P(),
            P(),
            P(None, None, None, "tensor"),
            P(None, "tensor", None),
            P(None, None, "tensor"),
            P(None, "tensor", None),
            P(None, "dp", "tensor", None),
        ),
        out_specs=(
            P(None, "dp", "tensor", None),
            P(None, "dp", "tensor", None),
            P(None, None, None, "tensor"),
            P(None, "tensor", None),
            P(None, None, "tensor"),
            P(None, "tensor", None),
            P(),
            P(),
            P(),
            P(),
        ),
        check_vma=False,
    )
```
